32 devices in a mesh: mic: 2 (over x), tile: 16 (over z, y, core).
Axes of the slice: x: 2, y: 2, z: 4, core: 2. Of those that a mesh axis runs over, the one named last changes fastest.
Arguments:
- micrograph: bfloat16 [32, 384, 384], P(('mic', 'tile')), parts along dimension 0, may hold values from -6 to 6
- templates: bfloat16 [16, 128, 128], P('tile'), may hold values from -0.046875 to 0.046875
- orient_list: int32 [32, 4], P('mic'), parts along dimension 0, may hold values from 0 to 15
- lengths: int32 [32], P('mic'), parts along dimension 0, may hold values from 1 to 4, 32 in all
- defocus: float32 [32], P('mic'), parts along dimension 0, may hold values from 8000 to 25000
Outputs:
- snr_map: float32 [32, 384, 384], P(('mic', 'tile')), parts along dimension 0
- mean_map: float32 [32, 384, 384], P(('mic', 'tile')), parts along dimension 0
- var_map: float32 [32, 384, 384], P(('mic', 'tile')), parts along dimension 0
The draws below stay inside these ranges and needn't reach their ends.
There are 2 independent parts, one for each index of `mic`. The reference program is written for one: setup_inputs(seed, part) draws one part's arguments, and reference() takes and returns one part's arrays. A program takes and returns all parts, laid end to end along the dimension named above; an argument that names none is the same for every part. Nothing has to cross between parts.
Inputs may be any that keep to these rules, and one draw needn't show every extreme that they name: `orient_list`: orientation numbers; a tile's list may name one orientation more than once. The lengths of all tiles of a micrograph sum to 32.
All inputs are finite; a program needn't handle non-finite values.
Results may differ from the reference program's by a relative error of at most 0.0098.
Values may be sent and summed in bfloat16 or wider, within the bound.
No kernel may reach another device: no remote copies, remote signals or barrier semaphores. Data moves between devices by JAX's collectives and lax.ppermute only.
A program may use at most 64 MiB of HBM per device.

```python
import math
import jax
import jax.numpy as jnp
import numpy as np
from jax import lax

BOX = 128
CENTRE = 384
GRID = 8
TILES = 16
ORIENTS = 16
LMAX = 4


def with_ends(drawn, own_key, smallest, high):
    longest = drawn.shape.index(max(drawn.shape))
    spots = []
    for shift in (0, 1):
        where = [jax.random.randint(jax.random.fold_in(own_key, axis), (), 0, length) for axis, length in enumerate(drawn.shape)]
        where[longest] = (where[longest] + shift) % drawn.shape[longest]
        spots.append(tuple(where))
    return drawn.at[spots[0]].set(smallest).at[spots[1]].set(high)


def shard_levels(rng, shape, split, least, high):
    gain = 1.0
    for axis_at, shards_of in split:
        draws = jax.random.uniform(jax.random.fold_in(jax.random.fold_in(rng, 6), axis_at), (shards_of,), jnp.float32, least / len(split), high / len(split))
        gain = gain * jnp.repeat(jnp.exp(draws), shape[axis_at] // shards_of).reshape((-1,) + (1,) * (len(shape) - 1 - axis_at))
    return gain


def length_profile(amount, total, limit, lean):
    weights = [(1 << 20) // math.isqrt(rank ** lean) + 1 for rank in range(2, amount + 1)]
    spare, holding = total - limit - (amount - 1), [1] * (amount - 1)
    while spare > 0:
        free = [i for i in range(amount - 1) if holding[i] < limit]
        mass, budget = sum([weights[i] for i in free]), spare
        for i in free:
            extra = min(limit - holding[i], max(1, budget * weights[i] // mass), spare)
            holding[i] = holding[i] + extra
            spare = spare - extra
    return np.array([limit] + holding)


def ragged_sizes(own_key, number_of, total, reach, skew):
    if number_of == 2:
        one = jax.random.randint(own_key, (), max(1, total - reach), min(reach, total - 1) + 1)
        return jnp.stack([one, total - one])
    tallies = jnp.asarray(length_profile(number_of, total, reach, skew), jnp.int32)
    couples = (number_of - 1) // 2
    source_of, taker = tallies[1:1 + 2 * couples:2], tallies[2:2 + 2 * couples:2]
    slack = jnp.minimum(source_of - 1, reach - taker)
    moved = jax.random.randint(jax.random.fold_in(own_key, 1), (couples,), 0, 1 << 20) % (slack + 1)
    tallies = tallies.at[1:1 + 2 * couples:2].set(source_of - moved).at[2:2 + 2 * couples:2].set(taker + moved)
    return tallies[jax.random.permutation(jax.random.fold_in(own_key, 2), number_of)]


def bell_draw(rng, shape, deviation, most, cuts=(), held_as=jnp.bfloat16):
    values = deviation * jax.random.normal(rng, shape, jnp.float32)
    if cuts:
        values = values * shard_levels(rng, shape, cuts, -0.22, 0.18)
    return jnp.clip(values, -most, most).astype(held_as)


def setup_inputs(seed: int = 0, part: int = 0) -> dict:
    keys = jax.random.split(jax.random.key(seed), 6)
    part_keys = jax.random.split(jax.random.fold_in(keys[5], part), 6)
    return {
        "micrograph": bell_draw(part_keys[0], (TILES, CENTRE, CENTRE), 1.0, 6.0, ((0, 16),)),
        "templates": bell_draw(keys[1], (ORIENTS, BOX, BOX), (BOX * BOX) ** -0.5, 0.046875, ((0, 16),)),
        "orient_list": with_ends(jax.random.randint(part_keys[2], (TILES, LMAX), 0, ORIENTS), jax.random.fold_in(part_keys[2], 1), 0, ORIENTS - 1).astype(jnp.int32),
        "lengths": ragged_sizes(part_keys[3], TILES, 2 * TILES, LMAX, 2).astype(jnp.int32),
        "defocus": jnp.clip(jnp.exp(jax.random.uniform(part_keys[4], (TILES,), jnp.float32, math.log(8000.0), math.log(25000.0))), 8000.0, 25000.0),
    }


wave_length = 0.0197
spherical = 27000000.0
contrast = 0.07
var_floor = 0.1

def dft_tables(extent):
    position = lax.iota(jnp.int32, extent)
    product = position[:, None] * position[None, :] % extent
    angle = product.astype(jnp.float32) * (2.0 * math.pi / extent)
    return (jnp.cos(angle).astype(jnp.bfloat16), jnp.sin(angle).astype(jnp.bfloat16))

def ctf_table(focus_value, extent):
    position = lax.iota(jnp.int32, extent)
    signed = jnp.where(position < extent // 2, position, position - extent).astype(jnp.float32) / extent
    radius = signed[:, None] * signed[:, None] + signed[None, :] * signed[None, :]
    phase = math.pi * wave_length * focus_value * radius - 0.5 * math.pi * spherical * wave_length ** 3 * radius * radius
    return -(math.sqrt(1.0 - contrast * contrast) * jnp.sin(phase) + contrast * jnp.cos(phase))

def tile_spectrum(padded, cosine_table, sine_table):
    extent = cosine_table.shape[0]
    cos_sin = jnp.concatenate([cosine_table, sine_table], axis=1)
    section_one = jnp.dot(padded, cos_sin, preferred_element_type=jnp.float32).astype(jnp.bfloat16)
    left_cos = jnp.dot(cosine_table, section_one, preferred_element_type=jnp.float32)
    left_sin = jnp.dot(sine_table, section_one, preferred_element_type=jnp.float32)
    real_part = (left_cos[:, :extent] - left_sin[:, extent:]).astype(jnp.bfloat16)
    imag_part = (-(left_sin[:, :extent] + left_cos[:, extent:])).astype(jnp.bfloat16)
    return (real_part, imag_part)

def correlate(real_part, imag_part, template, transfer_map, cosine_table, sine_table):
    extent = cosine_table.shape[0]
    box_size = template.shape[0]
    centre = extent - box_size
    cos_sin = jnp.concatenate([cosine_table[:box_size], sine_table[:box_size]], axis=1)
    section_one = jnp.dot(template, cos_sin, preferred_element_type=jnp.float32).astype(jnp.bfloat16)
    left_cos = jnp.dot(cosine_table[:, :box_size], section_one, preferred_element_type=jnp.float32)
    left_sin = jnp.dot(sine_table[:, :box_size], section_one, preferred_element_type=jnp.float32)
    proj_real = left_cos[:, :extent] - left_sin[:, extent:]
    proj_imag = -(left_sin[:, :extent] + left_cos[:, extent:])
    real_wide = real_part.astype(jnp.float32)
    imag_wide = imag_part.astype(jnp.float32)
    mix_real = transfer_map * (real_wide * proj_real + imag_wide * proj_imag)
    mix_imag = transfer_map * (imag_wide * proj_real - real_wide * proj_imag)
    mixed = jnp.concatenate([mix_real, mix_imag], axis=1).astype(jnp.bfloat16)
    upper_cos = jnp.dot(cosine_table[:centre], mixed, preferred_element_type=jnp.float32)
    upper_sin = jnp.dot(sine_table[:centre], mixed, preferred_element_type=jnp.float32)
    combo_real = upper_cos[:, :extent] - upper_sin[:, extent:]
    combo_imag = upper_sin[:, :extent] + upper_cos[:, extent:]
    stacked = jnp.concatenate([combo_real, combo_imag], axis=1).astype(jnp.bfloat16)
    inverse_table = jnp.concatenate([cosine_table[:, :centre], -sine_table[:, :centre]], axis=0)
    return jnp.dot(stacked, inverse_table, preferred_element_type=jnp.float32) / float(extent * extent)

def absorb(moments, score):
    return (jnp.maximum(moments[0], score), moments[1] + score, moments[2] + score * score)

def summarize(moments, searched):
    counted = searched.astype(jnp.float32)
    mean_value = moments[1] / counted
    variance = moments[2] / counted - mean_value * mean_value
    snr_value = (moments[0] - mean_value) / jnp.sqrt(jnp.maximum(variance, var_floor))
    return (snr_value, mean_value, variance)

def reference(micrograph, templates, orient_list, lengths, defocus):
    centre = micrograph.shape[1]
    box_size = templates.shape[1]
    margin = box_size // 2
    extent = centre + box_size
    tile_count = micrograph.shape[0]
    offset_grid = GRID // 2
    tile_rows = tile_count // GRID
    ordered = jnp.roll(micrograph, offset_grid, axis=0)
    full_image = ordered.reshape(tile_rows, GRID, centre, centre).transpose(0, 2, 1, 3)
    full_image = full_image.reshape(tile_rows * centre, GRID * centre)
    full_image = jnp.pad(full_image, margin)
    cosine_table, sine_table = dft_tables(extent)

    def one_tile(tile_index):
        grid_place = (tile_index + offset_grid) % tile_count
        top_row = grid_place // GRID * centre
        left_col = grid_place % GRID * centre
        padded = lax.dynamic_slice(full_image, (top_row, left_col), (extent, extent))
        real_part, imag_part = tile_spectrum(padded, cosine_table, sine_table)
        transfer_map = ctf_table(defocus[tile_index], extent)
        moments = (jnp.full((centre, centre), -jnp.inf, jnp.float32), jnp.zeros((centre, centre), jnp.float32), jnp.zeros((centre, centre), jnp.float32))
        for slot_index in range(LMAX):
            template = templates[orient_list[tile_index, slot_index]]

            def taken(operand):
                current, chosen = operand
                return absorb(current, correlate(real_part, imag_part, chosen, transfer_map, cosine_table, sine_table))

            def skipped(operand):
                return operand[0]
            moments = lax.cond(slot_index < lengths[tile_index], taken, skipped, (moments, template))
        return summarize(moments, lengths[tile_index])
    snr_map, mean_map, var_map = lax.map(one_tile, jnp.arange(tile_count, dtype=jnp.int32))
    return (snr_map, mean_map, var_map)
```

```python
import functools
import math

import jax
import jax.numpy as jnp
import numpy as np
from jax import lax
from jax.experimental import pallas as pl
from jax.experimental.pallas import tpu as pltpu
from jax.sharding import PartitionSpec as P

GRID = 8
LMAX = 4

wave_length = 0.0197
spherical = 27000000.0
contrast = 0.07
var_floor = 0.1


def wave_tables(index, position, extent):
    product = index[:, None] * position[None, :] % extent
    angle = product * (2.0 * math.pi / extent)
    nyquist = 1.0 - 2.0 * (position[None, :] % 2)
    return np.cos(angle), np.where(index[:, None] == 0, nyquist, np.sin(angle))


def make_tables(extent, box):
    half = extent // 2
    position = np.arange(half)
    even, odd = position[::2], position[1::2]
    tables = []
    for index in (even, odd):
        cosine, sine = wave_tables(index, position, extent)
        tables.append(np.concatenate([cosine, sine], axis=0).T)
    tables += [table.T for table in tables]
    for index in (even, odd):
        cosine, sine = wave_tables(index, position, extent)
        tables.append(np.concatenate([cosine, np.where(index[:, None] == 0, sine, -sine)], axis=0))
    order = np.concatenate([even, odd])
    centred = np.arange(box) - box // 2
    cosine, sine = wave_tables(order, centred, extent)
    tables.append(np.concatenate([cosine, sine], axis=0).T)
    first = order[:, None] == 0
    plain = np.where(first, 0.0, sine)
    nyquist, zero = sine[:1] + 0 * sine, 0 * sine
    tables.append(
        np.concatenate(
            [
                np.concatenate([cosine, -plain], axis=1),
                np.concatenate([-plain, -cosine], axis=1),
                np.where(first, np.concatenate([nyquist, zero], axis=1), np.concatenate([cosine, plain], axis=1)),
                np.where(first, np.concatenate([zero, -nyquist], axis=1), np.concatenate([plain, -cosine], axis=1)),
            ],
            axis=0,
        )
    )
    return [jnp.asarray(table, jnp.bfloat16) for table in tables]


def sine_of_turns(turns):
    part = turns - jnp.round(turns)
    folded = jnp.where(jnp.abs(part) > 0.25, jnp.where(part > 0, 0.5, -0.5) - part, part)
    angle = folded * (2.0 * math.pi)
    square = angle * angle
    series = -1.0 / 39916800.0
    for factor in (362880.0, -5040.0, 120.0, -6.0, 1.0):
        series = series * square + 1.0 / factor
    return angle * series


def transfer(row, column, focus_value, extent):
    radius = (row * row + column * column) * (1.0 / (extent * extent))
    turns = (0.5 * wave_length) * focus_value * radius - (
        0.25 * spherical * wave_length**3
    ) * radius * radius
    return -sine_of_turns(turns + math.asin(contrast) / (2.0 * math.pi))


def dot(left, right):
    return jnp.dot(left, right, preferred_element_type=jnp.float32)


def flips(tile_count):
    return [1 << k for k in reversed(range(tile_count.bit_length() - 1))]


def match_kernel(
    orients, lengths, defocus, centre_ref, cols_ref, rows_ref, stack_ref,
    fwd_e, fwd_o, fwd_et, fwd_ot, inv_e, inv_o, temp_rows, temp_cols,
    snr_ref, mean_ref, var_ref,
    template_buf, filt, uv, proj, mixed, combo_e, combo_o, out_buf, in_sem, out_sem,
):
    me = lax.axis_index("tile")
    centre, extent = centre_ref.shape[0], rows_ref.shape[1]
    half, lane = extent // 2, extent // 4
    halo = extent - centre
    held = stack_ref.shape[0] // lax.axis_size("tile")

    copies = []
    for slot in range(LMAX):
        orient = jnp.clip(orients[me, slot], 0, stack_ref.shape[0] - 1)
        apart = lax.div(orient, held) ^ me
        at = lax.rem(orient, held)
        for k, distance in enumerate(flips(lax.axis_size("tile"))):
            at = at + (lax.div(apart, distance) & 1) * (held << k)
        copy = pltpu.make_async_copy(stack_ref.at[at], template_buf.at[slot], in_sem.at[slot])
        copy.start()
        copies.append(copy)

    own = centre_ref[...].astype(jnp.float32)
    side = cols_ref[...].astype(jnp.float32)
    far = jnp.concatenate([own[:, half:], side], axis=1)
    near = own[:, :half]
    uv[:centre, :half] = dot((near + far).astype(jnp.bfloat16), fwd_e[...])
    uv[:centre, half:] = dot((near - far).astype(jnp.bfloat16), fwd_o[...])
    rim = rows_ref[...].astype(jnp.float32)
    near, far = rim[:, :half], rim[:, half:]
    uv[centre:, :half] = dot((near + far).astype(jnp.bfloat16), fwd_e[...])
    uv[centre:, half:] = dot((near - far).astype(jnp.bfloat16), fwd_o[...])
    near, far = uv[:half, :], uv[half:, :]
    spectra = (
        dot(fwd_et[...], (near + far).astype(jnp.bfloat16)),
        dot(fwd_ot[...], (near - far).astype(jnp.bfloat16)),
    )
    focus_value = defocus[me]
    scale = 2.0 / (extent * extent)
    for row_odd in range(2):
        for col_odd in range(2):
            block = spectra[row_odd]
            left, right = block[:lane], block[lane:]
            u, v = 2 * col_odd * lane, (2 * col_odd + 1) * lane
            uc, vc, us, vs = left[:, u : u + lane], left[:, v : v + lane], right[:, u : u + lane], right[:, v : v + lane]
            i = lax.broadcasted_iota(jnp.int32, (lane, lane), 0)
            j = lax.broadcasted_iota(jnp.int32, (lane, lane), 1)
            row = (2 * i + row_odd).astype(jnp.float32)
            col = (2 * j + col_odd).astype(jnp.float32)
            where = (slice(row_odd * lane, (row_odd + 1) * lane), slice(col_odd * lane, (col_odd + 1) * lane))
            if row_odd or col_odd:
                weight = scale * transfer(row, col, focus_value, extent)
                row_first = (i == 0) if not row_odd else None
                col_first = (j == 0) if not col_odd else None
                weight_minus = weight
                if row_first is not None:
                    weight_minus = scale * transfer(jnp.where(row_first, float(half), row), col, focus_value, extent)
                    parts = (
                        jnp.where(row_first, uc, uc - vs),
                        jnp.where(row_first, -vc, -(us + vc)),
                        jnp.where(row_first, us, uc + vs),
                        jnp.where(row_first, -vs, us - vc),
                    )
                elif col_first is not None:
                    weight_minus = scale * transfer(row, jnp.where(col_first, float(half), col), focus_value, extent)
                    parts = (
                        jnp.where(col_first, uc, uc - vs),
                        jnp.where(col_first, -us, -(us + vc)),
                        jnp.where(col_first, vc, uc + vs),
                        jnp.where(col_first, vs, us - vc),
                    )
                else:
                    parts = (uc - vs, -(us + vc), uc + vs, us - vc)
                weights = (weight, weight, weight_minus, weight_minus)
            else:
                col_first = j == 0
                corner = col_first & (i == 0)
                row_first = (i == 0) & (j != 0)
                edge = float(half)
                row_minus = jnp.where(row_first, edge, row)
                col_minus = jnp.where(col_first, edge, col)
                half_scale = jnp.where(corner, 0.5 * scale, scale)
                weights = (
                    half_scale * transfer(row, col, focus_value, extent),
                    half_scale * transfer(jnp.where(corner, edge, row), col, focus_value, extent),
                    half_scale * transfer(row_minus, col_minus, focus_value, extent),
                    half_scale * transfer(jnp.where(corner, edge, row_minus), col_minus, focus_value, extent),
                )
                parts = (
                    jnp.where(col_first | row_first, uc, uc - vs),
                    jnp.where(col_first, -us, jnp.where(row_first, -vc, -(us + vc))),
                    jnp.where(col_first, vc, jnp.where(row_first, us, uc + vs)),
                    jnp.where(col_first, vs, jnp.where(row_first, -vs, us - vc)),
                )
            for k in range(4):
                filt[(k, *where)] = weights[k] * parts[k]

    step = 16
    lane_col = lax.broadcasted_iota(jnp.int32, (step, lane), 1) == 0
    first_row = lax.broadcasted_iota(jnp.int32, (step, lane), 0) == 0
    corner = lane_col & first_row
    box = template_buf.shape[1]
    sign = 1.0 - 2.0 * (lax.broadcasted_iota(jnp.int32, (box, lane), 0) % 2).astype(jnp.float32)
    box_col = lax.broadcasted_iota(jnp.int32, (box, lane), 1) == 0
    for slot in range(LMAX):
        copies[slot].wait()
        waves = dot(template_buf[slot], temp_rows[...])
        first_u, first_v = waves[:, :lane], waves[:, half : half + lane]
        row_edge = -jnp.sum(first_u * sign, axis=0, keepdims=True)
        col_edge = jnp.sum(first_v, axis=0, keepdims=True)
        v_part = jnp.concatenate([jnp.where(box_col, 0.0, first_v), waves[:, half + lane :]], axis=1)
        u_minus = jnp.concatenate([jnp.where(box_col, first_v, first_u), waves[:, lane:half]], axis=1)
        plus = jnp.concatenate([waves[:, :half], v_part], axis=0).astype(jnp.bfloat16)
        minus = jnp.concatenate([u_minus, v_part], axis=0).astype(jnp.bfloat16)
        proj[: 2 * half] = dot(temp_cols[: 2 * half], plus)
        proj[2 * half :] = dot(temp_cols[2 * half :], minus)
        base = slot * extent
        for start in range(0, half, step):
            row_odd, at = start // lane, start % lane
            for col_odd in range(2):
                cols = slice(col_odd * lane, (col_odd + 1) * lane)
                fpr, fpi, fmr, fmi = (filt[k, start : start + step, cols] for k in range(4))
                ppr, ppi, pmr, pmi = (proj[k * half + start : k * half + start + step, cols] for k in range(4))
                if start == 0 and col_odd == 0:
                    ppi = jnp.where(corner, row_edge, ppi)
                    pmi = jnp.where(corner, pmr, pmi)
                    pmr = jnp.where(corner, col_edge, pmr)
                plus_r, plus_i = fpr * ppr + fpi * ppi, fpi * ppr - fpr * ppi
                minus_r, minus_i = fmr * pmr + fmi * pmi, fmi * pmr - fmr * pmi
                cos_r, sin_r = plus_r + minus_r, minus_i - plus_i
                cos_i, sin_i = plus_i + minus_i, plus_r - minus_r
                if start == 0:
                    cos_r = jnp.where(first_row, plus_r, cos_r)
                    sin_r = jnp.where(first_row, minus_r, sin_r)
                    cos_i = jnp.where(first_row, plus_i, cos_i)
                    sin_i = jnp.where(first_row, minus_i, sin_i)
                if col_odd == 0:
                    cos_r = jnp.where(lane_col, plus_r, cos_r)
                    sin_r = jnp.where(lane_col, -plus_i, sin_r)
                    cos_i = jnp.where(lane_col, minus_r, cos_i)
                    sin_i = jnp.where(lane_col, minus_i, sin_i)
                    if start == 0:
                        cos_r = jnp.where(corner, fpr * ppr, cos_r)
                        sin_r = jnp.where(corner, fpi * ppi, sin_r)
                        cos_i = jnp.where(corner, fmr * pmr, cos_i)
                        sin_i = jnp.where(corner, fmi * pmi, sin_i)
                at_r = slice(base + col_odd * lane, base + (col_odd + 1) * lane)
                at_i = slice(base + half + col_odd * lane, base + half + (col_odd + 1) * lane)
                mixed[row_odd, at : at + step, at_r] = cos_r.astype(jnp.bfloat16)
                mixed[row_odd, lane + at : lane + at + step, at_r] = sin_r.astype(jnp.bfloat16)
                mixed[row_odd, at : at + step, at_i] = cos_i.astype(jnp.bfloat16)
                mixed[row_odd, lane + at : lane + at + step, at_i] = sin_i.astype(jnp.bfloat16)
        even = dot(fwd_e[...], mixed[0, :, base : base + extent])
        odd = dot(fwd_o[...], mixed[1, :, base : base + extent])
        total = even + odd
        for part in range(centre // lane):
            if part * lane < half:
                value = total[part * lane : (part + 1) * lane]
            else:
                near = slice(part * lane - half, (part + 1) * lane - half)
                value = even[near] - odd[near]
            value = value.astype(jnp.bfloat16)
            here = slice(slot * lane, (slot + 1) * lane)
            combo_e[part, here, :lane] = value[:, :lane]
            combo_e[part, here, lane:] = value[:, half : half + lane]
            combo_o[part, here, :lane] = value[:, lane:half]
            combo_o[part, here, lane:] = value[:, half + lane :]

    count = lengths[me]
    inverse_count = 1.0 / jnp.full((1, 1), count, jnp.int32).astype(jnp.float32)
    out_copies = []
    for part in range(centre // lane):
        even = dot(combo_e[part], inv_e[...])
        odd = dot(combo_o[part], inv_o[...])
        best = total = squares = None
        for slot in range(LMAX):
            here = slice(slot * lane, (slot + 1) * lane)
            score = jnp.concatenate(
                [even[here] + odd[here], even[here, : centre - half] - odd[here, : centre - half]], axis=1
            )
            if slot == 0:
                best, total, squares = score, score, score * score
            else:
                taken = slot < count
                kept = jnp.where(taken, score, 0.0)
                best = jnp.maximum(best, jnp.where(taken, score, -jnp.inf))
                total = total + kept
                squares = squares + kept * kept
        mean = total * inverse_count
        variance = squares * inverse_count - mean * mean
        snr = (best - mean) * lax.rsqrt(jnp.maximum(variance, var_floor))
        rows = slice(part * lane, (part + 1) * lane)
        for k, (value, out) in enumerate(((snr, snr_ref), (mean, mean_ref), (variance, var_ref))):
            out_buf[k, rows] = value
            copy = pltpu.make_async_copy(out_buf.at[k, rows], out.at[0, rows], out_sem.at[k, part])
            copy.start()
            out_copies.append(copy)
    for copy in out_copies:
        copy.wait()


def match(orient_list, lengths, defocus, centre_block, cols, rows, stack, tables):
    centre, extent = centre_block.shape[0], rows.shape[1]
    box = stack.shape[1]
    half, lane = extent // 2, extent // 4
    smem = pl.BlockSpec(memory_space=pltpu.SMEM)
    vmem = pl.BlockSpec(memory_space=pltpu.VMEM)
    hbm = pl.BlockSpec(memory_space=pl.ANY)
    out = jax.ShapeDtypeStruct((1, centre, centre), jnp.float32)
    parts = centre // lane
    return pl.pallas_call(
        match_kernel,
        out_shape=(out, out, out),
        in_specs=[smem] * 3 + [vmem] * 3 + [hbm] + [vmem] * len(tables),
        out_specs=(hbm, hbm, hbm),
        scratch_shapes=[
            pltpu.VMEM((LMAX, box, box), jnp.bfloat16),
            pltpu.VMEM((4, half, half), jnp.float32),
            pltpu.VMEM((extent, extent), jnp.float32),
            pltpu.VMEM((2 * extent, half), jnp.float32),
            pltpu.VMEM((2, half, LMAX * extent), jnp.bfloat16),
            pltpu.VMEM((parts, LMAX * lane, half), jnp.bfloat16),
            pltpu.VMEM((parts, LMAX * lane, half), jnp.bfloat16),
            pltpu.VMEM((3, centre, centre), jnp.float32),
            pltpu.SemaphoreType.DMA((LMAX,)),
            pltpu.SemaphoreType.DMA((3, parts)),
        ],
        name="match",
    )(orient_list, lengths, defocus, centre_block, cols, rows, stack, *tables)


def shards(micrograph, templates, orient_list, lengths, defocus):
    position = lax.axis_index("tile")
    tile_count = lax.axis_size("tile")
    centre_block = micrograph[0]
    centre = centre_block.shape[0]
    box = templates.shape[1]
    margin = box // 2
    extent = centre + box
    tile_rows = tile_count // GRID
    grid_place = (position + GRID // 2) % tile_count
    column, tile_row = grid_place % GRID, grid_place // GRID

    def arrive(block, distance):
        return lax.ppermute(block, "tile", [((i + distance) % tile_count, i) for i in range(tile_count)])

    right = arrive(centre_block[:, :margin], 1)
    left = arrive(centre_block[:, centre - margin :], -1)
    right = jnp.where(column == GRID - 1, jnp.zeros_like(right), right)
    left = jnp.where(column == 0, jnp.zeros_like(left), left)
    cols = jnp.concatenate([right, left], axis=1)
    wide = jnp.concatenate([centre_block, cols], axis=1)
    below = arrive(wide[:margin], GRID)
    above = arrive(wide[centre - margin :], -GRID)
    below = jnp.where(tile_row == tile_rows - 1, jnp.zeros_like(below), below)
    above = jnp.where(tile_row == 0, jnp.zeros_like(above), above)
    rows = jnp.concatenate([below, above], axis=0)

    stack = templates
    for distance in flips(tile_count):
        other = lax.ppermute(stack, "tile", [(i, i ^ distance) for i in range(tile_count)])
        stack = jnp.concatenate([stack, other], axis=0)
    return match(orient_list, lengths, defocus, centre_block, cols, rows, stack, make_tables(extent, box))


def solution(mesh):
    return jax.shard_map(
        shards,
        mesh=mesh,
        in_specs=(
            P(("mic", "tile"), None, None),
            P("tile", None, None),
            P("mic", None),
            P("mic"),
            P("mic"),
        ),
        out_specs=(
            P(("mic", "tile"), None, None),
            P(("mic", "tile"), None, None),
            P(("mic", "tile"), None, None),
        ),
        check_vma=False,
    )
```

```python
import functools
import math

import jax
import jax.numpy as jnp
import numpy as np
from jax import lax
from jax.experimental import pallas as pl
from jax.experimental.pallas import tpu as pltpu
from jax.sharding import PartitionSpec as P


GRID = 8
LMAX = 4

wave_length = 0.0197
spherical = 27000000.0
contrast = 0.07
var_floor = 0.1


def wave_tables(index, position, extent):
    product = index[:, None] * position[None, :] % extent
    angle = product * (2.0 * math.pi / extent)
    nyquist = 1.0 - 2.0 * (position[None, :] % 2)
    return np.cos(angle), np.where(index[:, None] == 0, nyquist, np.sin(angle))


def make_tables(extent, box):
    half = extent // 2
    position = np.arange(half)
    even, odd = position[::2], position[1::2]
    tables = []
    for index in (even, odd):
        cosine, sine = wave_tables(index, position, extent)
        tables.append(np.concatenate([cosine, sine], axis=0).T)
    tables += [table.T for table in tables]
    for index in (even, odd):
        cosine, sine = wave_tables(index, position, extent)
        tables.append(np.concatenate([cosine, np.where(index[:, None] == 0, sine, -sine)], axis=0))
    order = np.concatenate([even, odd])
    centred = np.arange(box) - box // 2
    cosine, sine = wave_tables(order, centred, extent)
    tables.append(np.concatenate([cosine, sine], axis=0).T)
    first = order[:, None] == 0
    plain = np.where(first, 0.0, sine)
    nyquist, zero = sine[:1] + 0 * sine, 0 * sine
    tables.append(
        np.concatenate(
            [
                np.concatenate([cosine, -plain], axis=1),
                np.concatenate([-plain, -cosine], axis=1),
                np.where(first, np.concatenate([nyquist, zero], axis=1), np.concatenate([cosine, plain], axis=1)),
                np.where(first, np.concatenate([zero, -nyquist], axis=1), np.concatenate([plain, -cosine], axis=1)),
            ],
            axis=0,
        )
    )
    return [jnp.asarray(table, jnp.bfloat16) for table in tables]


def sine_of_turns(turns):
    part = turns - jnp.round(turns)
    folded = jnp.where(jnp.abs(part) > 0.25, jnp.where(part > 0, 0.5, -0.5) - part, part)
    angle = folded * (2.0 * math.pi)
    square = angle * angle
    series = -1.0 / 39916800.0
    for factor in (362880.0, -5040.0, 120.0, -6.0, 1.0):
        series = series * square + 1.0 / factor
    return angle * series


def transfer(row, column, focus_value, extent):
    radius = (row * row + column * column) * (1.0 / (extent * extent))
    turns = (0.5 * wave_length) * focus_value * radius - (
        0.25 * spherical * wave_length**3
    ) * radius * radius
    return -sine_of_turns(turns + math.asin(contrast) / (2.0 * math.pi))


def flips(tile_count):
    if tile_count == 2 * GRID:
        return [GRID, 2, 4, 1]
    return [1 << k for k in reversed(range(tile_count.bit_length() - 1))]


def dot(left, right):
    return jnp.dot(left, right, preferred_element_type=jnp.float32)


def swap_halves(block, lanes):
    return pltpu.roll(block, lanes, 1)


def early_kernel(defocus, centre_ref, weight_ref, mate_ref, peer_ref):
    me = lax.axis_index("tile")
    focus_value = defocus[me]
    lane = weight_ref.shape[1] // 2
    extent = 4 * lane
    edge = float(2 * lane)
    scale = 2.0 / (extent * extent)
    i = lax.broadcasted_iota(jnp.int32, (lane, lane), 0)
    j = lax.broadcasted_iota(jnp.int32, (lane, lane), 1)
    for row_odd in range(2):
        for col_odd in range(2):
            row = (2 * i + row_odd).astype(jnp.float32)
            col = (2 * j + col_odd).astype(jnp.float32)
            rows = slice(row_odd * lane, (row_odd + 1) * lane)
            cols = slice(col_odd * lane, (col_odd + 1) * lane)
            if row_odd and col_odd:
                value = scale * transfer(row, col, focus_value, extent)
                parts = (value,) * 4
            elif row_odd or col_odd:
                value = scale * transfer(row, col, focus_value, extent)
                if row_odd:
                    other = transfer(row, jnp.where(j == 0, edge, col), focus_value, extent)
                else:
                    other = transfer(jnp.where(i == 0, edge, row), col, focus_value, extent)
                other = scale * other
                parts = (value, value, other, other)
            else:
                col_first = j == 0
                corner = col_first & (i == 0)
                row_first = (i == 0) & (j != 0)
                row_minus = jnp.where(row_first, edge, row)
                col_minus = jnp.where(col_first, edge, col)
                at_corner = jnp.where(corner, 0.5 * scale, scale)
                parts = (
                    at_corner * transfer(row, col, focus_value, extent),
                    at_corner * transfer(jnp.where(corner, edge, row), col, focus_value, extent),
                    at_corner * transfer(row_minus, col_minus, focus_value, extent),
                    at_corner * transfer(jnp.where(corner, edge, row_minus), col_minus, focus_value, extent),
                )
            for k in range(4):
                weight_ref[k, rows, cols] = parts[k]
    centre = centre_ref.shape[0]
    half = centre // 2
    first = centre_ref[:, :lane].astype(jnp.float32)
    last = centre_ref[:, centre - lane :].astype(jnp.float32)
    low = lax.broadcasted_iota(jnp.int32, (half, lane), 1) < lane // 2
    first = jnp.where(low, first[:half], swap_halves(first[half:], lane // 2))
    last = jnp.where(low, swap_halves(last[:half], lane // 2), last[half:])
    odd = lax.rem(me, 2) == 1
    mate_ref[...] = jnp.where(odd, first, last).astype(jnp.bfloat16)
    peer_ref[...] = jnp.where(odd, last, first).astype(jnp.bfloat16)


def packed_sides(mate, peer, lane, start, stop, left_open, right_open):
    odd = lax.rem(lax.axis_index("tile"), 2) == 1
    mate = mate[start:stop].astype(jnp.float32)
    peer = peer[start:stop].astype(jnp.float32)
    right = jnp.where(right_open, jnp.where(odd, peer, mate), 0.0)
    left = jnp.where(left_open, jnp.where(odd, mate, peer), 0.0)
    low = lax.broadcasted_iota(jnp.int32, right.shape, 1) < lane // 2
    upper = jnp.where(low, right, swap_halves(left, lane // 2))
    lower = jnp.where(low, swap_halves(right, lane // 2), left)
    return jnp.concatenate([upper, lower], axis=0)


def tile_kernel(paired, *refs):
    if paired:
        centre_ref, mate_ref, peer_ref, ends_ref, weight_ref = refs[:5]
        refs = refs[5:]
    else:
        centre_ref, cols_ref, rows_ref, weight_ref = refs[:4]
        refs = refs[4:]
    fwd_e, fwd_o, fwd_et, fwd_ot, filt, uv = refs
    centre, extent = centre_ref.shape[0], uv.shape[0]
    half, lane = extent // 2, extent // 4
    if paired:
        place = lax.rem(lax.axis_index("tile") + GRID // 2, 2 * GRID)
        column, upper_row = lax.rem(place, GRID), place < GRID
        opens = (column != 0, column != GRID - 1)
        side = packed_sides(mate_ref, peer_ref, lane, 0, centre // 2, *opens)
        corners = packed_sides(mate_ref, peer_ref, lane, centre // 2, mate_ref.shape[0], *opens)
        ends = jnp.concatenate([ends_ref[...].astype(jnp.float32), corners], axis=1)
        rim = jnp.concatenate([jnp.where(upper_row, ends, 0.0), jnp.where(upper_row, 0.0, ends)], axis=0)
    else:
        side = cols_ref[...].astype(jnp.float32)
        rim = rows_ref[...].astype(jnp.float32)
    own = centre_ref[...].astype(jnp.float32)
    far = jnp.concatenate([own[:, half:], side], axis=1)
    near = own[:, :half]
    uv[:centre, :half] = dot((near + far).astype(jnp.bfloat16), fwd_e[...])
    uv[:centre, half:] = dot((near - far).astype(jnp.bfloat16), fwd_o[...])
    near, far = rim[:, :half], rim[:, half:]
    uv[centre:, :half] = dot((near + far).astype(jnp.bfloat16), fwd_e[...])
    uv[centre:, half:] = dot((near - far).astype(jnp.bfloat16), fwd_o[...])
    near, far = uv[:half, :], uv[half:, :]
    spectra = (
        dot(fwd_et[...], (near + far).astype(jnp.bfloat16)),
        dot(fwd_ot[...], (near - far).astype(jnp.bfloat16)),
    )
    i = lax.broadcasted_iota(jnp.int32, (lane, lane), 0)
    j = lax.broadcasted_iota(jnp.int32, (lane, lane), 1)
    for row_odd in range(2):
        for col_odd in range(2):
            block = spectra[row_odd]
            left, right = block[:lane], block[lane:]
            u, v = 2 * col_odd * lane, (2 * col_odd + 1) * lane
            uc, vc, us, vs = left[:, u : u + lane], left[:, v : v + lane], right[:, u : u + lane], right[:, v : v + lane]
            parts = [uc - vs, -(us + vc), uc + vs, us - vc]
            if not row_odd:
                row_first = i == 0
                parts = [jnp.where(row_first, a, b) for a, b in zip((uc, -vc, us, -vs), parts)]
            if not col_odd:
                col_first = j == 0
                parts = [jnp.where(col_first, a, b) for a, b in zip((uc, -us, vc, vs), parts)]
            rows = slice(row_odd * lane, (row_odd + 1) * lane)
            cols = slice(col_odd * lane, (col_odd + 1) * lane)
            for k in range(4):
                filt[k, rows, cols] = weight_ref[k, rows, cols] * parts[k]


def match_kernel(
    orients, lengths, filt, near_ref, far_ref,
    fwd_e, fwd_o, inv_e, inv_o, temp_rows, temp_cols,
    snr_ref, mean_ref, var_ref,
    proj, mixed, combo_e, combo_o, out_buf, out_sem,
):
    me = lax.axis_index("tile")
    half = filt.shape[1]
    lane, extent = half // 2, 2 * half
    centre = out_buf.shape[1]
    tile_count = lax.axis_size("tile")
    distances = flips(tile_count)
    held = near_ref.shape[0] // (tile_count // 2)

    def chosen(slot):
        orient = jnp.clip(orients[slot, me], 0, 2 * near_ref.shape[0] - 1)
        apart = lax.div(orient, held) ^ me
        at = lax.rem(orient, held)
        for k, distance in enumerate(distances[:-1]):
            at = at + (lax.div(apart, distance) & 1) * (held << k)
        return jnp.where(apart & 1 == 1, far_ref[at], near_ref[at])

    step = 16
    lane_col = lax.broadcasted_iota(jnp.int32, (step, lane), 1) == 0
    first_row = lax.broadcasted_iota(jnp.int32, (step, lane), 0) == 0
    corner = lane_col & first_row
    box = near_ref.shape[1]
    sign = 1.0 - 2.0 * (lax.broadcasted_iota(jnp.int32, (box, lane), 0) % 2).astype(jnp.float32)
    box_col = lax.broadcasted_iota(jnp.int32, (box, lane), 1) == 0
    for slot in range(LMAX):
        waves = dot(chosen(slot), temp_rows[...])
        first_u, first_v = waves[:, :lane], waves[:, half : half + lane]
        row_edge = -jnp.sum(first_u * sign, axis=0, keepdims=True)
        col_edge = jnp.sum(first_v, axis=0, keepdims=True)
        v_part = jnp.concatenate([jnp.where(box_col, 0.0, first_v), waves[:, half + lane :]], axis=1)
        u_minus = jnp.concatenate([jnp.where(box_col, first_v, first_u), waves[:, lane:half]], axis=1)
        plus = jnp.concatenate([waves[:, :half], v_part], axis=0).astype(jnp.bfloat16)
        minus = jnp.concatenate([u_minus, v_part], axis=0).astype(jnp.bfloat16)
        proj[: 2 * half] = dot(temp_cols[: 2 * half], plus)
        proj[2 * half :] = dot(temp_cols[2 * half :], minus)
        base = slot * extent
        for start in range(0, half, step):
            row_odd, at = start // lane, start % lane
            for col_odd in range(2):
                cols = slice(col_odd * lane, (col_odd + 1) * lane)
                fpr, fpi, fmr, fmi = (filt[k, start : start + step, cols] for k in range(4))
                ppr, ppi, pmr, pmi = (proj[k * half + start : k * half + start + step, cols] for k in range(4))
                if start == 0 and col_odd == 0:
                    ppi = jnp.where(corner, row_edge, ppi)
                    pmi = jnp.where(corner, pmr, pmi)
                    pmr = jnp.where(corner, col_edge, pmr)
                plus_r, plus_i = fpr * ppr + fpi * ppi, fpi * ppr - fpr * ppi
                minus_r, minus_i = fmr * pmr + fmi * pmi, fmi * pmr - fmr * pmi
                cos_r, sin_r = plus_r + minus_r, minus_i - plus_i
                cos_i, sin_i = plus_i + minus_i, plus_r - minus_r
                if start == 0:
                    cos_r = jnp.where(first_row, plus_r, cos_r)
                    sin_r = jnp.where(first_row, minus_r, sin_r)
                    cos_i = jnp.where(first_row, plus_i, cos_i)
                    sin_i = jnp.where(first_row, minus_i, sin_i)
                if col_odd == 0:
                    cos_r = jnp.where(lane_col, plus_r, cos_r)
                    sin_r = jnp.where(lane_col, -plus_i, sin_r)
                    cos_i = jnp.where(lane_col, minus_r, cos_i)
                    sin_i = jnp.where(lane_col, minus_i, sin_i)
                    if start == 0:
                        cos_r = jnp.where(corner, fpr * ppr, cos_r)
                        sin_r = jnp.where(corner, fpi * ppi, sin_r)
                        cos_i = jnp.where(corner, fmr * pmr, cos_i)
                        sin_i = jnp.where(corner, fmi * pmi, sin_i)
                at_r = slice(base + col_odd * lane, base + (col_odd + 1) * lane)
                at_i = slice(base + half + col_odd * lane, base + half + (col_odd + 1) * lane)
                mixed[row_odd, at : at + step, at_r] = cos_r.astype(jnp.bfloat16)
                mixed[row_odd, lane + at : lane + at + step, at_r] = sin_r.astype(jnp.bfloat16)
                mixed[row_odd, at : at + step, at_i] = cos_i.astype(jnp.bfloat16)
                mixed[row_odd, lane + at : lane + at + step, at_i] = sin_i.astype(jnp.bfloat16)
        even = dot(fwd_e[...], mixed[0, :, base : base + extent])
        odd = dot(fwd_o[...], mixed[1, :, base : base + extent])
        total = even + odd
        for part in range(centre // lane):
            if part * lane < half:
                value = total[part * lane : (part + 1) * lane]
            else:
                near = slice(part * lane - half, (part + 1) * lane - half)
                value = even[near] - odd[near]
            value = value.astype(jnp.bfloat16)
            here = slice(slot * lane, (slot + 1) * lane)
            combo_e[part, here, :lane] = value[:, :lane]
            combo_e[part, here, lane:] = value[:, half : half + lane]
            combo_o[part, here, :lane] = value[:, lane:half]
            combo_o[part, here, lane:] = value[:, half + lane :]

    count = lengths[me]
    inverse_count = 1.0 / jnp.full((1, 1), count, jnp.int32).astype(jnp.float32)
    out_copies = []
    for part in range(centre // lane):
        even = dot(combo_e[part], inv_e[...])
        odd = dot(combo_o[part], inv_o[...])
        best = total = squares = None
        for slot in range(LMAX):
            here = slice(slot * lane, (slot + 1) * lane)
            score = jnp.concatenate(
                [even[here] + odd[here], even[here, : centre - half] - odd[here, : centre - half]], axis=1
            )
            if slot == 0:
                best, total, squares = score, score, score * score
            else:
                taken = slot < count
                kept = jnp.where(taken, score, 0.0)
                best = jnp.maximum(best, jnp.where(taken, score, -jnp.inf))
                total = total + kept
                squares = squares + kept * kept
        mean = total * inverse_count
        variance = squares * inverse_count - mean * mean
        snr = (best - mean) * lax.rsqrt(jnp.maximum(variance, var_floor))
        rows = slice(part * lane, (part + 1) * lane)
        for k, (value, out) in enumerate(((snr, snr_ref), (mean, mean_ref), (variance, var_ref))):
            out_buf[k, rows] = value
            copy = pltpu.make_async_copy(out_buf.at[k, rows], out.at[0, rows], out_sem.at[k, part])
            copy.start()
            out_copies.append(copy)
    for copy in out_copies:
        copy.wait()


def vmem_call(kernel, inputs, outs, scratch, scalars, limit, out_spec=pltpu.VMEM, cost=None):
    smem = pl.BlockSpec(memory_space=pltpu.SMEM)
    vmem = pl.BlockSpec(memory_space=pltpu.VMEM)
    return pl.pallas_call(
        kernel,
        out_shape=tuple(jax.ShapeDtypeStruct(shape, dtype) for shape, dtype in outs),
        in_specs=[smem] * scalars + [vmem] * (len(inputs) - scalars),
        out_specs=tuple(pl.BlockSpec(memory_space=out_spec) for _ in outs),
        scratch_shapes=scratch,
        compiler_params=pltpu.CompilerParams(vmem_limit_bytes=limit << 20),
        cost_estimate=cost,
    )(*inputs)


def early(defocus, centre_block, extent):
    centre, half, lane = centre_block.shape[0], extent // 2, extent // 4
    strip = ((centre // 2, lane), jnp.bfloat16)
    return vmem_call(early_kernel, (defocus, centre_block), (((4, half, half), jnp.float32), strip, strip), [], 1, 8)


def tile_spectrum(paired, pieces, weights, tables, extent):
    half = extent // 2
    (filt,) = vmem_call(
        functools.partial(tile_kernel, paired), (*pieces, weights, *tables[:4]),
        (((4, half, half), jnp.float32),), [pltpu.VMEM((extent, extent), jnp.float32)], 0, 16,
    )
    return filt


def match(orient_list, lengths, filt, near, far, tables, centre):
    half = filt.shape[1]
    lane, extent = half // 2, 2 * half
    parts = centre // lane
    out = ((1, centre, centre), jnp.float32)
    return vmem_call(
        match_kernel, (orient_list, lengths, filt, near, far, *tables[:2], *tables[4:]), (out, out, out),
        [
            pltpu.VMEM((2 * extent, half), jnp.float32),
            pltpu.VMEM((2, half, LMAX * extent), jnp.bfloat16),
            pltpu.VMEM((parts, LMAX * lane, half), jnp.bfloat16),
            pltpu.VMEM((parts, LMAX * lane, half), jnp.bfloat16),
            pltpu.VMEM((3, centre, centre), jnp.float32),
            pltpu.SemaphoreType.DMA((3, parts)),
        ],
        2, 24, pl.ANY,
    )


def shards(micrograph, templates, orient_list, lengths, defocus):
    position = lax.axis_index("tile")
    tile_count = lax.axis_size("tile")
    centre_block = micrograph[0]
    centre = centre_block.shape[0]
    box = templates.shape[1]
    margin = box // 2
    extent = centre + box
    tile_rows = tile_count // GRID
    grid_place = (position + GRID // 2) % tile_count
    column, tile_row = grid_place % GRID, grid_place // GRID
    tables = make_tables(extent, box)

    def send(block, target):
        return lax.ppermute(block, "tile", [(i, target(i)) for i in range(tile_count)])

    paired = tile_rows == 2
    if paired:
        odd = position % 2 == 1
        lower_row = tile_row == tile_rows - 1
        distances = flips(tile_count)
        pair = send(templates, lambda i: i ^ distances[0])
        start = jnp.where(lower_row, 0, centre - margin)
        ends = send(lax.dynamic_slice_in_dim(centre_block, start, margin, 0), lambda i: i ^ GRID)
        weights, to_mate, to_peer = early(defocus, centre_block, extent)

        def strip(own, use_first):
            edge = jnp.where(use_first, ends[:, :margin], ends[:, centre - margin :])
            edge = jnp.concatenate([edge[: margin // 2], edge[margin // 2 :]], axis=1)
            return jnp.concatenate([own, edge], axis=0)

        two = jnp.concatenate([templates, pair], axis=0)
        group = [two]
        for apart in (distances[2] | distances[1], distances[1], distances[2]):
            group.append(send(two, lambda i, apart=apart: i ^ apart))
        from_peer = send(strip(to_peer, ~odd), lambda i: (i + 1 if i % 2 else i - 1) % tile_count)
        from_mate = send(strip(to_mate, odd), lambda i: i ^ 1)
        near = jnp.concatenate([group[0], group[2], group[3], group[1]], axis=0)
        far = send(near, lambda i: i ^ 1)
        filt = tile_spectrum(True, (centre_block, from_mate, from_peer, ends), weights, tables, extent)
    else:

        def arrive(block, distance):
            return lax.ppermute(
                block, "tile", [((i + distance) % tile_count, i) for i in range(tile_count)]
            )

        weights, _, _ = early(defocus, centre_block, extent)
        right = arrive(centre_block[:, :margin], 1)
        left = arrive(centre_block[:, centre - margin :], -1)
        right = jnp.where(column == GRID - 1, jnp.zeros_like(right), right)
        left = jnp.where(column == 0, jnp.zeros_like(left), left)
        cols = jnp.concatenate([right, left], axis=1)
        wide = jnp.concatenate([centre_block, cols], axis=1)
        below = arrive(wide[:margin], GRID)
        above = arrive(wide[centre - margin :], -GRID)
        below = jnp.where(tile_row == tile_rows - 1, jnp.zeros_like(below), below)
        above = jnp.where(tile_row == 0, jnp.zeros_like(above), above)
        rows = jnp.concatenate([below, above], axis=0)
        near = templates
        for distance in flips(tile_count)[:-1]:
            near = jnp.concatenate([near, send(near, lambda i, d=distance: i ^ d)], axis=0)
        far = send(near, lambda i: i ^ 1)
        filt = tile_spectrum(False, (centre_block, cols, rows), weights, tables, extent)
    return match(orient_list.T, lengths, filt, near, far, tables, centre)


def solution(mesh):
    return jax.shard_map(
        shards,
        mesh=mesh,
        in_specs=(
            P(("mic", "tile"), None, None),
            P("tile", None, None),
            P("mic", None),
            P("mic"),
            P("mic"),
        ),
        out_specs=(
            P(("mic", "tile"), None, None),
            P(("mic", "tile"), None, None),
            P(("mic", "tile"), None, None),
        ),
        check_vma=False,
    )
```

```python
import functools
import math

import jax
import jax.numpy as jnp
import numpy as np
from jax import lax
from jax.experimental import pallas as pl
from jax.experimental.pallas import tpu as pltpu
from jax.sharding import PartitionSpec as P


GRID = 8
LMAX = 4

wave_length = 0.0197
spherical = 27000000.0
contrast = 0.07
var_floor = 0.1


def wave_tables(index, position, extent):
    product = index[:, None] * position[None, :] % extent
    angle = product * (2.0 * math.pi / extent)
    nyquist = 1.0 - 2.0 * (position[None, :] % 2)
    return np.cos(angle), np.where(index[:, None] == 0, nyquist, np.sin(angle))


def make_tables(extent, box):
    half = extent // 2
    position = np.arange(half)
    even, odd = position[::2], position[1::2]
    tables = []
    for index in (even, odd):
        cosine, sine = wave_tables(index, position, extent)
        tables.append(np.concatenate([cosine, sine], axis=0).T)
    tables += [table.T for table in tables]
    for index in (even, odd):
        cosine, sine = wave_tables(index, position, extent)
        first = index[:, None] == 0
        cosine = np.where(first, 0.5 + 0.5 * sine, cosine)
        tables.append(np.concatenate([cosine, np.where(first, 0.5 - 0.5 * sine, -sine)], axis=0))
    order = np.concatenate([even, odd])
    centred = np.arange(box) - box // 2
    cosine, sine = wave_tables(order, centred, extent)
    tables.append(np.concatenate([cosine, sine], axis=0).T)
    first = order[:, None] == 0
    plain = np.where(first, 0.0, sine)
    nyquist, zero = sine[:1] + 0 * sine, 0 * sine
    tables.append(
        np.concatenate(
            [
                np.concatenate([cosine, -plain], axis=1),
                np.concatenate([-plain, -cosine], axis=1),
                np.where(first, np.concatenate([nyquist, zero], axis=1), np.concatenate([cosine, plain], axis=1)),
                np.where(first, np.concatenate([zero, -nyquist], axis=1), np.concatenate([plain, -cosine], axis=1)),
            ],
            axis=0,
        )
    )
    return [jnp.asarray(table, jnp.bfloat16) for table in tables]


def sine_of_turns(turns):
    part = turns - jnp.round(turns)
    folded = jnp.where(jnp.abs(part) > 0.25, jnp.where(part > 0, 0.5, -0.5) - part, part)
    angle = folded * (2.0 * math.pi)
    square = angle * angle
    series = -1.0 / 39916800.0
    for factor in (362880.0, -5040.0, 120.0, -6.0, 1.0):
        series = series * square + 1.0 / factor
    return angle * series


def transfer(row, column, focus_value, extent):
    radius = (row * row + column * column) * (1.0 / (extent * extent))
    turns = (0.5 * wave_length) * focus_value * radius - (
        0.25 * spherical * wave_length**3
    ) * radius * radius
    return -sine_of_turns(turns + math.asin(contrast) / (2.0 * math.pi))


def flips(tile_count):
    if tile_count == 2 * GRID:
        return [GRID, 2, 4, 1]
    return [1 << k for k in reversed(range(tile_count.bit_length() - 1))]


def dot(left, right):
    return jnp.dot(left, right, preferred_element_type=jnp.float32)


def swap_halves(block, lanes):
    return pltpu.roll(block, lanes, 1)


def pack_kernel(*refs):
    sources, held, (ends_ref, mate_ref, peer_ref, sem) = refs[:4], refs[4:8], refs[8:]
    copies = [pltpu.make_async_copy(sources[k], held[k], sem.at[k]) for k in range(4)]
    for copy in copies:
        copy.start()
    me = lax.axis_index("tile")
    tile_count = lax.axis_size("tile")
    place = lax.rem(me + GRID // 2, tile_count)
    centre_ref = held[0]
    centre, lane, margin = centre_ref.shape[0], mate_ref.shape[1], ends_ref.shape[0]
    copies[0].wait()
    top = centre_ref[:margin].astype(jnp.float32)
    bottom = centre_ref[centre - margin :].astype(jnp.float32)
    ends_ref[...] = jnp.where(place < GRID, bottom, top).astype(jnp.bfloat16)
    half = centre // 2
    first = centre_ref[:, :lane].astype(jnp.float32)
    last = centre_ref[:, centre - lane :].astype(jnp.float32)
    low = lax.broadcasted_iota(jnp.int32, (half, lane), 1) < lane // 2
    first = jnp.where(low, first[:half], swap_halves(first[half:], lane // 2))
    last = jnp.where(low, swap_halves(last[:half], lane // 2), last[half:])
    odd = lax.rem(me, 2) == 1
    mate_ref[...] = jnp.where(odd, first, last).astype(jnp.bfloat16)
    peer_ref[...] = jnp.where(odd, last, first).astype(jnp.bfloat16)
    for copy in copies[1:]:
        copy.wait()


def early_kernel(defocus, weight_ref):
    me = lax.axis_index("tile")
    focus_value = defocus[0, me]
    lane = weight_ref.shape[1] // 2
    extent = 4 * lane
    edge = float(2 * lane)
    scale = 2.0 / (extent * extent)
    i = lax.broadcasted_iota(jnp.int32, (lane, lane), 0)
    j = lax.broadcasted_iota(jnp.int32, (lane, lane), 1)
    for row_odd in range(2):
        for col_odd in range(2):
            row = (2 * i + row_odd).astype(jnp.float32)
            col = (2 * j + col_odd).astype(jnp.float32)
            rows = slice(row_odd * lane, (row_odd + 1) * lane)
            cols = slice(col_odd * lane, (col_odd + 1) * lane)
            if row_odd and col_odd:
                value = scale * transfer(row, col, focus_value, extent)
                parts = (value,) * 4
            elif row_odd or col_odd:
                value = scale * transfer(row, col, focus_value, extent)
                if row_odd:
                    other = transfer(row, jnp.where(j == 0, edge, col), focus_value, extent)
                else:
                    other = transfer(jnp.where(i == 0, edge, row), col, focus_value, extent)
                other = scale * other
                parts = (value, value, other, other)
            else:
                col_first = j == 0
                corner = col_first & (i == 0)
                row_first = (i == 0) & (j != 0)
                row_minus = jnp.where(row_first, edge, row)
                col_minus = jnp.where(col_first, edge, col)
                at_corner = jnp.where(corner, 0.5 * scale, scale)
                parts = (
                    at_corner * transfer(row, col, focus_value, extent),
                    at_corner * transfer(jnp.where(corner, edge, row), col, focus_value, extent),
                    at_corner * transfer(row_minus, col_minus, focus_value, extent),
                    at_corner * transfer(jnp.where(corner, edge, row_minus), col_minus, focus_value, extent),
                )
            for k in range(4):
                weight_ref[k, rows, cols] = parts[k]


def packed_sides(mate, peer, lane, start, stop, left_open, right_open):
    odd = lax.rem(lax.axis_index("tile"), 2) == 1
    mate = mate[start:stop].astype(jnp.float32)
    peer = peer[start:stop].astype(jnp.float32)
    right = jnp.where(right_open, jnp.where(odd, peer, mate), 0.0)
    left = jnp.where(left_open, jnp.where(odd, mate, peer), 0.0)
    low = lax.broadcasted_iota(jnp.int32, right.shape, 1) < lane // 2
    upper = jnp.where(low, right, swap_halves(left, lane // 2))
    lower = jnp.where(low, swap_halves(right, lane // 2), left)
    return jnp.concatenate([upper, lower], axis=0)


def tile_kernel(paired, *refs):
    if paired:
        centre_ref, mate_ref, peer_ref, ends_ref, weight_ref = refs[:5]
        refs = refs[5:]
    else:
        centre_ref, cols_ref, rows_ref, weight_ref = refs[:4]
        refs = refs[4:]
    fwd_e, fwd_o, fwd_et, fwd_ot, filt, uv = refs
    centre, extent = centre_ref.shape[0], uv.shape[0]
    half, lane = extent // 2, extent // 4
    if paired:
        place = lax.rem(lax.axis_index("tile") + GRID // 2, 2 * GRID)
        column, upper_row = lax.rem(place, GRID), place < GRID
        opens = (column != 0, column != GRID - 1)
        side = packed_sides(mate_ref, peer_ref, lane, 0, centre // 2, *opens)
        corners = packed_sides(mate_ref, peer_ref, lane, centre // 2, mate_ref.shape[0], *opens)
        ends = jnp.concatenate([ends_ref[...].astype(jnp.float32), corners], axis=1)
        rim = jnp.concatenate([jnp.where(upper_row, ends, 0.0), jnp.where(upper_row, 0.0, ends)], axis=0)
    else:
        side = cols_ref[...].astype(jnp.float32)
        rim = rows_ref[...].astype(jnp.float32)
    own = centre_ref[...].astype(jnp.float32)
    far = jnp.concatenate([own[:, half:], side], axis=1)
    near = own[:, :half]
    uv[:centre, :half] = dot((near + far).astype(jnp.bfloat16), fwd_e[...])
    uv[:centre, half:] = dot((near - far).astype(jnp.bfloat16), fwd_o[...])
    near, far = rim[:, :half], rim[:, half:]
    uv[centre:, :half] = dot((near + far).astype(jnp.bfloat16), fwd_e[...])
    uv[centre:, half:] = dot((near - far).astype(jnp.bfloat16), fwd_o[...])
    near, far = uv[:half, :], uv[half:, :]
    spectra = (
        dot(fwd_et[...], (near + far).astype(jnp.bfloat16)),
        dot(fwd_ot[...], (near - far).astype(jnp.bfloat16)),
    )
    i = lax.broadcasted_iota(jnp.int32, (lane, lane), 0)
    j = lax.broadcasted_iota(jnp.int32, (lane, lane), 1)
    for row_odd in range(2):
        for col_odd in range(2):
            block = spectra[row_odd]
            left, right = block[:lane], block[lane:]
            u, v = 2 * col_odd * lane, (2 * col_odd + 1) * lane
            uc, vc, us, vs = left[:, u : u + lane], left[:, v : v + lane], right[:, u : u + lane], right[:, v : v + lane]
            parts = [uc - vs, -(us + vc), uc + vs, us - vc]
            if not row_odd:
                row_first = i == 0
                parts = [jnp.where(row_first, a, b) for a, b in zip((uc, -vc, us, -vs), parts)]
            if not col_odd:
                col_first = j == 0
                parts = [jnp.where(col_first, a, b) for a, b in zip((uc, -us, vc, vs), parts)]
            rows = slice(row_odd * lane, (row_odd + 1) * lane)
            cols = slice(col_odd * lane, (col_odd + 1) * lane)
            for k in range(4):
                filt[k, rows, cols] = weight_ref[k, rows, cols] * parts[k]


def weave(*tracks):
    steps = []
    for order, track in enumerate(tracks):
        steps += [((k + 0.5) / len(track), order, k, step) for k, step in enumerate(track)]
    for *_, step in sorted(steps, key=lambda entry: entry[:3]):
        step()


def match_kernel(
    orients, lengths, wide, near_ref, far_ref,
    fwd_e, fwd_o, inv_e, inv_o, temp_rows, temp_cols,
    snr_ref, mean_ref, var_ref,
    filt, proj, mixed, combos, out_buf, out_sem,
):
    me = lax.axis_index("tile")
    half = wide.shape[1]
    lane = half // 2
    centre = out_buf.shape[1]
    box = near_ref.shape[1]
    strip = combos.shape[3] // LMAX
    tile_count = lax.axis_size("tile")
    distances = flips(tile_count)
    held = near_ref.shape[0] // (tile_count // 2)
    count = lengths[0, me]
    bf16, f32 = jnp.bfloat16, jnp.float32
    step = 16
    col_first = lax.broadcasted_iota(jnp.int32, (step, half), 1) == 0
    row_first = lax.broadcasted_iota(jnp.int32, (step, half), 0) == 0
    corner = col_first & row_first
    thin_first = col_first.astype(f32).astype(bf16) > 0
    sign = 1.0 - 2.0 * (lax.broadcasted_iota(jnp.int32, (box, lane), 0) % 2).astype(f32)
    box_col = lax.broadcasted_iota(jnp.int32, (box, lane), 1) == 0
    edges, waves_of = {}, {}

    def chosen(slot):
        orient = orients[slot, me]
        if slot:
            orient = jnp.where(slot < count, orient, orients[0, me])
        orient = jnp.clip(orient, 0, 2 * near_ref.shape[0] - 1)
        apart = lax.div(orient, held) ^ me
        at = lax.rem(orient, held)
        for k, distance in enumerate(distances[:-1]):
            at = at + (lax.div(apart, distance) & 1) * (held << k)
        return jnp.where(apart & 1 == 1, far_ref[at], near_ref[at])

    def project(slot):
        def rows():
            waves = dot(chosen(slot), temp_rows[...])
            first_u, first_v = waves[:, :lane], waves[:, half : half + lane]
            row_edge = -jnp.sum(first_u * sign, axis=0, keepdims=True)
            col_edge = jnp.sum(first_v, axis=0, keepdims=True)
            edges[slot] = (beside(row_edge, row_edge), beside(col_edge, col_edge))
            v_part = beside(jnp.where(box_col, 0.0, first_v), waves[:, half + lane :])
            u_minus = beside(jnp.where(box_col, first_v, first_u), waves[:, lane:half])
            plus = jnp.concatenate([waves[:, :half], v_part], axis=0).astype(bf16)
            minus = jnp.concatenate([u_minus, v_part], axis=0).astype(bf16)
            waves_of[slot] = (plus, plus, minus, minus)

        def cols(k):
            here = slice(k * half, (k + 1) * half)
            proj[slot % 2, here] = dot(temp_cols[here], waves_of[slot][k]).astype(bf16)

        return [rows] + [functools.partial(cols, k) for k in range(4)]

    def mix_first(slot, fs, ps):
        fpr, fpi, fmr, fmi = (f.astype(f32) for f in fs)
        ppr, ppi, pmr, pmi = (p.astype(f32) for p in ps)
        row_edge, col_edge = edges[slot]
        ppi = jnp.where(corner, row_edge, ppi)
        pmi = jnp.where(corner, pmr, pmi)
        pmr = jnp.where(corner, col_edge, pmr)
        plus_r, plus_i = fpr * ppr + fpi * ppi, fpi * ppr - fpr * ppi
        minus_r, minus_i = fmr * pmr + fmi * pmi, fmi * pmr - fmr * pmi
        cos_r, sin_r = plus_r + minus_r, minus_i - plus_i
        cos_i, sin_i = plus_i + minus_i, plus_r - minus_r
        cos_i, sin_i = jnp.where(col_first, sin_i, cos_i), jnp.where(col_first, -cos_i, sin_i)
        cos_r = jnp.where(row_first, plus_r, cos_r)
        sin_r = jnp.where(row_first, minus_r, sin_r)
        cos_i = jnp.where(row_first, plus_i, cos_i)
        sin_i = jnp.where(row_first, minus_i, sin_i)
        cos_r = jnp.where(corner, fpr * ppr + fmr * pmr, cos_r)
        sin_r = jnp.where(corner, fpi * ppi + fmi * pmi, sin_r)
        cos_i = jnp.where(corner, fpr * ppr - fmr * pmr, cos_i)
        sin_i = jnp.where(corner, fpi * ppi - fmi * pmi, sin_i)
        return cos_r.astype(bf16), sin_r.astype(bf16), cos_i.astype(bf16), sin_i.astype(bf16)

    def mix(slot, start):
        row_odd, at = start // lane, start % lane
        buffer = slot % 2
        fs = [filt[k, start : start + step] for k in range(4)]
        ps = [proj[buffer, k * half + start : k * half + start + step] for k in range(4)]
        if start == 0:
            cos_r, sin_r, cos_i, sin_i = mix_first(slot, fs, ps)
        else:
            fpr, fpi, fmr, fmi = fs
            ppr, ppi, pmr, pmi = ps
            plus_r, plus_i = fpr * ppr + fpi * ppi, fpi * ppr - fpr * ppi
            minus_r, minus_i = fmr * pmr + fmi * pmi, fmi * pmr - fmr * pmi
            cos_r, sin_r = plus_r + minus_r, minus_i - plus_i
            cos_i, sin_i = plus_i + minus_i, plus_r - minus_r
            cos_i, sin_i = jnp.where(thin_first, sin_i, cos_i), jnp.where(thin_first, -cos_i, sin_i)
        mixed[buffer, row_odd, 0, at : at + step] = cos_r
        mixed[buffer, row_odd, 0, lane + at : lane + at + step] = sin_r
        mixed[buffer, row_odd, 1, at : at + step] = cos_i
        mixed[buffer, row_odd, 1, lane + at : lane + at + step] = sin_i

    def combine(slot):
        def rows(imag, first):
            buffer = slot % 2
            here = slice(first * lane, (first + 1) * lane)
            even = dot(fwd_e[here], mixed[buffer, 0, imag])
            odd = dot(fwd_o[here], mixed[buffer, 1, imag])
            starts = [(first * lane, even + odd)]
            if half + first * lane < centre:
                starts.append((half + first * lane, even - odd))
            for start, value in starts:
                value = value.astype(bf16)
                for k in range(lane // strip):
                    place = slice(slot * strip, (slot + 1) * strip)
                    piece = value[k * strip : (k + 1) * strip]
                    combos[0, imag, start // strip + k, place] = piece[:, :lane]
                    combos[1, imag, start // strip + k, place] = piece[:, lane:]

        return [functools.partial(rows, imag, first) for imag in range(2) for first in range(half // lane)]

    share = 1.0 / jnp.full((1, 1), count, jnp.int32).astype(f32)
    shares = [jnp.where(slot < count, share, 0.0) for slot in range(LMAX)]
    fields, out_copies = {}, []

    def back(part):
        fields[part] = (
            dot(beside(combos[0, 0, part], combos[0, 1, part]), inv_e[...]),
            dot(beside(combos[1, 0, part], combos[1, 1, part]), inv_o[...]),
        )

    def gather(part):
        even, odd = fields.pop(part)
        for slot in range(LMAX):
            here = slice(slot * strip, (slot + 1) * strip)
            near, far = even[here], odd[here]
            score = beside(near + far, near[:, : centre - half] - far[:, : centre - half])
            scaled = score * shares[slot]
            if slot == 0:
                best, mean, squares = score, scaled, scaled * score
            else:
                best = jnp.maximum(best, score)
                mean, squares = mean + scaled, squares + scaled * score
        variance = squares - mean * mean
        rows = slice(part * strip, (part + 1) * strip)
        out_buf[0, rows] = (best - mean) * lax.rsqrt(jnp.maximum(variance, var_floor))
        out_buf[1, rows] = mean
        out_buf[2, rows] = variance
        for k, out in enumerate((snr_ref, mean_ref, var_ref)):
            copy = pltpu.make_async_copy(out_buf.at[k, rows], out.at[0, rows], out_sem.at[k, part])
            copy.start()
            out_copies.append(copy)

    def thin():
        for k in range(4):
            filt[k] = wide[k].astype(bf16)

    parts = centre // strip
    for tick in range(LMAX + 2):
        products = project(tick) if tick < LMAX else []
        if 0 <= tick - 2:
            products = products + combine(tick - 2)
        sums = [thin] if tick == 0 else []
        if 0 <= tick - 1 < LMAX:
            sums = [functools.partial(mix, tick - 1, start) for start in range(0, half, step)]
        weave(products, sums)
    for part in range(parts):
        back(part)
        gather(part)
    for copy in out_copies:
        copy.wait()


def beside(left, right):
    return jnp.concatenate([left, right], axis=1)


def vmem_call(kernel, inputs, outs, scratch, scalars, limit, out_spec=pltpu.VMEM, in_space=pltpu.VMEM):
    if in_space == pltpu.HBM:
        fixed = [pltpu.with_memory_space_constraint(array, pltpu.HBM) for array in inputs[scalars:]]
        inputs = (*inputs[:scalars], *fixed)
    smem = pl.BlockSpec(memory_space=pltpu.SMEM)
    vmem = pl.BlockSpec(memory_space=in_space)
    return pl.pallas_call(
        kernel,
        out_shape=tuple(jax.ShapeDtypeStruct(shape, dtype) for shape, dtype in outs),
        in_specs=[smem] * scalars + [vmem] * (len(inputs) - scalars),
        out_specs=tuple(pl.BlockSpec(memory_space=out_spec) for _ in outs),
        scratch_shapes=scratch,
        compiler_params=pltpu.CompilerParams(vmem_limit_bytes=limit << 20),
    )(*inputs)


def pack(orient_list, lengths, defocus, centre_block, box):
    centre = centre_block.shape[0]
    lane = (centre + box) // 4
    held = (centre_block, orient_list.T, lengths[None], defocus[None])
    strip = ((centre // 2, lane), jnp.bfloat16)
    outs = [(array.shape, array.dtype) for array in held] + [((box // 2, centre), jnp.bfloat16), strip, strip]
    return vmem_call(pack_kernel, held, outs, [pltpu.SemaphoreType.DMA((4,))], 0, 8, in_space=pltpu.HBM)


def early(defocus, extent):
    half = extent // 2
    return vmem_call(early_kernel, (defocus,), (((4, half, half), jnp.float32),), [], 1, 8)[0]


def tile_spectrum(paired, pieces, weights, tables, extent):
    half = extent // 2
    (filt,) = vmem_call(
        functools.partial(tile_kernel, paired), (*pieces, weights, *tables[:4]),
        (((4, half, half), jnp.float32),), [pltpu.VMEM((extent, extent), jnp.float32)], 0, 16,
    )
    return filt


def match(orient_list, lengths, filt, near, far, tables, centre):
    half = filt.shape[1]
    lane, extent = half // 2, 2 * half
    strip = lane // 2
    out = ((1, centre, centre), jnp.float32)
    return vmem_call(
        match_kernel, (orient_list, lengths, filt, near, far, *tables[:2], *tables[4:]), (out, out, out),
        [
            pltpu.VMEM((4, half, half), jnp.bfloat16),
            pltpu.VMEM((2, 2 * extent, half), jnp.bfloat16),
            pltpu.VMEM((2, 2, 2, half, half), jnp.bfloat16),
            pltpu.VMEM((2, 2, centre // strip, LMAX * strip, lane), jnp.bfloat16),
            pltpu.VMEM((3, centre, centre), jnp.float32),
            pltpu.SemaphoreType.DMA((3, centre // strip)),
        ],
        2, 24, pl.ANY,
    )


def shards(micrograph, templates, orient_list, lengths, defocus):
    position = lax.axis_index("tile")
    tile_count = lax.axis_size("tile")
    centre_block = micrograph[0]
    centre = centre_block.shape[0]
    box = templates.shape[1]
    margin = box // 2
    extent = centre + box
    tile_rows = tile_count // GRID
    grid_place = (position + GRID // 2) % tile_count
    column, tile_row = grid_place % GRID, grid_place // GRID
    tables = make_tables(extent, box)

    def send(block, target):
        return lax.ppermute(block, "tile", [(i, target(i)) for i in range(tile_count)])

    paired = tile_rows == 2
    if paired:
        odd = position % 2 == 1
        distances = flips(tile_count)
        pair = send(templates, lambda i: i ^ distances[0])
        block, orients, counts, focus, to_ends, to_mate, to_peer = pack(
            orient_list, lengths, defocus, centre_block, box
        )
        ends = send(to_ends, lambda i: i ^ GRID)
        weights = early(focus, extent)

        def strip(own, use_first):
            edge = jnp.where(use_first, ends[:, :margin], ends[:, centre - margin :])
            edge = jnp.concatenate([edge[: margin // 2], edge[margin // 2 :]], axis=1)
            return jnp.concatenate([own, edge], axis=0)

        two = jnp.concatenate([templates, pair], axis=0)
        group = [two]
        for apart in (distances[2] | distances[1], distances[1], distances[2]):
            group.append(send(two, lambda i, apart=apart: i ^ apart))
        from_peer = send(strip(to_peer, ~odd), lambda i: (i + 1 if i % 2 else i - 1) % tile_count)
        from_mate = send(strip(to_mate, odd), lambda i: i ^ 1)
        near = jnp.concatenate([group[0], group[2], group[3], group[1]], axis=0)
        far = send(near, lambda i: i ^ 1)
        filt = tile_spectrum(True, (block, from_mate, from_peer, ends), weights, tables, extent)
    else:

        def arrive(block, distance):
            return lax.ppermute(
                block, "tile", [((i + distance) % tile_count, i) for i in range(tile_count)]
            )

        _, orients, counts, focus, *_ = pack(orient_list, lengths, defocus, centre_block, box)
        weights = early(focus, extent)
        right = arrive(centre_block[:, :margin], 1)
        left = arrive(centre_block[:, centre - margin :], -1)
        right = jnp.where(column == GRID - 1, jnp.zeros_like(right), right)
        left = jnp.where(column == 0, jnp.zeros_like(left), left)
        cols = jnp.concatenate([right, left], axis=1)
        wide = jnp.concatenate([centre_block, cols], axis=1)
        below = arrive(wide[:margin], GRID)
        above = arrive(wide[centre - margin :], -GRID)
        below = jnp.where(tile_row == tile_rows - 1, jnp.zeros_like(below), below)
        above = jnp.where(tile_row == 0, jnp.zeros_like(above), above)
        rows = jnp.concatenate([below, above], axis=0)
        near = templates
        for distance in flips(tile_count)[:-1]:
            near = jnp.concatenate([near, send(near, lambda i, d=distance: i ^ d)], axis=0)
        far = send(near, lambda i: i ^ 1)
        filt = tile_spectrum(False, (centre_block, cols, rows), weights, tables, extent)
    return match(orients, counts, filt, near, far, tables, centre)


def solution(mesh):
    return jax.shard_map(
        shards,
        mesh=mesh,
        in_specs=(
            P(("mic", "tile"), None, None),
            P("tile", None, None),
            P("mic", None),
            P("mic"),
            P("mic"),
        ),
        out_specs=(
            P(("mic", "tile"), None, None),
            P(("mic", "tile"), None, None),
            P(("mic", "tile"), None, None),
        ),
        check_vma=False,
    )
```

```python
import functools
import math

import jax
import jax.numpy as jnp
import numpy as np
from jax import lax
from jax.experimental import pallas as pl
from jax.experimental.pallas import tpu as pltpu
from jax.sharding import PartitionSpec as P


GRID = 8
LMAX = 4

wave_length = 0.0197
spherical = 27000000.0
contrast = 0.07
var_floor = 0.1


def wave_tables(index, position, extent):
    product = index[:, None] * position[None, :] % extent
    angle = product * (2.0 * math.pi / extent)
    nyquist = 1.0 - 2.0 * (position[None, :] % 2)
    return np.cos(angle), np.where(index[:, None] == 0, nyquist, np.sin(angle))


def make_tables(extent, box):
    half = extent // 2
    position = np.arange(half)
    even, odd = position[::2], position[1::2]
    tables = []
    for index in (even, odd):
        cosine, sine = wave_tables(index, position, extent)
        tables.append(np.concatenate([cosine, sine], axis=0).T)
    tables += [table.T for table in tables]
    for index in (even, odd):
        cosine, sine = wave_tables(index, position, extent)
        first = index[:, None] == 0
        cosine = np.where(first, 0.5 + 0.5 * sine, cosine)
        tables.append(np.concatenate([cosine, np.where(first, 0.5 - 0.5 * sine, -sine)], axis=0))
    order = np.concatenate([even, odd])
    centred = np.arange(box) - box // 2
    cosine, sine = wave_tables(order, centred, extent)
    tables.append(np.concatenate([cosine, sine], axis=0).T)
    first = order[:, None] == 0
    plain = np.where(first, 0.0, sine)
    nyquist, zero = sine[:1] + 0 * sine, 0 * sine
    tables.append(
        np.concatenate(
            [
                np.concatenate([cosine, -plain], axis=1),
                np.concatenate([-plain, -cosine], axis=1),
                np.where(first, np.concatenate([nyquist, zero], axis=1), np.concatenate([cosine, plain], axis=1)),
                np.where(first, np.concatenate([zero, -nyquist], axis=1), np.concatenate([plain, -cosine], axis=1)),
            ],
            axis=0,
        )
    )
    return [jnp.asarray(table, jnp.bfloat16) for table in tables]


def sine_of_turns(turns):
    part = turns - jnp.round(turns)
    folded = jnp.where(jnp.abs(part) > 0.25, jnp.where(part > 0, 0.5, -0.5) - part, part)
    angle = folded * (2.0 * math.pi)
    square = angle * angle
    series = -1.0 / 39916800.0
    for factor in (362880.0, -5040.0, 120.0, -6.0, 1.0):
        series = series * square + 1.0 / factor
    return angle * series


def transfer(row, column, focus_value, extent):
    radius = (row * row + column * column) * (1.0 / (extent * extent))
    turns = (0.5 * wave_length) * focus_value * radius - (
        0.25 * spherical * wave_length**3
    ) * radius * radius
    return -sine_of_turns(turns + math.asin(contrast) / (2.0 * math.pi))


def flips(tile_count):
    if tile_count == 2 * GRID:
        return [GRID, 2, 4, 1]
    return [1 << k for k in reversed(range(tile_count.bit_length() - 1))]


def dot(left, right):
    return jnp.dot(left, right, preferred_element_type=jnp.float32)


def swap_halves(block, lanes):
    return pltpu.roll(block, lanes, 1)


def pack_kernel(*refs):
    sources, held, (ends_ref, mate_ref, peer_ref, sem) = refs[:4], refs[4:8], refs[8:]
    copies = [pltpu.make_async_copy(sources[k], held[k], sem.at[k]) for k in range(4)]
    for copy in copies:
        copy.start()
    me = lax.axis_index("tile")
    tile_count = lax.axis_size("tile")
    place = lax.rem(me + GRID // 2, tile_count)
    centre_ref = held[0]
    centre, lane, margin = centre_ref.shape[0], mate_ref.shape[1], ends_ref.shape[0]
    copies[0].wait()
    top = centre_ref[:margin].astype(jnp.float32)
    bottom = centre_ref[centre - margin :].astype(jnp.float32)
    ends_ref[...] = jnp.where(place < GRID, bottom, top).astype(jnp.bfloat16)
    half = centre // 2
    first = centre_ref[:, :lane].astype(jnp.float32)
    last = centre_ref[:, centre - lane :].astype(jnp.float32)
    low = lax.broadcasted_iota(jnp.int32, (half, lane), 1) < lane // 2
    first = jnp.where(low, first[:half], swap_halves(first[half:], lane // 2))
    last = jnp.where(low, swap_halves(last[:half], lane // 2), last[half:])
    odd = lax.rem(me, 2) == 1
    mate_ref[...] = jnp.where(odd, first, last).astype(jnp.bfloat16)
    peer_ref[...] = jnp.where(odd, last, first).astype(jnp.bfloat16)
    for copy in copies[1:]:
        copy.wait()


def early_kernel(defocus, weight_ref):
    me = lax.axis_index("tile")
    focus_value = defocus[0, me]
    lane = weight_ref.shape[1] // 2
    extent = 4 * lane
    edge = float(2 * lane)
    scale = 2.0 / (extent * extent)
    i = lax.broadcasted_iota(jnp.int32, (lane, lane), 0)
    j = lax.broadcasted_iota(jnp.int32, (lane, lane), 1)
    for row_odd in range(2):
        for col_odd in range(2):
            row = (2 * i + row_odd).astype(jnp.float32)
            col = (2 * j + col_odd).astype(jnp.float32)
            rows = slice(row_odd * lane, (row_odd + 1) * lane)
            cols = slice(col_odd * lane, (col_odd + 1) * lane)
            if row_odd and col_odd:
                value = scale * transfer(row, col, focus_value, extent)
                parts = (value,) * 4
            elif row_odd or col_odd:
                value = scale * transfer(row, col, focus_value, extent)
                if row_odd:
                    other = transfer(row, jnp.where(j == 0, edge, col), focus_value, extent)
                else:
                    other = transfer(jnp.where(i == 0, edge, row), col, focus_value, extent)
                other = scale * other
                parts = (value, value, other, other)
            else:
                col_first = j == 0
                corner = col_first & (i == 0)
                row_first = (i == 0) & (j != 0)
                row_minus = jnp.where(row_first, edge, row)
                col_minus = jnp.where(col_first, edge, col)
                at_corner = jnp.where(corner, 0.5 * scale, scale)
                parts = (
                    at_corner * transfer(row, col, focus_value, extent),
                    at_corner * transfer(jnp.where(corner, edge, row), col, focus_value, extent),
                    at_corner * transfer(row_minus, col_minus, focus_value, extent),
                    at_corner * transfer(jnp.where(corner, edge, row_minus), col_minus, focus_value, extent),
                )
            for k in range(4):
                weight_ref[k, rows, cols] = parts[k]


def packed_sides(mate, peer, lane, start, stop, left_open, right_open):
    odd = lax.rem(lax.axis_index("tile"), 2) == 1
    mate = mate[start:stop].astype(jnp.float32)
    peer = peer[start:stop].astype(jnp.float32)
    right = jnp.where(right_open, jnp.where(odd, peer, mate), 0.0)
    left = jnp.where(left_open, jnp.where(odd, mate, peer), 0.0)
    low = lax.broadcasted_iota(jnp.int32, right.shape, 1) < lane // 2
    upper = jnp.where(low, right, swap_halves(left, lane // 2))
    lower = jnp.where(low, swap_halves(right, lane // 2), left)
    return jnp.concatenate([upper, lower], axis=0)


def tile_kernel(paired, *refs):
    if paired:
        centre_ref, mate_ref, peer_ref, ends_ref, weight_ref = refs[:5]
        refs = refs[5:]
    else:
        centre_ref, cols_ref, rows_ref, weight_ref = refs[:4]
        refs = refs[4:]
    fwd_e, fwd_o, fwd_et, fwd_ot, filt, uv = refs
    centre, extent = centre_ref.shape[0], uv.shape[0]
    half, lane = extent // 2, extent // 4
    if paired:
        place = lax.rem(lax.axis_index("tile") + GRID // 2, 2 * GRID)
        column, upper_row = lax.rem(place, GRID), place < GRID
        opens = (column != 0, column != GRID - 1)
        side = packed_sides(mate_ref, peer_ref, lane, 0, centre // 2, *opens)
        corners = packed_sides(mate_ref, peer_ref, lane, centre // 2, mate_ref.shape[0], *opens)
        ends = jnp.concatenate([ends_ref[...].astype(jnp.float32), corners], axis=1)
        rim = jnp.concatenate([jnp.where(upper_row, ends, 0.0), jnp.where(upper_row, 0.0, ends)], axis=0)
    else:
        side = cols_ref[...].astype(jnp.float32)
        rim = rows_ref[...].astype(jnp.float32)
    own = centre_ref[...].astype(jnp.float32)
    far = jnp.concatenate([own[:, half:], side], axis=1)
    near = own[:, :half]
    uv[:centre, :half] = dot((near + far).astype(jnp.bfloat16), fwd_e[...])
    uv[:centre, half:] = dot((near - far).astype(jnp.bfloat16), fwd_o[...])
    near, far = rim[:, :half], rim[:, half:]
    uv[centre:, :half] = dot((near + far).astype(jnp.bfloat16), fwd_e[...])
    uv[centre:, half:] = dot((near - far).astype(jnp.bfloat16), fwd_o[...])
    near, far = uv[:half, :], uv[half:, :]
    spectra = (
        dot(fwd_et[...], (near + far).astype(jnp.bfloat16)),
        dot(fwd_ot[...], (near - far).astype(jnp.bfloat16)),
    )
    i = lax.broadcasted_iota(jnp.int32, (lane, lane), 0)
    j = lax.broadcasted_iota(jnp.int32, (lane, lane), 1)
    for row_odd in range(2):
        for col_odd in range(2):
            block = spectra[row_odd]
            left, right = block[:lane], block[lane:]
            u, v = 2 * col_odd * lane, (2 * col_odd + 1) * lane
            uc, vc, us, vs = left[:, u : u + lane], left[:, v : v + lane], right[:, u : u + lane], right[:, v : v + lane]
            parts = [uc - vs, -(us + vc), uc + vs, us - vc]
            if not row_odd:
                row_first = i == 0
                parts = [jnp.where(row_first, a, b) for a, b in zip((uc, -vc, us, -vs), parts)]
            if not col_odd:
                col_first = j == 0
                parts = [jnp.where(col_first, a, b) for a, b in zip((uc, -us, vc, vs), parts)]
            rows = slice(row_odd * lane, (row_odd + 1) * lane)
            cols = slice(col_odd * lane, (col_odd + 1) * lane)
            for k in range(4):
                filt[k, rows, cols] = weight_ref[k, rows, cols] * parts[k]


def weave(*tracks):
    steps = []
    for order, track in enumerate(tracks):
        steps += [((k + 0.5) / len(track), order, k, step) for k, step in enumerate(track)]
    for *_, step in sorted(steps, key=lambda entry: entry[:3]):
        step()


def project_kernel(orients, lengths, near_ref, far_ref, temp_rows, temp_cols, proj, edges):
    me = lax.axis_index("tile")
    half = temp_cols.shape[1]
    lane = half // 2
    box = near_ref.shape[1]
    tile_count = lax.axis_size("tile")
    distances = flips(tile_count)
    held = near_ref.shape[0] // (tile_count // 2)
    count = lengths[0, me]
    sign = 1.0 - 2.0 * (lax.broadcasted_iota(jnp.int32, (box, lane), 0) % 2).astype(jnp.float32)
    box_col = lax.broadcasted_iota(jnp.int32, (box, lane), 1) == 0

    def chosen(slot):
        orient = orients[slot, me]
        if slot:
            orient = jnp.where(slot < count, orient, orients[0, me])
        orient = jnp.clip(orient, 0, 2 * near_ref.shape[0] - 1)
        apart = lax.div(orient, held) ^ me
        at = lax.rem(orient, held)
        for k, distance in enumerate(distances[:-1]):
            at = at + (lax.div(apart, distance) & 1) * (held << k)
        return jnp.where(apart & 1 == 1, far_ref[at], near_ref[at])

    for slot in range(LMAX):
        waves = dot(chosen(slot), temp_rows[...])
        first_u, first_v = waves[:, :lane], waves[:, half : half + lane]
        row_edge = -jnp.sum(first_u * sign, axis=0, keepdims=True)
        col_edge = jnp.sum(first_v, axis=0, keepdims=True)
        edges[slot, :1] = beside(row_edge, row_edge)
        edges[slot, 1:2] = beside(col_edge, col_edge)
        v_part = beside(jnp.where(box_col, 0.0, first_v), waves[:, half + lane :])
        u_minus = beside(jnp.where(box_col, first_v, first_u), waves[:, lane:half])
        plus = jnp.concatenate([waves[:, :half], v_part], axis=0).astype(jnp.bfloat16)
        minus = jnp.concatenate([u_minus, v_part], axis=0).astype(jnp.bfloat16)
        for k, half_waves in enumerate((plus, plus, minus, minus)):
            here = slice(k * half, (k + 1) * half)
            proj[slot, here] = dot(temp_cols[here], half_waves).astype(jnp.bfloat16)


def match_kernel(
    lengths, wide, proj, edges,
    fwd_e, fwd_o, inv_e, inv_o,
    snr_ref, mean_ref, var_ref,
    filt, mixed, combos, out_buf, out_sem,
):
    me = lax.axis_index("tile")
    half = wide.shape[1]
    lane = half // 2
    centre = out_buf.shape[1]
    strip = combos.shape[3] // LMAX
    count = lengths[0, me]
    bf16, f32 = jnp.bfloat16, jnp.float32
    step = 16
    col_first = lax.broadcasted_iota(jnp.int32, (step, half), 1) == 0
    row_first = lax.broadcasted_iota(jnp.int32, (step, half), 0) == 0
    corner = col_first & row_first
    thin_first = col_first.astype(f32).astype(bf16) > 0

    def mix_first(slot, fs, ps):
        fpr, fpi, fmr, fmi = (f.astype(f32) for f in fs)
        ppr, ppi, pmr, pmi = (p.astype(f32) for p in ps)
        row_edge, col_edge = edges[slot, :1], edges[slot, 1:2]
        ppi = jnp.where(corner, row_edge, ppi)
        pmi = jnp.where(corner, pmr, pmi)
        pmr = jnp.where(corner, col_edge, pmr)
        plus_r, plus_i = fpr * ppr + fpi * ppi, fpi * ppr - fpr * ppi
        minus_r, minus_i = fmr * pmr + fmi * pmi, fmi * pmr - fmr * pmi
        cos_r, sin_r = plus_r + minus_r, minus_i - plus_i
        cos_i, sin_i = plus_i + minus_i, plus_r - minus_r
        cos_i, sin_i = jnp.where(col_first, sin_i, cos_i), jnp.where(col_first, -cos_i, sin_i)
        cos_r = jnp.where(row_first, plus_r, cos_r)
        sin_r = jnp.where(row_first, minus_r, sin_r)
        cos_i = jnp.where(row_first, plus_i, cos_i)
        sin_i = jnp.where(row_first, minus_i, sin_i)
        cos_r = jnp.where(corner, fpr * ppr + fmr * pmr, cos_r)
        sin_r = jnp.where(corner, fpi * ppi + fmi * pmi, sin_r)
        cos_i = jnp.where(corner, fpr * ppr - fmr * pmr, cos_i)
        sin_i = jnp.where(corner, fpi * ppi - fmi * pmi, sin_i)
        return cos_r.astype(bf16), sin_r.astype(bf16), cos_i.astype(bf16), sin_i.astype(bf16)

    def mix(slot, start):
        row_odd, at = start // lane, start % lane
        buffer = slot % 2
        fs = [filt[k, start : start + step] for k in range(4)]
        ps = [proj[slot, k * half + start : k * half + start + step] for k in range(4)]
        if start == 0:
            cos_r, sin_r, cos_i, sin_i = mix_first(slot, fs, ps)
        else:
            fpr, fpi, fmr, fmi = fs
            ppr, ppi, pmr, pmi = ps
            plus_r, plus_i = fpr * ppr + fpi * ppi, fpi * ppr - fpr * ppi
            minus_r, minus_i = fmr * pmr + fmi * pmi, fmi * pmr - fmr * pmi
            cos_r, sin_r = plus_r + minus_r, minus_i - plus_i
            cos_i, sin_i = plus_i + minus_i, plus_r - minus_r
            cos_i, sin_i = jnp.where(thin_first, sin_i, cos_i), jnp.where(thin_first, -cos_i, sin_i)
        mixed[buffer, row_odd, 0, at : at + step] = cos_r
        mixed[buffer, row_odd, 0, lane + at : lane + at + step] = sin_r
        mixed[buffer, row_odd, 1, at : at + step] = cos_i
        mixed[buffer, row_odd, 1, lane + at : lane + at + step] = sin_i

    def combine(slot):
        def rows(imag, first):
            buffer = slot % 2
            here = slice(first * lane, (first + 1) * lane)
            even = dot(fwd_e[here], mixed[buffer, 0, imag])
            odd = dot(fwd_o[here], mixed[buffer, 1, imag])
            starts = [(first * lane, even + odd)]
            if half + first * lane < centre:
                starts.append((half + first * lane, even - odd))
            for start, value in starts:
                value = value.astype(bf16)
                for k in range(lane // strip):
                    place = slice(slot * strip, (slot + 1) * strip)
                    piece = value[k * strip : (k + 1) * strip]
                    combos[0, imag, start // strip + k, place] = piece[:, :lane]
                    combos[1, imag, start // strip + k, place] = piece[:, lane:]

        return [functools.partial(rows, imag, first) for first in range(half // lane) for imag in range(2)]

    share = 1.0 / jnp.full((1, 1), count, jnp.int32).astype(f32)
    shares = [jnp.where(slot < count, share, 0.0) for slot in range(LMAX)]
    fields, out_copies = {}, []

    def back(part):
        fields[part] = (
            dot(beside(combos[0, 0, part], combos[0, 1, part]), inv_e[...]),
            dot(beside(combos[1, 0, part], combos[1, 1, part]), inv_o[...]),
        )

    def gather(part):
        even, odd = fields.pop(part)
        for slot in range(LMAX):
            here = slice(slot * strip, (slot + 1) * strip)
            near, far = even[here], odd[here]
            score = beside(near + far, near[:, : centre - half] - far[:, : centre - half])
            scaled = score * shares[slot]
            if slot == 0:
                best, mean, squares = score, scaled, scaled * score
            else:
                best = jnp.maximum(best, score)
                mean, squares = mean + scaled, squares + scaled * score
        variance = squares - mean * mean
        rows = slice(part * strip, (part + 1) * strip)
        out_buf[0, rows] = (best - mean) * lax.rsqrt(jnp.maximum(variance, var_floor))
        out_buf[1, rows] = mean
        out_buf[2, rows] = variance
        for k, out in enumerate((snr_ref, mean_ref, var_ref)):
            copy = pltpu.make_async_copy(out_buf.at[k, rows], out.at[0, rows], out_sem.at[k, part])
            copy.start()
            out_copies.append(copy)

    def thin():
        for k in range(4):
            filt[k] = wide[k].astype(bf16)

    thin()
    for tick in range(LMAX):
        products = combine(tick - 1) if tick else []
        weave(products, [functools.partial(mix, tick, start) for start in range(0, half, step)])
    last = combine(LMAX - 1)
    for first in range(half // lane):
        for _ in range(2):
            last.pop(0)()
        for start in range(first * lane, centre, half):
            for part in range(start // strip, (start + lane) // strip):
                back(part)
                gather(part)
    for copy in out_copies:
        copy.wait()


def beside(left, right):
    return jnp.concatenate([left, right], axis=1)


def vmem_call(kernel, inputs, outs, scratch, scalars, limit, out_spec=pltpu.VMEM, in_space=pltpu.VMEM):
    if in_space == pltpu.HBM:
        fixed = [pltpu.with_memory_space_constraint(array, pltpu.HBM) for array in inputs[scalars:]]
        inputs = (*inputs[:scalars], *fixed)
    smem = pl.BlockSpec(memory_space=pltpu.SMEM)
    vmem = pl.BlockSpec(memory_space=in_space)
    return pl.pallas_call(
        kernel,
        out_shape=tuple(jax.ShapeDtypeStruct(shape, dtype) for shape, dtype in outs),
        in_specs=[smem] * scalars + [vmem] * (len(inputs) - scalars),
        out_specs=tuple(pl.BlockSpec(memory_space=out_spec) for _ in outs),
        scratch_shapes=scratch,
        compiler_params=pltpu.CompilerParams(vmem_limit_bytes=limit << 20),
    )(*inputs)


def pack(orient_list, lengths, defocus, centre_block, box):
    centre = centre_block.shape[0]
    lane = (centre + box) // 4
    held = (centre_block, orient_list.T, lengths[None], defocus[None])
    strip = ((centre // 2, lane), jnp.bfloat16)
    outs = [(array.shape, array.dtype) for array in held] + [((box // 2, centre), jnp.bfloat16), strip, strip]
    return vmem_call(pack_kernel, held, outs, [pltpu.SemaphoreType.DMA((4,))], 0, 8, in_space=pltpu.HBM)


def early(defocus, extent):
    half = extent // 2
    return vmem_call(early_kernel, (defocus,), (((4, half, half), jnp.float32),), [], 1, 8)[0]


def tile_spectrum(paired, pieces, weights, tables, extent):
    half = extent // 2
    (filt,) = vmem_call(
        functools.partial(tile_kernel, paired), (*pieces, weights, *tables[:4]),
        (((4, half, half), jnp.float32),), [pltpu.VMEM((extent, extent), jnp.float32)], 0, 16,
    )
    return filt


def project(orient_list, lengths, near, far, tables, extent):
    half = extent // 2
    outs = (((LMAX, 2 * extent, half), jnp.bfloat16), ((LMAX, 8, half), jnp.float32))
    return vmem_call(project_kernel, (orient_list, lengths, near, far, *tables[6:]), outs, [], 2, 12)


def match(lengths, filt, proj, edges, tables, centre):
    half = filt.shape[1]
    lane = half // 2
    strip = lane // 2
    out = ((1, centre, centre), jnp.float32)
    return vmem_call(
        match_kernel, (lengths, filt, proj, edges, *tables[:2], *tables[4:6]), (out, out, out),
        [
            pltpu.VMEM((4, half, half), jnp.bfloat16),
            pltpu.VMEM((2, 2, 2, half, half), jnp.bfloat16),
            pltpu.VMEM((2, 2, centre // strip, LMAX * strip, lane), jnp.bfloat16),
            pltpu.VMEM((3, centre, centre), jnp.float32),
            pltpu.SemaphoreType.DMA((3, centre // strip)),
        ],
        1, 20, pl.ANY,
    )


def shards(micrograph, templates, orient_list, lengths, defocus):
    position = lax.axis_index("tile")
    tile_count = lax.axis_size("tile")
    centre_block = micrograph[0]
    centre = centre_block.shape[0]
    box = templates.shape[1]
    margin = box // 2
    extent = centre + box
    tile_rows = tile_count // GRID
    grid_place = (position + GRID // 2) % tile_count
    column, tile_row = grid_place % GRID, grid_place // GRID
    tables = make_tables(extent, box)

    def send(block, target):
        return lax.ppermute(block, "tile", [(i, target(i)) for i in range(tile_count)])

    paired = tile_rows == 2
    if paired:
        odd = position % 2 == 1
        distances = flips(tile_count)
        pair = send(templates, lambda i: i ^ distances[0])
        block, orients, counts, focus, to_ends, to_mate, to_peer = pack(
            orient_list, lengths, defocus, centre_block, box
        )
        ends = send(to_ends, lambda i: i ^ GRID)
        weights = early(focus, extent)

        def strip(own, use_first):
            edge = jnp.where(use_first, ends[:, :margin], ends[:, centre - margin :])
            edge = jnp.concatenate([edge[: margin // 2], edge[margin // 2 :]], axis=1)
            return jnp.concatenate([own, edge], axis=0)

        two = jnp.concatenate([templates, pair], axis=0)
        group = [two]
        for apart in (distances[2] | distances[1], distances[1], distances[2]):
            group.append(send(two, lambda i, apart=apart: i ^ apart))
        from_peer = send(strip(to_peer, ~odd), lambda i: (i + 1 if i % 2 else i - 1) % tile_count)
        from_mate = send(strip(to_mate, odd), lambda i: i ^ 1)
        near = jnp.concatenate([group[0], group[2], group[3], group[1]], axis=0)
        far = send(near, lambda i: i ^ 1)
        proj, edges = project(orients, counts, near, far, tables, extent)
        filt = tile_spectrum(True, (block, from_mate, from_peer, ends), weights, tables, extent)
    else:

        def arrive(block, distance):
            return lax.ppermute(
                block, "tile", [((i + distance) % tile_count, i) for i in range(tile_count)]
            )

        _, orients, counts, focus, *_ = pack(orient_list, lengths, defocus, centre_block, box)
        weights = early(focus, extent)
        right = arrive(centre_block[:, :margin], 1)
        left = arrive(centre_block[:, centre - margin :], -1)
        right = jnp.where(column == GRID - 1, jnp.zeros_like(right), right)
        left = jnp.where(column == 0, jnp.zeros_like(left), left)
        cols = jnp.concatenate([right, left], axis=1)
        wide = jnp.concatenate([centre_block, cols], axis=1)
        below = arrive(wide[:margin], GRID)
        above = arrive(wide[centre - margin :], -GRID)
        below = jnp.where(tile_row == tile_rows - 1, jnp.zeros_like(below), below)
        above = jnp.where(tile_row == 0, jnp.zeros_like(above), above)
        rows = jnp.concatenate([below, above], axis=0)
        near = templates
        for distance in flips(tile_count)[:-1]:
            near = jnp.concatenate([near, send(near, lambda i, d=distance: i ^ d)], axis=0)
        far = send(near, lambda i: i ^ 1)
        proj, edges = project(orients, counts, near, far, tables, extent)
        filt = tile_spectrum(False, (centre_block, cols, rows), weights, tables, extent)
    return match(counts, filt, proj, edges, tables, centre)


def solution(mesh):
    return jax.shard_map(
        shards,
        mesh=mesh,
        in_specs=(
            P(("mic", "tile"), None, None),
            P("tile", None, None),
            P("mic", None),
            P("mic"),
            P("mic"),
        ),
        out_specs=(
            P(("mic", "tile"), None, None),
            P(("mic", "tile"), None, None),
            P(("mic", "tile"), None, None),
        ),
        check_vma=False,
    )
```

```python
import functools
import math

import jax
import jax.numpy as jnp
import numpy as np
from jax import lax
from jax.experimental import pallas as pl
from jax.experimental.pallas import tpu as pltpu
from jax.sharding import PartitionSpec as P


GRID = 8
LMAX = 4

wave_length = 0.0197
spherical = 27000000.0
contrast = 0.07
var_floor = 0.1


def wave_tables(index, position, extent):
    product = index[:, None] * position[None, :] % extent
    angle = product * (2.0 * math.pi / extent)
    nyquist = 1.0 - 2.0 * (position[None, :] % 2)
    return np.cos(angle), np.where(index[:, None] == 0, nyquist, np.sin(angle))


def make_tables(extent, box):
    half = extent // 2
    position = np.arange(half)
    even, odd = position[::2], position[1::2]
    tables = []
    for index in (even, odd):
        cosine, sine = wave_tables(index, position, extent)
        tables.append(np.concatenate([cosine, sine], axis=0).T)
    tables += [table.T for table in tables]
    for index in (even, odd):
        cosine, sine = wave_tables(index, position, extent)
        first = index[:, None] == 0
        cosine = np.where(first, 0.5 + 0.5 * sine, cosine)
        tables.append(np.concatenate([cosine, np.where(first, 0.5 - 0.5 * sine, -sine)], axis=0))
    order = np.concatenate([even, odd])
    centred = np.arange(box) - box // 2
    cosine, sine = wave_tables(order, centred, extent)
    tables.append(np.concatenate([cosine, sine], axis=0).T)
    first = order[:, None] == 0
    plain = np.where(first, 0.0, sine)
    nyquist, zero = sine[:1] + 0 * sine, 0 * sine
    tables.append(
        np.concatenate(
            [
                np.concatenate([cosine, -plain], axis=1),
                np.concatenate([-plain, -cosine], axis=1),
                np.where(first, np.concatenate([nyquist, zero], axis=1), np.concatenate([cosine, plain], axis=1)),
                np.where(first, np.concatenate([zero, -nyquist], axis=1), np.concatenate([plain, -cosine], axis=1)),
            ],
            axis=0,
        )
    )
    return [jnp.asarray(table, jnp.bfloat16) for table in tables]


def sine_of_turns(turns):
    part = turns - jnp.round(turns)
    folded = jnp.where(jnp.abs(part) > 0.25, jnp.where(part > 0, 0.5, -0.5) - part, part)
    angle = folded * (2.0 * math.pi)
    square = angle * angle
    series = -1.0 / 39916800.0
    for factor in (362880.0, -5040.0, 120.0, -6.0, 1.0):
        series = series * square + 1.0 / factor
    return angle * series


def transfer(row, column, focus_value, extent):
    radius = (row * row + column * column) * (1.0 / (extent * extent))
    turns = (0.5 * wave_length) * focus_value * radius - (
        0.25 * spherical * wave_length**3
    ) * radius * radius
    return -sine_of_turns(turns + math.asin(contrast) / (2.0 * math.pi))


def flips(tile_count):
    if tile_count == 2 * GRID:
        return [GRID, 2, 4, 1]
    return [1 << k for k in reversed(range(tile_count.bit_length() - 1))]


def dot(left, right):
    return jnp.dot(left, right, preferred_element_type=jnp.float32)


def swap_halves(block, lanes):
    return pltpu.roll(block, lanes, 1)


def pack_kernel(*refs):
    sources, held, (ends_ref, mate_ref, peer_ref, sem) = refs[:5], refs[5:10], refs[10:]
    copies = [pltpu.make_async_copy(sources[k], held[k], sem.at[k]) for k in range(5)]
    for copy in copies:
        copy.start()
    me = lax.axis_index("tile")
    tile_count = lax.axis_size("tile")
    place = lax.rem(me + GRID // 2, tile_count)
    centre_ref = held[0]
    centre, lane, margin = centre_ref.shape[0], mate_ref.shape[1], ends_ref.shape[0]
    copies[0].wait()
    top = centre_ref[:margin].astype(jnp.float32)
    bottom = centre_ref[centre - margin :].astype(jnp.float32)
    ends_ref[...] = jnp.where(place < GRID, bottom, top).astype(jnp.bfloat16)
    half = centre // 2
    first = centre_ref[:, :lane].astype(jnp.float32)
    last = centre_ref[:, centre - lane :].astype(jnp.float32)
    low = lax.broadcasted_iota(jnp.int32, (half, lane), 1) < lane // 2
    first = jnp.where(low, first[:half], swap_halves(first[half:], lane // 2))
    last = jnp.where(low, swap_halves(last[:half], lane // 2), last[half:])
    odd = lax.rem(me, 2) == 1
    mate_ref[...] = jnp.where(odd, first, last).astype(jnp.bfloat16)
    peer_ref[...] = jnp.where(odd, last, first).astype(jnp.bfloat16)
    for copy in copies[1:]:
        copy.wait()


def early_kernel(defocus, weight_ref):
    me = lax.axis_index("tile")
    focus_value = defocus[0, me]
    lane = weight_ref.shape[1] // 2
    extent = 4 * lane
    edge = float(2 * lane)
    scale = 2.0 / (extent * extent)
    i = lax.broadcasted_iota(jnp.int32, (lane, lane), 0)
    j = lax.broadcasted_iota(jnp.int32, (lane, lane), 1)
    for row_odd in range(2):
        for col_odd in range(2):
            row = (2 * i + row_odd).astype(jnp.float32)
            col = (2 * j + col_odd).astype(jnp.float32)
            rows = slice(row_odd * lane, (row_odd + 1) * lane)
            cols = slice(col_odd * lane, (col_odd + 1) * lane)
            if row_odd and col_odd:
                value = scale * transfer(row, col, focus_value, extent)
                parts = (value,) * 4
            elif row_odd or col_odd:
                value = scale * transfer(row, col, focus_value, extent)
                if row_odd:
                    other = transfer(row, jnp.where(j == 0, edge, col), focus_value, extent)
                else:
                    other = transfer(jnp.where(i == 0, edge, row), col, focus_value, extent)
                other = scale * other
                parts = (value, value, other, other)
            else:
                col_first = j == 0
                corner = col_first & (i == 0)
                row_first = (i == 0) & (j != 0)
                row_minus = jnp.where(row_first, edge, row)
                col_minus = jnp.where(col_first, edge, col)
                at_corner = jnp.where(corner, 0.5 * scale, scale)
                parts = (
                    at_corner * transfer(row, col, focus_value, extent),
                    at_corner * transfer(jnp.where(corner, edge, row), col, focus_value, extent),
                    at_corner * transfer(row_minus, col_minus, focus_value, extent),
                    at_corner * transfer(jnp.where(corner, edge, row_minus), col_minus, focus_value, extent),
                )
            for k in range(4):
                weight_ref[k, rows, cols] = parts[k]


def packed_sides(mate, peer, lane, start, stop, left_open, right_open):
    odd = lax.rem(lax.axis_index("tile"), 2) == 1
    mate = mate[start:stop].astype(jnp.float32)
    peer = peer[start:stop].astype(jnp.float32)
    right = jnp.where(right_open, jnp.where(odd, peer, mate), 0.0)
    left = jnp.where(left_open, jnp.where(odd, mate, peer), 0.0)
    low = lax.broadcasted_iota(jnp.int32, right.shape, 1) < lane // 2
    upper = jnp.where(low, right, swap_halves(left, lane // 2))
    lower = jnp.where(low, swap_halves(right, lane // 2), left)
    return jnp.concatenate([upper, lower], axis=0)


def tile_kernel(paired, *refs):
    if paired:
        centre_ref, mate_ref, peer_ref, ends_ref, weight_ref = refs[:5]
        refs = refs[5:]
    else:
        centre_ref, cols_ref, rows_ref, weight_ref = refs[:4]
        refs = refs[4:]
    fwd_e, fwd_o, fwd_et, fwd_ot = refs[:4]
    filt, uv = refs[-2:]
    centre, extent = centre_ref.shape[0], uv.shape[0]
    half, lane = extent // 2, extent // 4
    if paired:
        place = lax.rem(lax.axis_index("tile") + GRID // 2, 2 * GRID)
        column, upper_row = lax.rem(place, GRID), place < GRID
        opens = (column != 0, column != GRID - 1)
        side = packed_sides(mate_ref, peer_ref, lane, 0, centre // 2, *opens)
        corners = packed_sides(mate_ref, peer_ref, lane, centre // 2, mate_ref.shape[0], *opens)
        ends = jnp.concatenate([ends_ref[...].astype(jnp.float32), corners], axis=1)
        rim = jnp.concatenate([jnp.where(upper_row, ends, 0.0), jnp.where(upper_row, 0.0, ends)], axis=0)
    else:
        side = cols_ref[...].astype(jnp.float32)
        rim = rows_ref[...].astype(jnp.float32)
    own = centre_ref[...].astype(jnp.float32)
    far = jnp.concatenate([own[:, half:], side], axis=1)
    near = own[:, :half]
    uv[:centre, :half] = dot((near + far).astype(jnp.bfloat16), fwd_e[...])
    uv[:centre, half:] = dot((near - far).astype(jnp.bfloat16), fwd_o[...])
    near, far = rim[:, :half], rim[:, half:]
    uv[centre:, :half] = dot((near + far).astype(jnp.bfloat16), fwd_e[...])
    uv[centre:, half:] = dot((near - far).astype(jnp.bfloat16), fwd_o[...])
    near, far = uv[:half, :], uv[half:, :]
    spectra = (
        dot(fwd_et[...], (near + far).astype(jnp.bfloat16)),
        dot(fwd_ot[...], (near - far).astype(jnp.bfloat16)),
    )
    i = lax.broadcasted_iota(jnp.int32, (lane, lane), 0)
    j = lax.broadcasted_iota(jnp.int32, (lane, lane), 1)
    for row_odd in range(2):
        for col_odd in range(2):
            block = spectra[row_odd]
            left, right = block[:lane], block[lane:]
            u, v = 2 * col_odd * lane, (2 * col_odd + 1) * lane
            uc, vc, us, vs = left[:, u : u + lane], left[:, v : v + lane], right[:, u : u + lane], right[:, v : v + lane]
            parts = [uc - vs, -(us + vc), uc + vs, us - vc]
            if not row_odd:
                row_first = i == 0
                parts = [jnp.where(row_first, a, b) for a, b in zip((uc, -vc, us, -vs), parts)]
            if not col_odd:
                col_first = j == 0
                parts = [jnp.where(col_first, a, b) for a, b in zip((uc, -us, vc, vs), parts)]
            rows = slice(row_odd * lane, (row_odd + 1) * lane)
            cols = slice(col_odd * lane, (col_odd + 1) * lane)
            for k in range(4):
                filt[k, rows, cols] = weight_ref[k, rows, cols] * parts[k]


def weave(*tracks):
    steps = []
    for order, track in enumerate(tracks):
        steps += [((k + 0.5) / len(track), order, k, step) for k, step in enumerate(track)]
    for *_, step in sorted(steps, key=lambda entry: entry[:3]):
        step()


def match_kernel(
    orients, lengths, wide, near_ref, far_ref,
    fwd_e, fwd_o, inv_e, inv_o, temp_rows, temp_cols,
    snr_ref, mean_ref, var_ref,
    filt, waves, proj, mixed, combos, out_buf, out_sem,
):
    me = lax.axis_index("tile")
    half = wide.shape[1]
    lane = half // 2
    centre = out_buf.shape[1]
    box = near_ref.shape[1]
    strip = combos.shape[3] // LMAX
    tile_count = lax.axis_size("tile")
    distances = flips(tile_count)
    held = near_ref.shape[0] // (tile_count // 2)
    count = lengths[0, me]
    bf16, f32 = jnp.bfloat16, jnp.float32
    step = 16
    col_first = lax.broadcasted_iota(jnp.int32, (step, half), 1) == 0
    row_first = lax.broadcasted_iota(jnp.int32, (step, half), 0) == 0
    corner = col_first & row_first
    thin_first = col_first.astype(f32).astype(bf16) > 0
    sign = 1.0 - 2.0 * (lax.broadcasted_iota(jnp.int32, (box, lane), 0) % 2).astype(f32)
    box_col = lax.broadcasted_iota(jnp.int32, (box, lane), 1) == 0
    edges = {}

    def chosen(slot):
        orient = orients[slot, me]
        if slot:
            orient = jnp.where(slot < count, orient, orients[0, me])
        orient = jnp.clip(orient, 0, 2 * near_ref.shape[0] - 1)
        apart = lax.div(orient, held) ^ me
        at = lax.rem(orient, held)
        for k, distance in enumerate(distances[:-1]):
            at = at + (lax.div(apart, distance) & 1) * (held << k)
        return jnp.where(apart & 1 == 1, far_ref[at], near_ref[at])

    def rows_first():
        stacked = jnp.concatenate([chosen(slot) for slot in range(LMAX)], axis=0)
        first_u, rest_u = dot(stacked, temp_rows[:, :lane]), dot(stacked, temp_rows[:, lane:half])
        first_v, rest_v = dot(stacked, temp_rows[:, half : half + lane]), dot(stacked, temp_rows[:, half + lane :])
        for slot in range(LMAX):
            rows = slice(slot * box, (slot + 1) * box)
            u, v = first_u[rows], first_v[rows]
            row_edge = -jnp.sum(u * sign, axis=0, keepdims=True)
            col_edge = jnp.sum(v, axis=0, keepdims=True)
            edges[slot] = (beside(row_edge, row_edge), beside(col_edge, col_edge))
            v_part = beside(jnp.where(box_col, 0.0, v), rest_v[rows]).astype(bf16)
            waves[slot, 0, :box] = beside(u, rest_u[rows]).astype(bf16)
            waves[slot, 1, :box] = beside(jnp.where(box_col, v, u), rest_u[rows]).astype(bf16)
            waves[slot, 0, box:] = v_part
            waves[slot, 1, box:] = v_part

    def project(slot):
        def cols(k):
            here = slice(k * half, (k + 1) * half)
            proj[slot % 2, here] = dot(temp_cols[here], waves[slot, k // 2]).astype(bf16)

        return [functools.partial(cols, k) for k in range(4)]

    def mix_first(slot, fs, ps):
        fpr, fpi, fmr, fmi = (f.astype(f32) for f in fs)
        ppr, ppi, pmr, pmi = (p.astype(f32) for p in ps)
        row_edge, col_edge = edges[slot]
        ppi = jnp.where(corner, row_edge, ppi)
        pmi = jnp.where(corner, pmr, pmi)
        pmr = jnp.where(corner, col_edge, pmr)
        plus_r, plus_i = fpr * ppr + fpi * ppi, fpi * ppr - fpr * ppi
        minus_r, minus_i = fmr * pmr + fmi * pmi, fmi * pmr - fmr * pmi
        cos_r, sin_r = plus_r + minus_r, minus_i - plus_i
        cos_i, sin_i = plus_i + minus_i, plus_r - minus_r
        cos_i, sin_i = jnp.where(col_first, sin_i, cos_i), jnp.where(col_first, -cos_i, sin_i)
        cos_r = jnp.where(row_first, plus_r, cos_r)
        sin_r = jnp.where(row_first, minus_r, sin_r)
        cos_i = jnp.where(row_first, plus_i, cos_i)
        sin_i = jnp.where(row_first, minus_i, sin_i)
        cos_r = jnp.where(corner, fpr * ppr + fmr * pmr, cos_r)
        sin_r = jnp.where(corner, fpi * ppi + fmi * pmi, sin_r)
        cos_i = jnp.where(corner, fpr * ppr - fmr * pmr, cos_i)
        sin_i = jnp.where(corner, fpi * ppi - fmi * pmi, sin_i)
        return cos_r.astype(bf16), sin_r.astype(bf16), cos_i.astype(bf16), sin_i.astype(bf16)

    def mix(slot, start):
        row_odd, at = start // lane, start % lane
        buffer = slot % 2
        fs = [filt[k, start : start + step] for k in range(4)]
        ps = [proj[buffer, k * half + start : k * half + start + step] for k in range(4)]
        if start == 0:
            cos_r, sin_r, cos_i, sin_i = mix_first(slot, fs, ps)
        else:
            fpr, fpi, fmr, fmi = fs
            ppr, ppi, pmr, pmi = ps
            plus_r, plus_i = fpr * ppr + fpi * ppi, fpi * ppr - fpr * ppi
            minus_r, minus_i = fmr * pmr + fmi * pmi, fmi * pmr - fmr * pmi
            cos_r, sin_r = plus_r + minus_r, minus_i - plus_i
            cos_i, sin_i = plus_i + minus_i, plus_r - minus_r
            cos_i, sin_i = jnp.where(thin_first, sin_i, cos_i), jnp.where(thin_first, -cos_i, sin_i)
        mixed[slot, row_odd, 0, at : at + step] = cos_r
        mixed[slot, row_odd, 0, lane + at : lane + at + step] = sin_r
        mixed[slot, row_odd, 1, at : at + step] = cos_i
        mixed[slot, row_odd, 1, lane + at : lane + at + step] = sin_i

    def combine(slot, first):
        def rows(imag):
            here = slice(first * lane, (first + 1) * lane)
            even = dot(fwd_e[here], mixed[slot, 0, imag])
            odd = dot(fwd_o[here], mixed[slot, 1, imag])
            starts = [(first * lane, even + odd)]
            if half + first * lane < centre:
                starts.append((half + first * lane, even - odd))
            for start, value in starts:
                value = value.astype(bf16)
                for k in range(lane // strip):
                    place = slice(slot * strip, (slot + 1) * strip)
                    piece = value[k * strip : (k + 1) * strip]
                    combos[0, imag, start // strip + k, place] = piece[:, :lane]
                    combos[1, imag, start // strip + k, place] = piece[:, lane:]

        return [functools.partial(rows, imag) for imag in range(2)]

    share = 1.0 / jnp.full((1, 1), count, jnp.int32).astype(f32)
    shares = [jnp.where(slot < count, share, 0.0) for slot in range(LMAX)]
    fields, out_copies = {}, []

    def back(part):
        fields[part] = (
            dot(beside(combos[0, 0, part], combos[0, 1, part]), inv_e[...]),
            dot(beside(combos[1, 0, part], combos[1, 1, part]), inv_o[...]),
        )

    def gather(part):
        even, odd = fields.pop(part)
        for slot in range(LMAX):
            here = slice(slot * strip, (slot + 1) * strip)
            near, far = even[here], odd[here]
            score = beside(near + far, near[:, : centre - half] - far[:, : centre - half])
            scaled = score * shares[slot]
            if slot == 0:
                best, mean, squares = score, scaled, scaled * score
            else:
                best = jnp.maximum(best, score)
                mean, squares = mean + scaled, squares + scaled * score
        variance = squares - mean * mean
        rows = slice(part * strip, (part + 1) * strip)
        out_buf[0, rows] = (best - mean) * lax.rsqrt(jnp.maximum(variance, var_floor))
        out_buf[1, rows] = mean
        out_buf[2, rows] = variance
        for k, out in enumerate((snr_ref, mean_ref, var_ref)):
            copy = pltpu.make_async_copy(out_buf.at[k, rows], out.at[0, rows], out_sem.at[k, part])
            copy.start()
            out_copies.append(copy)

    def thin():
        for k in range(4):
            filt[k] = wide[k].astype(bf16)

    rows_first()
    thin()
    for tick in range(LMAX + 1):
        products = project(tick) if tick < LMAX else []
        if tick > 1:
            products = products + combine(tick - 2, 0)
        sums = [functools.partial(mix, tick - 1, start) for start in range(0, half, step)] if tick else []
        weave(products, sums)
    for step_ in combine(LMAX - 1, 0):
        step_()
    for first in range(half // lane):
        later = []
        if first + 1 < half // lane:
            later = [step_ for slot in range(LMAX) for step_ in combine(slot, first + 1)]
        ready = []
        for start in range(first * lane, centre, half):
            for part in range(start // strip, (start + lane) // strip):
                ready += [functools.partial(back, part), functools.partial(gather, part)]
        weave(later, ready)
    for copy in out_copies:
        copy.wait()


def beside(left, right):
    return jnp.concatenate([left, right], axis=1)


def vmem_call(kernel, inputs, outs, scratch, scalars, limit, out_spec=pltpu.VMEM, in_space=pltpu.VMEM):
    if in_space == pltpu.HBM:
        fixed = [pltpu.with_memory_space_constraint(array, pltpu.HBM) for array in inputs[scalars:]]
        inputs = (*inputs[:scalars], *fixed)
    smem = pl.BlockSpec(memory_space=pltpu.SMEM)
    vmem = pl.BlockSpec(memory_space=in_space)
    return pl.pallas_call(
        kernel,
        out_shape=tuple(jax.ShapeDtypeStruct(shape, dtype) for shape, dtype in outs),
        in_specs=[smem] * scalars + [vmem] * (len(inputs) - scalars),
        out_specs=tuple(pl.BlockSpec(memory_space=out_spec) for _ in outs),
        scratch_shapes=scratch,
        compiler_params=pltpu.CompilerParams(vmem_limit_bytes=limit << 20),
    )(*inputs)


def pack(orient_list, lengths, defocus, centre_block, templates):
    centre, box = centre_block.shape[0], templates.shape[1]
    lane = (centre + box) // 4
    held = (centre_block, orient_list.T, lengths[None], defocus[None], templates)
    strip = ((centre // 2, lane), jnp.bfloat16)
    outs = [(array.shape, array.dtype) for array in held] + [((box // 2, centre), jnp.bfloat16), strip, strip]
    return vmem_call(pack_kernel, held, outs, [pltpu.SemaphoreType.DMA((5,))], 0, 8, in_space=pltpu.HBM)


def early(defocus, extent):
    half = extent // 2
    return vmem_call(early_kernel, (defocus,), (((4, half, half), jnp.float32),), [], 1, 8)[0]


def tile_spectrum(paired, pieces, weights, tables, extent):
    half = extent // 2
    (filt,) = vmem_call(
        functools.partial(tile_kernel, paired), (*pieces, weights, *tables),
        (((4, half, half), jnp.float32),), [pltpu.VMEM((extent, extent), jnp.float32)], 0, 16,
    )
    return filt


def match(orient_list, lengths, filt, near, far, tables, centre):
    half = filt.shape[1]
    lane, extent = half // 2, 2 * half
    strip = lane // 2
    out = ((1, centre, centre), jnp.float32)
    return vmem_call(
        match_kernel, (orient_list, lengths, filt, near, far, *tables[:2], *tables[4:]), (out, out, out),
        [
            pltpu.VMEM((4, half, half), jnp.bfloat16),
            pltpu.VMEM((LMAX, 2, 2 * near.shape[1], half), jnp.bfloat16),
            pltpu.VMEM((2, 2 * extent, half), jnp.bfloat16),
            pltpu.VMEM((LMAX, 2, 2, half, half), jnp.bfloat16),
            pltpu.VMEM((2, 2, centre // strip, LMAX * strip, lane), jnp.bfloat16),
            pltpu.VMEM((3, centre, centre), jnp.float32),
            pltpu.SemaphoreType.DMA((3, centre // strip)),
        ],
        2, 24, pl.ANY,
    )


def shards(micrograph, templates, orient_list, lengths, defocus):
    position = lax.axis_index("tile")
    tile_count = lax.axis_size("tile")
    centre_block = micrograph[0]
    centre = centre_block.shape[0]
    box = templates.shape[1]
    margin = box // 2
    extent = centre + box
    tile_rows = tile_count // GRID
    grid_place = (position + GRID // 2) % tile_count
    column, tile_row = grid_place % GRID, grid_place // GRID
    tables = make_tables(extent, box)

    def send(block, target):
        return lax.ppermute(block, "tile", [(i, target(i)) for i in range(tile_count)])

    paired = tile_rows == 2
    if paired:
        odd = position % 2 == 1
        distances = flips(tile_count)
        pair = send(templates, lambda i: i ^ distances[0])
        block, orients, counts, focus, own, to_ends, to_mate, to_peer = pack(
            orient_list, lengths, defocus, centre_block, templates
        )
        ends = send(to_ends, lambda i: i ^ GRID)
        weights = early(focus, extent)

        def strip(own, use_first):
            edge = jnp.where(use_first, ends[:, :margin], ends[:, centre - margin :])
            edge = jnp.concatenate([edge[: margin // 2], edge[margin // 2 :]], axis=1)
            return jnp.concatenate([own, edge], axis=0)

        two = jnp.concatenate([own, pair], axis=0)
        group = [two]
        for apart in (distances[2] | distances[1], distances[1], distances[2]):
            group.append(send(two, lambda i, apart=apart: i ^ apart))
        from_peer = send(strip(to_peer, ~odd), lambda i: (i + 1 if i % 2 else i - 1) % tile_count)
        from_mate = send(strip(to_mate, odd), lambda i: i ^ 1)
        near = jnp.concatenate([group[0], group[2], group[3], group[1]], axis=0)
        far = send(near, lambda i: i ^ 1)
        filt = tile_spectrum(True, (block, from_mate, from_peer, ends), weights, tables, extent)
    else:

        def arrive(block, distance):
            return lax.ppermute(
                block, "tile", [((i + distance) % tile_count, i) for i in range(tile_count)]
            )

        _, orients, counts, focus, *_ = pack(orient_list, lengths, defocus, centre_block, templates)
        weights = early(focus, extent)
        right = arrive(centre_block[:, :margin], 1)
        left = arrive(centre_block[:, centre - margin :], -1)
        right = jnp.where(column == GRID - 1, jnp.zeros_like(right), right)
        left = jnp.where(column == 0, jnp.zeros_like(left), left)
        cols = jnp.concatenate([right, left], axis=1)
        wide = jnp.concatenate([centre_block, cols], axis=1)
        below = arrive(wide[:margin], GRID)
        above = arrive(wide[centre - margin :], -GRID)
        below = jnp.where(tile_row == tile_rows - 1, jnp.zeros_like(below), below)
        above = jnp.where(tile_row == 0, jnp.zeros_like(above), above)
        rows = jnp.concatenate([below, above], axis=0)
        near = templates
        for distance in flips(tile_count)[:-1]:
            near = jnp.concatenate([near, send(near, lambda i, d=distance: i ^ d)], axis=0)
        far = send(near, lambda i: i ^ 1)
        filt = tile_spectrum(False, (centre_block, cols, rows), weights, tables, extent)
    return match(orients, counts, filt, near, far, tables, centre)


def solution(mesh):
    return jax.shard_map(
        shards,
        mesh=mesh,
        in_specs=(
            P(("mic", "tile"), None, None),
            P("tile", None, None),
            P("mic", None),
            P("mic"),
            P("mic"),
        ),
        out_specs=(
            P(("mic", "tile"), None, None),
            P(("mic", "tile"), None, None),
            P(("mic", "tile"), None, None),
        ),
        check_vma=False,
    )
```

```python
import functools
import math

import jax
import jax.numpy as jnp
import numpy as np
from jax import lax
from jax.experimental import pallas as pl
from jax.experimental.pallas import tpu as pltpu
from jax.sharding import PartitionSpec as P


GRID = 8
LMAX = 4

wave_length = 0.0197
spherical = 27000000.0
contrast = 0.07
var_floor = 0.1


def wave_tables(index, position, extent):
    product = index[:, None] * position[None, :] % extent
    angle = product * (2.0 * math.pi / extent)
    nyquist = 1.0 - 2.0 * (position[None, :] % 2)
    return np.cos(angle), np.where(index[:, None] == 0, nyquist, np.sin(angle))


def make_tables(extent, box):
    half = extent // 2
    position = np.arange(half)
    even, odd = position[::2], position[1::2]
    tables = []
    for index in (even, odd):
        cosine, sine = wave_tables(index, position, extent)
        tables.append(np.concatenate([cosine, sine], axis=0).T)
    tables += [table.T for table in tables]
    for index in (even, odd):
        cosine, sine = wave_tables(index, position, extent)
        first = index[:, None] == 0
        cosine = np.where(first, 0.5 + 0.5 * sine, cosine)
        tables.append(np.concatenate([cosine, np.where(first, 0.5 - 0.5 * sine, -sine)], axis=0))
    order = np.concatenate([even, odd])
    centred = np.arange(box) - box // 2
    cosine, sine = wave_tables(order, centred, extent)
    tables.append(np.concatenate([cosine, sine], axis=0).T)
    first = order[:, None] == 0
    plain = np.where(first, 0.0, sine)
    nyquist, zero = sine[:1] + 0 * sine, 0 * sine
    tables.append(
        np.concatenate(
            [
                np.concatenate([cosine, -plain], axis=1),
                np.concatenate([-plain, -cosine], axis=1),
                np.where(first, np.concatenate([nyquist, zero], axis=1), np.concatenate([cosine, plain], axis=1)),
                np.where(first, np.concatenate([zero, -nyquist], axis=1), np.concatenate([plain, -cosine], axis=1)),
            ],
            axis=0,
        )
    )
    return [jnp.asarray(table, jnp.bfloat16) for table in tables]


def sine_of_turns(turns):
    part = turns - jnp.round(turns)
    folded = jnp.where(jnp.abs(part) > 0.25, jnp.where(part > 0, 0.5, -0.5) - part, part)
    angle = folded * (2.0 * math.pi)
    square = angle * angle
    series = -1.0 / 39916800.0
    for factor in (362880.0, -5040.0, 120.0, -6.0, 1.0):
        series = series * square + 1.0 / factor
    return angle * series


def transfer(row, column, focus_value, extent):
    radius = (row * row + column * column) * (1.0 / (extent * extent))
    turns = (0.5 * wave_length) * focus_value * radius - (
        0.25 * spherical * wave_length**3
    ) * radius * radius
    return -sine_of_turns(turns + math.asin(contrast) / (2.0 * math.pi))


def flips(tile_count):
    if tile_count == 2 * GRID:
        return [GRID, 2, 4, 1]
    return [1 << k for k in reversed(range(tile_count.bit_length() - 1))]


def dot(left, right):
    return jnp.dot(left, right, preferred_element_type=jnp.float32)


def swap_halves(block, lanes):
    return pltpu.roll(block, lanes, 1)


def pack_kernel(*refs):
    sources, held, (ends_ref, mate_ref, peer_ref, sem) = refs[:5], refs[5:10], refs[10:]
    copies = [pltpu.make_async_copy(sources[k], held[k], sem.at[k]) for k in range(5)]
    for copy in copies:
        copy.start()
    me = lax.axis_index("tile")
    tile_count = lax.axis_size("tile")
    place = lax.rem(me + GRID // 2, tile_count)
    centre_ref = held[0]
    centre, lane, margin = centre_ref.shape[0], mate_ref.shape[1], ends_ref.shape[0]
    copies[0].wait()
    top = centre_ref[:margin].astype(jnp.float32)
    bottom = centre_ref[centre - margin :].astype(jnp.float32)
    ends_ref[...] = jnp.where(place < GRID, bottom, top).astype(jnp.bfloat16)
    half = centre // 2
    first = centre_ref[:, :lane].astype(jnp.float32)
    last = centre_ref[:, centre - lane :].astype(jnp.float32)
    low = lax.broadcasted_iota(jnp.int32, (half, lane), 1) < lane // 2
    first = jnp.where(low, first[:half], swap_halves(first[half:], lane // 2))
    last = jnp.where(low, swap_halves(last[:half], lane // 2), last[half:])
    odd = lax.rem(me, 2) == 1
    mate_ref[...] = jnp.where(odd, first, last).astype(jnp.bfloat16)
    peer_ref[...] = jnp.where(odd, last, first).astype(jnp.bfloat16)
    for copy in copies[1:]:
        copy.wait()


def early_kernel(defocus, weight_ref):
    me = lax.axis_index("tile")
    focus_value = defocus[0, me]
    lane = weight_ref.shape[1] // 2
    extent = 4 * lane
    edge = float(2 * lane)
    scale = 2.0 / (extent * extent)
    i = lax.broadcasted_iota(jnp.int32, (lane, lane), 0)
    j = lax.broadcasted_iota(jnp.int32, (lane, lane), 1)
    for row_odd in range(2):
        for col_odd in range(2):
            row = (2 * i + row_odd).astype(jnp.float32)
            col = (2 * j + col_odd).astype(jnp.float32)
            rows = slice(row_odd * lane, (row_odd + 1) * lane)
            cols = slice(col_odd * lane, (col_odd + 1) * lane)
            if row_odd and col_odd:
                value = scale * transfer(row, col, focus_value, extent)
                parts = (value,) * 4
            elif row_odd or col_odd:
                value = scale * transfer(row, col, focus_value, extent)
                if row_odd:
                    other = transfer(row, jnp.where(j == 0, edge, col), focus_value, extent)
                else:
                    other = transfer(jnp.where(i == 0, edge, row), col, focus_value, extent)
                other = scale * other
                parts = (value, value, other, other)
            else:
                col_first = j == 0
                corner = col_first & (i == 0)
                row_first = (i == 0) & (j != 0)
                row_minus = jnp.where(row_first, edge, row)
                col_minus = jnp.where(col_first, edge, col)
                at_corner = jnp.where(corner, 0.5 * scale, scale)
                parts = (
                    at_corner * transfer(row, col, focus_value, extent),
                    at_corner * transfer(jnp.where(corner, edge, row), col, focus_value, extent),
                    at_corner * transfer(row_minus, col_minus, focus_value, extent),
                    at_corner * transfer(jnp.where(corner, edge, row_minus), col_minus, focus_value, extent),
                )
            for k in range(4):
                weight_ref[k, rows, cols] = parts[k]


def packed_sides(mate, peer, lane, start, stop, left_open, right_open):
    odd = lax.rem(lax.axis_index("tile"), 2) == 1
    mate = mate[start:stop].astype(jnp.float32)
    peer = peer[start:stop].astype(jnp.float32)
    right = jnp.where(right_open, jnp.where(odd, peer, mate), 0.0)
    left = jnp.where(left_open, jnp.where(odd, mate, peer), 0.0)
    low = lax.broadcasted_iota(jnp.int32, right.shape, 1) < lane // 2
    upper = jnp.where(low, right, swap_halves(left, lane // 2))
    lower = jnp.where(low, swap_halves(right, lane // 2), left)
    return jnp.concatenate([upper, lower], axis=0)


def tile_steps(paired, pieces, weight_ref, tables, filt, uv):
    fwd_e, fwd_o, fwd_et, fwd_ot = tables
    centre_ref = pieces[0]
    centre, extent = centre_ref.shape[0], uv.shape[0]
    half, lane = extent // 2, extent // 4
    held = {}

    def assemble():
        if paired:
            _, mate_ref, peer_ref, ends_ref = pieces
            place = lax.rem(lax.axis_index("tile") + GRID // 2, 2 * GRID)
            column, upper_row = lax.rem(place, GRID), place < GRID
            opens = (column != 0, column != GRID - 1)
            held["side"] = packed_sides(mate_ref, peer_ref, lane, 0, centre // 2, *opens)
            corners = packed_sides(mate_ref, peer_ref, lane, centre // 2, mate_ref.shape[0], *opens)
            ends = jnp.concatenate([ends_ref[...].astype(jnp.float32), corners], axis=1)
            held["rim"] = jnp.concatenate([jnp.where(upper_row, ends, 0.0), jnp.where(upper_row, 0.0, ends)], axis=0)
        else:
            held["side"] = pieces[1][...].astype(jnp.float32)
            held["rim"] = pieces[2][...].astype(jnp.float32)

    def own_rows(first):
        rows = slice(first * lane, (first + 1) * lane)
        own = centre_ref[rows].astype(jnp.float32)
        far = jnp.concatenate([own[:, half:], held["side"][rows]], axis=1)
        near = own[:, :half]
        uv[rows, :half] = dot((near + far).astype(jnp.bfloat16), fwd_e[...])
        uv[rows, half:] = dot((near - far).astype(jnp.bfloat16), fwd_o[...])

    def rim_rows():
        near, far = held["rim"][:, :half], held["rim"][:, half:]
        uv[centre:, :half] = dot((near + far).astype(jnp.bfloat16), fwd_e[...])
        uv[centre:, half:] = dot((near - far).astype(jnp.bfloat16), fwd_o[...])

    def columns(row_odd, col_odd):
        cols = slice(col_odd * half, (col_odd + 1) * half)
        near, far = uv[:half, cols], uv[half:, cols]
        total = near - far if row_odd else near + far
        block = dot((fwd_ot if row_odd else fwd_et)[...], total.astype(jnp.bfloat16))
        i = lax.broadcasted_iota(jnp.int32, (lane, lane), 0)
        j = lax.broadcasted_iota(jnp.int32, (lane, lane), 1)
        uc, vc, us, vs = block[:lane, :lane], block[:lane, lane:], block[lane:, :lane], block[lane:, lane:]
        parts = [uc - vs, -(us + vc), uc + vs, us - vc]
        if not row_odd:
            row_first = i == 0
            parts = [jnp.where(row_first, a, b) for a, b in zip((uc, -vc, us, -vs), parts)]
        if not col_odd:
            col_first = j == 0
            parts = [jnp.where(col_first, a, b) for a, b in zip((uc, -us, vc, vs), parts)]
        rows = slice(row_odd * lane, (row_odd + 1) * lane)
        cols = slice(col_odd * lane, (col_odd + 1) * lane)
        for k in range(4):
            filt[k, rows, cols] = (weight_ref[k, rows, cols] * parts[k]).astype(jnp.bfloat16)

    steps = [assemble] + [functools.partial(own_rows, first) for first in range(centre // lane)] + [rim_rows]
    return steps + [functools.partial(columns, r, c) for r in range(2) for c in range(2)]


def weave(*tracks):
    steps = []
    for order, track in enumerate(tracks):
        steps += [((k + 0.5) / len(track), order, k, step) for k, step in enumerate(track)]
    for *_, step in sorted(steps, key=lambda entry: entry[:3]):
        step()


def match_kernel(paired, orients, lengths, *refs):
    count_in = 4 if paired else 3
    pieces, (weight_ref, near_ref, far_ref) = refs[:count_in], refs[count_in : count_in + 3]
    fwd_e, fwd_o, fwd_et, fwd_ot, inv_e, inv_o, temp_rows, temp_cols = refs[count_in + 3 : count_in + 11]
    snr_ref, mean_ref, var_ref = refs[count_in + 11 : count_in + 14]
    filt, uv, waves, proj, mixed, combos, out_buf, out_sem = refs[count_in + 14 :]
    me = lax.axis_index("tile")
    half = filt.shape[1]
    lane = half // 2
    centre = out_buf.shape[1]
    box = near_ref.shape[1]
    strip = combos.shape[3] // LMAX
    tile_count = lax.axis_size("tile")
    distances = flips(tile_count)
    held = near_ref.shape[0] // (tile_count // 2)
    count = lengths[0, me]
    bf16, f32 = jnp.bfloat16, jnp.float32
    step = 16
    col_first = lax.broadcasted_iota(jnp.int32, (step, half), 1) == 0
    row_first = lax.broadcasted_iota(jnp.int32, (step, half), 0) == 0
    corner = col_first & row_first
    thin_first = col_first.astype(f32).astype(bf16) > 0
    sign = 1.0 - 2.0 * (lax.broadcasted_iota(jnp.int32, (box, lane), 0) % 2).astype(f32)
    box_col = lax.broadcasted_iota(jnp.int32, (box, lane), 1) == 0
    edges = {}

    def chosen(slot):
        orient = orients[slot, me]
        if slot:
            orient = jnp.where(slot < count, orient, orients[0, me])
        orient = jnp.clip(orient, 0, 2 * near_ref.shape[0] - 1)
        apart = lax.div(orient, held) ^ me
        at = lax.rem(orient, held)
        for k, distance in enumerate(distances[:-1]):
            at = at + (lax.div(apart, distance) & 1) * (held << k)
        return jnp.where(apart & 1 == 1, far_ref[at], near_ref[at])

    def rows_first():
        stacked = jnp.concatenate([chosen(slot) for slot in range(LMAX)], axis=0)
        first_u, rest_u = dot(stacked, temp_rows[:, :lane]), dot(stacked, temp_rows[:, lane:half])
        first_v, rest_v = dot(stacked, temp_rows[:, half : half + lane]), dot(stacked, temp_rows[:, half + lane :])
        for slot in range(LMAX):
            rows = slice(slot * box, (slot + 1) * box)
            u, v = first_u[rows], first_v[rows]
            row_edge = -jnp.sum(u * sign, axis=0, keepdims=True)
            col_edge = jnp.sum(v, axis=0, keepdims=True)
            edges[slot] = (beside(row_edge, row_edge), beside(col_edge, col_edge))
            v_part = beside(jnp.where(box_col, 0.0, v), rest_v[rows]).astype(bf16)
            waves[slot, 0, :box] = beside(u, rest_u[rows]).astype(bf16)
            waves[slot, 1, :box] = beside(jnp.where(box_col, v, u), rest_u[rows]).astype(bf16)
            waves[slot, 0, box:] = v_part
            waves[slot, 1, box:] = v_part

    def project(slot):
        def cols(k):
            here = slice(k * half, (k + 1) * half)
            proj[slot % 2, here] = dot(temp_cols[here], waves[slot, k // 2]).astype(bf16)

        return [functools.partial(cols, k) for k in range(4)]

    def mix_first(slot, fs, ps):
        fpr, fpi, fmr, fmi = (f.astype(f32) for f in fs)
        ppr, ppi, pmr, pmi = (p.astype(f32) for p in ps)
        row_edge, col_edge = edges[slot]
        ppi = jnp.where(corner, row_edge, ppi)
        pmi = jnp.where(corner, pmr, pmi)
        pmr = jnp.where(corner, col_edge, pmr)
        plus_r, plus_i = fpr * ppr + fpi * ppi, fpi * ppr - fpr * ppi
        minus_r, minus_i = fmr * pmr + fmi * pmi, fmi * pmr - fmr * pmi
        cos_r, sin_r = plus_r + minus_r, minus_i - plus_i
        cos_i, sin_i = plus_i + minus_i, plus_r - minus_r
        cos_i, sin_i = jnp.where(col_first, sin_i, cos_i), jnp.where(col_first, -cos_i, sin_i)
        cos_r = jnp.where(row_first, plus_r, cos_r)
        sin_r = jnp.where(row_first, minus_r, sin_r)
        cos_i = jnp.where(row_first, plus_i, cos_i)
        sin_i = jnp.where(row_first, minus_i, sin_i)
        cos_r = jnp.where(corner, fpr * ppr + fmr * pmr, cos_r)
        sin_r = jnp.where(corner, fpi * ppi + fmi * pmi, sin_r)
        cos_i = jnp.where(corner, fpr * ppr - fmr * pmr, cos_i)
        sin_i = jnp.where(corner, fpi * ppi - fmi * pmi, sin_i)
        return cos_r.astype(bf16), sin_r.astype(bf16), cos_i.astype(bf16), sin_i.astype(bf16)

    def mix(slot, start):
        row_odd, at = start // lane, start % lane
        buffer = slot % 2
        fs = [filt[k, start : start + step] for k in range(4)]
        ps = [proj[buffer, k * half + start : k * half + start + step] for k in range(4)]
        if start == 0:
            cos_r, sin_r, cos_i, sin_i = mix_first(slot, fs, ps)
        else:
            fpr, fpi, fmr, fmi = fs
            ppr, ppi, pmr, pmi = ps
            plus_r, plus_i = fpr * ppr + fpi * ppi, fpi * ppr - fpr * ppi
            minus_r, minus_i = fmr * pmr + fmi * pmi, fmi * pmr - fmr * pmi
            cos_r, sin_r = plus_r + minus_r, minus_i - plus_i
            cos_i, sin_i = plus_i + minus_i, plus_r - minus_r
            cos_i, sin_i = jnp.where(thin_first, sin_i, cos_i), jnp.where(thin_first, -cos_i, sin_i)
        mixed[slot, row_odd, 0, at : at + step] = cos_r
        mixed[slot, row_odd, 0, lane + at : lane + at + step] = sin_r
        mixed[slot, row_odd, 1, at : at + step] = cos_i
        mixed[slot, row_odd, 1, lane + at : lane + at + step] = sin_i

    def combine(slot, first):
        def rows(imag):
            here = slice(first * lane, (first + 1) * lane)
            even = dot(fwd_e[here], mixed[slot, 0, imag])
            odd = dot(fwd_o[here], mixed[slot, 1, imag])
            starts = [(first * lane, even + odd)]
            if half + first * lane < centre:
                starts.append((half + first * lane, even - odd))
            for start, value in starts:
                value = value.astype(bf16)
                for k in range(lane // strip):
                    place = slice(slot * strip, (slot + 1) * strip)
                    piece = value[k * strip : (k + 1) * strip]
                    combos[0, imag, start // strip + k, place] = piece[:, :lane]
                    combos[1, imag, start // strip + k, place] = piece[:, lane:]

        return [functools.partial(rows, imag) for imag in range(2)]

    share = 1.0 / jnp.full((1, 1), count, jnp.int32).astype(f32)
    shares = [jnp.where(slot < count, share, 0.0) for slot in range(LMAX)]
    fields, out_copies = {}, []

    def back(part):
        fields[part] = (
            dot(beside(combos[0, 0, part], combos[0, 1, part]), inv_e[...]),
            dot(beside(combos[1, 0, part], combos[1, 1, part]), inv_o[...]),
        )

    def gather(part):
        even, odd = fields.pop(part)
        for slot in range(LMAX):
            here = slice(slot * strip, (slot + 1) * strip)
            near, far = even[here], odd[here]
            score = beside(near + far, near[:, : centre - half] - far[:, : centre - half])
            scaled = score * shares[slot]
            if slot == 0:
                best, mean, squares = score, scaled, scaled * score
            else:
                best = jnp.maximum(best, score)
                mean, squares = mean + scaled, squares + scaled * score
        variance = squares - mean * mean
        rows = slice(part * strip, (part + 1) * strip)
        out_buf[0, rows] = (best - mean) * lax.rsqrt(jnp.maximum(variance, var_floor))
        out_buf[1, rows] = mean
        out_buf[2, rows] = variance
        for k, out in enumerate((snr_ref, mean_ref, var_ref)):
            copy = pltpu.make_async_copy(out_buf.at[k, rows], out.at[0, rows], out_sem.at[k, part])
            copy.start()
            out_copies.append(copy)

    tile = tile_steps(paired, pieces, weight_ref, (fwd_e, fwd_o, fwd_et, fwd_ot), filt, uv)
    weave(tile, [rows_first] + project(0) + project(1))
    for tick in range(1, LMAX + 1):
        products = project(tick) if 1 < tick < LMAX else []
        if tick > 1:
            products = products + combine(tick - 2, 0)
        sums = [functools.partial(mix, tick - 1, start) for start in range(0, half, step)]
        weave(products, sums)
    for step_ in combine(LMAX - 1, 0):
        step_()
    for first in range(half // lane):
        later = []
        if first + 1 < half // lane:
            later = [step_ for slot in range(LMAX) for step_ in combine(slot, first + 1)]
        ready = []
        for start in range(first * lane, centre, half):
            for part in range(start // strip, (start + lane) // strip):
                ready += [functools.partial(back, part), functools.partial(gather, part)]
        weave(later, ready)
    for copy in out_copies:
        copy.wait()


def beside(left, right):
    return jnp.concatenate([left, right], axis=1)


def vmem_call(kernel, inputs, outs, scratch, scalars, limit, out_spec=pltpu.VMEM, in_space=pltpu.VMEM):
    if in_space == pltpu.HBM:
        fixed = [pltpu.with_memory_space_constraint(array, pltpu.HBM) for array in inputs[scalars:]]
        inputs = (*inputs[:scalars], *fixed)
    smem = pl.BlockSpec(memory_space=pltpu.SMEM)
    vmem = pl.BlockSpec(memory_space=in_space)
    return pl.pallas_call(
        kernel,
        out_shape=tuple(jax.ShapeDtypeStruct(shape, dtype) for shape, dtype in outs),
        in_specs=[smem] * scalars + [vmem] * (len(inputs) - scalars),
        out_specs=tuple(pl.BlockSpec(memory_space=out_spec) for _ in outs),
        scratch_shapes=scratch,
        compiler_params=pltpu.CompilerParams(vmem_limit_bytes=limit << 20),
    )(*inputs)


def pack(orient_list, lengths, defocus, centre_block, templates):
    centre, box = centre_block.shape[0], templates.shape[1]
    lane = (centre + box) // 4
    held = (centre_block, orient_list.T, lengths[None], defocus[None], templates)
    strip = ((centre // 2, lane), jnp.bfloat16)
    outs = [(array.shape, array.dtype) for array in held] + [((box // 2, centre), jnp.bfloat16), strip, strip]
    return vmem_call(pack_kernel, held, outs, [pltpu.SemaphoreType.DMA((5,))], 0, 8, in_space=pltpu.HBM)


def early(defocus, extent):
    half = extent // 2
    return vmem_call(early_kernel, (defocus,), (((4, half, half), jnp.float32),), [], 1, 8)[0]


def match(orient_list, lengths, pieces, weights, near, far, tables):
    centre, half = pieces[0].shape[0], weights.shape[1]
    lane, extent = half // 2, 2 * half
    strip = lane // 2
    out = ((1, centre, centre), jnp.float32)
    kernel = functools.partial(match_kernel, len(pieces) == 4)
    return vmem_call(
        kernel, (orient_list, lengths, *pieces, weights, near, far, *tables), (out, out, out),
        [
            pltpu.VMEM((4, half, half), jnp.bfloat16),
            pltpu.VMEM((extent, extent), jnp.float32),
            pltpu.VMEM((LMAX, 2, 2 * near.shape[1], half), jnp.bfloat16),
            pltpu.VMEM((2, 2 * extent, half), jnp.bfloat16),
            pltpu.VMEM((LMAX, 2, 2, half, half), jnp.bfloat16),
            pltpu.VMEM((2, 2, centre // strip, LMAX * strip, lane), jnp.bfloat16),
            pltpu.VMEM((3, centre, centre), jnp.float32),
            pltpu.SemaphoreType.DMA((3, centre // strip)),
        ],
        2, 24, pl.ANY,
    )


def shards(micrograph, templates, orient_list, lengths, defocus):
    position = lax.axis_index("tile")
    tile_count = lax.axis_size("tile")
    centre_block = micrograph[0]
    centre = centre_block.shape[0]
    box = templates.shape[1]
    margin = box // 2
    extent = centre + box
    tile_rows = tile_count // GRID
    grid_place = (position + GRID // 2) % tile_count
    column, tile_row = grid_place % GRID, grid_place // GRID
    tables = make_tables(extent, box)

    def send(block, target):
        return lax.ppermute(block, "tile", [(i, target(i)) for i in range(tile_count)])

    paired = tile_rows == 2
    if paired:
        odd = position % 2 == 1
        distances = flips(tile_count)
        pair = send(templates, lambda i: i ^ distances[0])
        block, orients, counts, focus, own, to_ends, to_mate, to_peer = pack(
            orient_list, lengths, defocus, centre_block, templates
        )
        ends = send(to_ends, lambda i: i ^ GRID)
        weights = early(focus, extent)

        def strip(own, use_first):
            edge = jnp.where(use_first, ends[:, :margin], ends[:, centre - margin :])
            edge = jnp.concatenate([edge[: margin // 2], edge[margin // 2 :]], axis=1)
            return jnp.concatenate([own, edge], axis=0)

        two = jnp.concatenate([own, pair], axis=0)
        group = [two]
        for apart in (distances[2] | distances[1], distances[1], distances[2]):
            group.append(send(two, lambda i, apart=apart: i ^ apart))
        from_peer = send(strip(to_peer, ~odd), lambda i: (i + 1 if i % 2 else i - 1) % tile_count)
        from_mate = send(strip(to_mate, odd), lambda i: i ^ 1)
        near = jnp.concatenate([group[0], group[2], group[3], group[1]], axis=0)
        far = send(near, lambda i: i ^ 1)
        pieces = (block, from_mate, from_peer, ends)
    else:

        def arrive(block, distance):
            return lax.ppermute(
                block, "tile", [((i + distance) % tile_count, i) for i in range(tile_count)]
            )

        _, orients, counts, focus, *_ = pack(orient_list, lengths, defocus, centre_block, templates)
        weights = early(focus, extent)
        right = arrive(centre_block[:, :margin], 1)
        left = arrive(centre_block[:, centre - margin :], -1)
        right = jnp.where(column == GRID - 1, jnp.zeros_like(right), right)
        left = jnp.where(column == 0, jnp.zeros_like(left), left)
        cols = jnp.concatenate([right, left], axis=1)
        wide = jnp.concatenate([centre_block, cols], axis=1)
        below = arrive(wide[:margin], GRID)
        above = arrive(wide[centre - margin :], -GRID)
        below = jnp.where(tile_row == tile_rows - 1, jnp.zeros_like(below), below)
        above = jnp.where(tile_row == 0, jnp.zeros_like(above), above)
        rows = jnp.concatenate([below, above], axis=0)
        near = templates
        for distance in flips(tile_count)[:-1]:
            near = jnp.concatenate([near, send(near, lambda i, d=distance: i ^ d)], axis=0)
        far = send(near, lambda i: i ^ 1)
        pieces = (centre_block, cols, rows)
    return match(orients, counts, pieces, weights, near, far, tables)


def solution(mesh):
    return jax.shard_map(
        shards,
        mesh=mesh,
        in_specs=(
            P(("mic", "tile"), None, None),
            P("tile", None, None),
            P("mic", None),
            P("mic"),
            P("mic"),
        ),
        out_specs=(
            P(("mic", "tile"), None, None),
            P(("mic", "tile"), None, None),
            P(("mic", "tile"), None, None),
        ),
        check_vma=False,
    )
```

```python
import functools
import math

import jax
import jax.numpy as jnp
import numpy as np
from jax import lax
from jax.experimental import pallas as pl
from jax.experimental.pallas import tpu as pltpu
from jax.sharding import PartitionSpec as P


GRID = 8
LMAX = 4

wave_length = 0.0197
spherical = 27000000.0
contrast = 0.07
var_floor = 0.1


def wave_tables(index, position, extent):
    product = index[:, None] * position[None, :] % extent
    angle = product * (2.0 * math.pi / extent)
    nyquist = 1.0 - 2.0 * (position[None, :] % 2)
    return np.cos(angle), np.where(index[:, None] == 0, nyquist, np.sin(angle))


def make_tables(extent, box):
    half = extent // 2
    position = np.arange(half)
    even, odd = position[::2], position[1::2]
    tables = []
    for index in (even, odd):
        cosine, sine = wave_tables(index, position, extent)
        tables.append(np.concatenate([cosine, sine], axis=0).T)
    tables += [table.T for table in tables]
    for index in (even, odd):
        cosine, sine = wave_tables(index, position, extent)
        first = index[:, None] == 0
        cosine = np.where(first, 0.5 + 0.5 * sine, cosine)
        tables.append(np.concatenate([cosine, np.where(first, 0.5 - 0.5 * sine, -sine)], axis=0))
    order = np.concatenate([even, odd])
    centred = np.arange(box) - box // 2
    cosine, sine = wave_tables(order, centred, extent)
    tables.append(np.concatenate([cosine, sine], axis=0).T)
    first = order[:, None] == 0
    plain = np.where(first, 0.0, sine)
    nyquist, zero = sine[:1] + 0 * sine, 0 * sine
    tables.append(
        np.concatenate(
            [
                np.concatenate([cosine, -plain], axis=1),
                np.concatenate([-plain, -cosine], axis=1),
                np.where(first, np.concatenate([nyquist, zero], axis=1), np.concatenate([cosine, plain], axis=1)),
                np.where(first, np.concatenate([zero, -nyquist], axis=1), np.concatenate([plain, -cosine], axis=1)),
            ],
            axis=0,
        )
    )
    return [jnp.asarray(table, jnp.bfloat16) for table in tables]


def sine_of_turns(turns):
    part = turns - jnp.round(turns)
    folded = jnp.where(jnp.abs(part) > 0.25, jnp.where(part > 0, 0.5, -0.5) - part, part)
    angle = folded * (2.0 * math.pi)
    square = angle * angle
    series = -1.0 / 39916800.0
    for factor in (362880.0, -5040.0, 120.0, -6.0, 1.0):
        series = series * square + 1.0 / factor
    return angle * series


def transfer(row, column, focus_value, extent):
    radius = (row * row + column * column) * (1.0 / (extent * extent))
    turns = (0.5 * wave_length) * focus_value * radius - (
        0.25 * spherical * wave_length**3
    ) * radius * radius
    return -sine_of_turns(turns + math.asin(contrast) / (2.0 * math.pi))


def flips(tile_count):
    if tile_count == 2 * GRID:
        return [GRID, 2, 4, 1]
    return [1 << k for k in reversed(range(tile_count.bit_length() - 1))]


def dot(left, right):
    return jnp.dot(left, right, preferred_element_type=jnp.float32)


def swap_halves(block, lanes):
    return pltpu.roll(block, lanes, 1)


def pack_kernel(*refs):
    sources, held, (ends_ref, mate_ref, peer_ref, sem) = refs[:5], refs[5:10], refs[10:]
    copies = [pltpu.make_async_copy(sources[k], held[k], sem.at[k]) for k in range(5)]
    for copy in copies:
        copy.start()
    me = lax.axis_index("tile")
    tile_count = lax.axis_size("tile")
    place = lax.rem(me + GRID // 2, tile_count)
    centre_ref = held[0]
    centre, lane, margin = centre_ref.shape[0], mate_ref.shape[1], ends_ref.shape[0]
    copies[0].wait()
    top = centre_ref[:margin].astype(jnp.float32)
    bottom = centre_ref[centre - margin :].astype(jnp.float32)
    ends_ref[...] = jnp.where(place < GRID, bottom, top).astype(jnp.bfloat16)
    half = centre // 2
    first = centre_ref[:, :lane].astype(jnp.float32)
    last = centre_ref[:, centre - lane :].astype(jnp.float32)
    low = lax.broadcasted_iota(jnp.int32, (half, lane), 1) < lane // 2
    first = jnp.where(low, first[:half], swap_halves(first[half:], lane // 2))
    last = jnp.where(low, swap_halves(last[:half], lane // 2), last[half:])
    odd = lax.rem(me, 2) == 1
    mate_ref[...] = jnp.where(odd, first, last).astype(jnp.bfloat16)
    peer_ref[...] = jnp.where(odd, last, first).astype(jnp.bfloat16)
    for copy in copies[1:]:
        copy.wait()


def early_kernel(defocus, weight_ref):
    me = lax.axis_index("tile")
    focus_value = defocus[0, me]
    lane = weight_ref.shape[1] // 2
    extent = 4 * lane
    edge = float(2 * lane)
    scale = 2.0 / (extent * extent)
    i = lax.broadcasted_iota(jnp.int32, (lane, lane), 0)
    j = lax.broadcasted_iota(jnp.int32, (lane, lane), 1)
    for row_odd in range(2):
        for col_odd in range(2):
            row = (2 * i + row_odd).astype(jnp.float32)
            col = (2 * j + col_odd).astype(jnp.float32)
            rows = slice(row_odd * lane, (row_odd + 1) * lane)
            cols = slice(col_odd * lane, (col_odd + 1) * lane)
            if row_odd and col_odd:
                value = scale * transfer(row, col, focus_value, extent)
                parts = (value,) * 4
            elif row_odd or col_odd:
                value = scale * transfer(row, col, focus_value, extent)
                if row_odd:
                    other = transfer(row, jnp.where(j == 0, edge, col), focus_value, extent)
                else:
                    other = transfer(jnp.where(i == 0, edge, row), col, focus_value, extent)
                other = scale * other
                parts = (value, value, other, other)
            else:
                col_first = j == 0
                corner = col_first & (i == 0)
                row_first = (i == 0) & (j != 0)
                row_minus = jnp.where(row_first, edge, row)
                col_minus = jnp.where(col_first, edge, col)
                at_corner = jnp.where(corner, 0.5 * scale, scale)
                parts = (
                    at_corner * transfer(row, col, focus_value, extent),
                    at_corner * transfer(jnp.where(corner, edge, row), col, focus_value, extent),
                    at_corner * transfer(row_minus, col_minus, focus_value, extent),
                    at_corner * transfer(jnp.where(corner, edge, row_minus), col_minus, focus_value, extent),
                )
            for k in range(4):
                weight_ref[k, rows, cols] = parts[k]


def packed_sides(mate, peer, lane, start, stop, left_open, right_open):
    odd = lax.rem(lax.axis_index("tile"), 2) == 1
    mate = mate[start:stop].astype(jnp.float32)
    peer = peer[start:stop].astype(jnp.float32)
    right = jnp.where(right_open, jnp.where(odd, peer, mate), 0.0)
    left = jnp.where(left_open, jnp.where(odd, mate, peer), 0.0)
    low = lax.broadcasted_iota(jnp.int32, right.shape, 1) < lane // 2
    upper = jnp.where(low, right, swap_halves(left, lane // 2))
    lower = jnp.where(low, swap_halves(right, lane // 2), left)
    return jnp.concatenate([upper, lower], axis=0)


def tile_steps(paired, pieces, weight_ref, tables, filt, uv):
    fwd_e, fwd_o, fwd_et, fwd_ot = tables
    centre_ref = pieces[0]
    centre, extent = centre_ref.shape[0], uv.shape[0]
    half, lane = extent // 2, extent // 4
    held = {}

    def assemble():
        if paired:
            _, mate_ref, peer_ref, ends_ref = pieces
            place = lax.rem(lax.axis_index("tile") + GRID // 2, 2 * GRID)
            column, upper_row = lax.rem(place, GRID), place < GRID
            opens = (column != 0, column != GRID - 1)
            held["side"] = packed_sides(mate_ref, peer_ref, lane, 0, centre // 2, *opens)
            corners = packed_sides(mate_ref, peer_ref, lane, centre // 2, mate_ref.shape[0], *opens)
            ends = jnp.concatenate([ends_ref[...].astype(jnp.float32), corners], axis=1)
            held["rim"] = jnp.concatenate([jnp.where(upper_row, ends, 0.0), jnp.where(upper_row, 0.0, ends)], axis=0)
        else:
            held["side"] = pieces[1][...].astype(jnp.float32)
            held["rim"] = pieces[2][...].astype(jnp.float32)

    def own_rows(first):
        rows = slice(first * lane, (first + 1) * lane)
        own = centre_ref[rows].astype(jnp.float32)
        far = jnp.concatenate([own[:, half:], held["side"][rows]], axis=1)
        near = own[:, :half]
        uv[rows, :half] = dot((near + far).astype(jnp.bfloat16), fwd_e[...])
        uv[rows, half:] = dot((near - far).astype(jnp.bfloat16), fwd_o[...])

    def rim_rows():
        near, far = held["rim"][:, :half], held["rim"][:, half:]
        uv[centre:, :half] = dot((near + far).astype(jnp.bfloat16), fwd_e[...])
        uv[centre:, half:] = dot((near - far).astype(jnp.bfloat16), fwd_o[...])

    def columns(row_odd, col_odd):
        cols = slice(col_odd * half, (col_odd + 1) * half)
        near, far = uv[:half, cols], uv[half:, cols]
        total = near - far if row_odd else near + far
        block = dot((fwd_ot if row_odd else fwd_et)[...], total.astype(jnp.bfloat16))
        i = lax.broadcasted_iota(jnp.int32, (lane, lane), 0)
        j = lax.broadcasted_iota(jnp.int32, (lane, lane), 1)
        uc, vc, us, vs = block[:lane, :lane], block[:lane, lane:], block[lane:, :lane], block[lane:, lane:]
        parts = [uc - vs, -(us + vc), uc + vs, us - vc]
        if not row_odd:
            row_first = i == 0
            parts = [jnp.where(row_first, a, b) for a, b in zip((uc, -vc, us, -vs), parts)]
        if not col_odd:
            col_first = j == 0
            parts = [jnp.where(col_first, a, b) for a, b in zip((uc, -us, vc, vs), parts)]
        rows = slice(row_odd * lane, (row_odd + 1) * lane)
        cols = slice(col_odd * lane, (col_odd + 1) * lane)
        for k in range(4):
            filt[k, rows, cols] = (weight_ref[k, rows, cols] * parts[k]).astype(jnp.bfloat16)

    steps = [assemble] + [functools.partial(own_rows, first) for first in range(centre // lane)] + [rim_rows]
    return steps + [functools.partial(columns, r, c) for r in range(2) for c in range(2)]


def weave(*tracks):
    steps = []
    for order, track in enumerate(tracks):
        steps += [((k + 0.5) / len(track), order, k, step) for k, step in enumerate(track)]
    for *_, step in sorted(steps, key=lambda entry: entry[:3]):
        step()


def match_kernel(paired, orients, lengths, *refs):
    count_in = 4 if paired else 3
    pieces, (weight_ref, near_ref, far_ref) = refs[:count_in], refs[count_in : count_in + 3]
    fwd_e, fwd_o, fwd_et, fwd_ot, inv_e, inv_o, temp_rows, temp_cols = refs[count_in + 3 : count_in + 11]
    snr_ref, mean_ref, var_ref = refs[count_in + 11 : count_in + 14]
    filt, uv, waves, proj, mixed, combos, out_buf, out_sem = refs[count_in + 14 :]
    me = lax.axis_index("tile")
    half = filt.shape[1]
    lane = half // 2
    centre = out_buf.shape[1]
    box = near_ref.shape[1]
    strip = combos.shape[3] // LMAX
    tile_count = lax.axis_size("tile")
    distances = flips(tile_count)
    held = near_ref.shape[0] // (tile_count // 2)
    count = lengths[0, me]
    bf16, f32 = jnp.bfloat16, jnp.float32
    step = 16
    col_first = lax.broadcasted_iota(jnp.int32, (step, half), 1) == 0
    row_first = lax.broadcasted_iota(jnp.int32, (step, half), 0) == 0
    corner = col_first & row_first
    thin_first = col_first.astype(f32).astype(bf16) > 0
    sign = 1.0 - 2.0 * (lax.broadcasted_iota(jnp.int32, (box, lane), 0) % 2).astype(f32)
    box_col = lax.broadcasted_iota(jnp.int32, (box, lane), 1) == 0
    edges = {}

    def chosen(slot):
        orient = orients[slot, me]
        if slot:
            orient = jnp.where(slot < count, orient, orients[0, me])
        orient = jnp.clip(orient, 0, 2 * near_ref.shape[0] - 1)
        apart = lax.div(orient, held) ^ me
        at = lax.rem(orient, held)
        for k, distance in enumerate(distances[:-1]):
            at = at + (lax.div(apart, distance) & 1) * (held << k)
        return jnp.where(apart & 1 == 1, far_ref[at], near_ref[at])

    def rows_first():
        stacked = jnp.concatenate([chosen(slot) for slot in range(LMAX)], axis=0)
        first_u, rest_u = dot(stacked, temp_rows[:, :lane]), dot(stacked, temp_rows[:, lane:half])
        first_v, rest_v = dot(stacked, temp_rows[:, half : half + lane]), dot(stacked, temp_rows[:, half + lane :])
        for slot in range(LMAX):
            rows = slice(slot * box, (slot + 1) * box)
            u, v = first_u[rows], first_v[rows]
            row_edge = -jnp.sum(u * sign, axis=0, keepdims=True)
            col_edge = jnp.sum(v, axis=0, keepdims=True)
            edges[slot] = (beside(row_edge, row_edge), beside(col_edge, col_edge))
            v_part = beside(jnp.where(box_col, 0.0, v), rest_v[rows]).astype(bf16)
            waves[slot, 0, :box] = beside(u, rest_u[rows]).astype(bf16)
            waves[slot, 1, :box] = beside(jnp.where(box_col, v, u), rest_u[rows]).astype(bf16)
            waves[slot, 0, box:] = v_part
            waves[slot, 1, box:] = v_part

    def project(slot):
        def cols(k):
            here = slice(k * half, (k + 1) * half)
            proj[slot % 2, here] = dot(temp_cols[here], waves[slot, k // 2]).astype(bf16)

        return [functools.partial(cols, k) for k in range(4)]

    def mix_first(slot, fs, ps):
        fpr, fpi, fmr, fmi = (f.astype(f32) for f in fs)
        ppr, ppi, pmr, pmi = (p.astype(f32) for p in ps)
        row_edge, col_edge = edges[slot]
        ppi = jnp.where(corner, row_edge, ppi)
        pmi = jnp.where(corner, pmr, pmi)
        pmr = jnp.where(corner, col_edge, pmr)
        plus_r, plus_i = fpr * ppr + fpi * ppi, fpi * ppr - fpr * ppi
        minus_r, minus_i = fmr * pmr + fmi * pmi, fmi * pmr - fmr * pmi
        cos_r, sin_r = plus_r + minus_r, minus_i - plus_i
        cos_i, sin_i = plus_i + minus_i, plus_r - minus_r
        cos_i, sin_i = jnp.where(col_first, sin_i, cos_i), jnp.where(col_first, -cos_i, sin_i)
        cos_r = jnp.where(row_first, plus_r, cos_r)
        sin_r = jnp.where(row_first, minus_r, sin_r)
        cos_i = jnp.where(row_first, plus_i, cos_i)
        sin_i = jnp.where(row_first, minus_i, sin_i)
        cos_r = jnp.where(corner, fpr * ppr + fmr * pmr, cos_r)
        sin_r = jnp.where(corner, fpi * ppi + fmi * pmi, sin_r)
        cos_i = jnp.where(corner, fpr * ppr - fmr * pmr, cos_i)
        sin_i = jnp.where(corner, fpi * ppi - fmi * pmi, sin_i)
        return cos_r.astype(bf16), sin_r.astype(bf16), cos_i.astype(bf16), sin_i.astype(bf16)

    def mix(slot, start):
        row_odd, at = start // lane, start % lane
        buffer = slot % 2
        fs = [filt[k, start : start + step] for k in range(4)]
        ps = [proj[buffer, k * half + start : k * half + start + step] for k in range(4)]
        if start == 0:
            cos_r, sin_r, cos_i, sin_i = mix_first(slot, fs, ps)
        else:
            fpr, fpi, fmr, fmi = fs
            ppr, ppi, pmr, pmi = ps
            plus_r, plus_i = fpr * ppr + fpi * ppi, fpi * ppr - fpr * ppi
            minus_r, minus_i = fmr * pmr + fmi * pmi, fmi * pmr - fmr * pmi
            cos_r, sin_r = plus_r + minus_r, minus_i - plus_i
            cos_i, sin_i = plus_i + minus_i, plus_r - minus_r
            cos_i, sin_i = jnp.where(thin_first, sin_i, cos_i), jnp.where(thin_first, -cos_i, sin_i)
        mixed[slot, row_odd, 0, at : at + step] = cos_r
        mixed[slot, row_odd, 0, lane + at : lane + at + step] = sin_r
        mixed[slot, row_odd, 1, at : at + step] = cos_i
        mixed[slot, row_odd, 1, lane + at : lane + at + step] = sin_i

    def combine(slot):
        def rows(imag):
            even = dot(fwd_e[...], mixed[slot, 0, imag])
            odd = dot(fwd_o[...], mixed[slot, 1, imag])
            place = slice(slot * strip, (slot + 1) * strip)
            for start in range(0, centre, strip):
                here = slice(start % half, start % half + strip)
                value = even[here] + odd[here] if start < half else even[here] - odd[here]
                value = value.astype(bf16)
                combos[0, imag, start // strip, place] = value[:, :lane]
                combos[1, imag, start // strip, place] = value[:, lane:]

        return [functools.partial(rows, imag) for imag in range(2)]

    share = 1.0 / jnp.full((1, 1), count, jnp.int32).astype(f32)
    shares = [jnp.where(slot < count, share, 0.0) for slot in range(LMAX)]
    fields, out_copies = {}, []

    def back(part):
        fields[part] = (
            dot(beside(combos[0, 0, part], combos[0, 1, part]), inv_e[...]),
            dot(beside(combos[1, 0, part], combos[1, 1, part]), inv_o[...]),
        )

    def gather(part):
        even, odd = fields.pop(part)
        for slot in range(LMAX):
            here = slice(slot * strip, (slot + 1) * strip)
            near, far = even[here], odd[here]
            score = beside(near + far, near[:, : centre - half] - far[:, : centre - half])
            scaled = score * shares[slot]
            if slot == 0:
                best, mean, squares = score, scaled, scaled * score
            else:
                best = jnp.maximum(best, score)
                mean, squares = mean + scaled, squares + scaled * score
        variance = squares - mean * mean
        rows = slice(part * strip, (part + 1) * strip)
        out_buf[0, rows] = (best - mean) * lax.rsqrt(jnp.maximum(variance, var_floor))
        out_buf[1, rows] = mean
        out_buf[2, rows] = variance
        for k, out in enumerate((snr_ref, mean_ref, var_ref)):
            copy = pltpu.make_async_copy(out_buf.at[k, rows], out.at[0, rows], out_sem.at[k, part])
            copy.start()
            out_copies.append(copy)

    tile = tile_steps(paired, pieces, weight_ref, (fwd_e, fwd_o, fwd_et, fwd_ot), filt, uv)
    weave(tile, [rows_first] + project(0) + project(1))
    for tick in range(1, LMAX + 1):
        products = project(tick) if 1 < tick < LMAX else []
        if tick > 1:
            products = products + combine(tick - 2)
        sums = [functools.partial(mix, tick - 1, start) for start in range(0, half, step)]
        weave(products, sums)
    for step_ in combine(LMAX - 1):
        step_()
    for part in range(centre // strip):
        back(part)
        gather(part)
    for copy in out_copies:
        copy.wait()


def beside(left, right):
    return jnp.concatenate([left, right], axis=1)


def vmem_call(kernel, inputs, outs, scratch, scalars, limit, out_spec=pltpu.VMEM, in_space=pltpu.VMEM):
    if in_space == pltpu.HBM:
        fixed = [pltpu.with_memory_space_constraint(array, pltpu.HBM) for array in inputs[scalars:]]
        inputs = (*inputs[:scalars], *fixed)
    smem = pl.BlockSpec(memory_space=pltpu.SMEM)
    vmem = pl.BlockSpec(memory_space=in_space)
    return pl.pallas_call(
        kernel,
        out_shape=tuple(jax.ShapeDtypeStruct(shape, dtype) for shape, dtype in outs),
        in_specs=[smem] * scalars + [vmem] * (len(inputs) - scalars),
        out_specs=tuple(pl.BlockSpec(memory_space=out_spec) for _ in outs),
        scratch_shapes=scratch,
        compiler_params=pltpu.CompilerParams(vmem_limit_bytes=limit << 20),
    )(*inputs)


def pack(orient_list, lengths, defocus, centre_block, templates):
    centre, box = centre_block.shape[0], templates.shape[1]
    lane = (centre + box) // 4
    held = (centre_block, orient_list.T, lengths[None], defocus[None], templates)
    strip = ((centre // 2, lane), jnp.bfloat16)
    outs = [(array.shape, array.dtype) for array in held] + [((box // 2, centre), jnp.bfloat16), strip, strip]
    return vmem_call(pack_kernel, held, outs, [pltpu.SemaphoreType.DMA((5,))], 0, 8, in_space=pltpu.HBM)


def early(defocus, extent):
    half = extent // 2
    return vmem_call(early_kernel, (defocus,), (((4, half, half), jnp.float32),), [], 1, 8)[0]


def match(orient_list, lengths, pieces, weights, near, far, tables):
    centre, half = pieces[0].shape[0], weights.shape[1]
    lane, extent = half // 2, 2 * half
    strip = lane // 2
    out = ((1, centre, centre), jnp.float32)
    kernel = functools.partial(match_kernel, len(pieces) == 4)
    return vmem_call(
        kernel, (orient_list, lengths, *pieces, weights, near, far, *tables), (out, out, out),
        [
            pltpu.VMEM((4, half, half), jnp.bfloat16),
            pltpu.VMEM((extent, extent), jnp.float32),
            pltpu.VMEM((LMAX, 2, 2 * near.shape[1], half), jnp.bfloat16),
            pltpu.VMEM((2, 2 * extent, half), jnp.bfloat16),
            pltpu.VMEM((LMAX, 2, 2, half, half), jnp.bfloat16),
            pltpu.VMEM((2, 2, centre // strip, LMAX * strip, lane), jnp.bfloat16),
            pltpu.VMEM((3, centre, centre), jnp.float32),
            pltpu.SemaphoreType.DMA((3, centre // strip)),
        ],
        2, 24, pl.ANY,
    )


def shards(micrograph, templates, orient_list, lengths, defocus):
    position = lax.axis_index("tile")
    tile_count = lax.axis_size("tile")
    centre_block = micrograph[0]
    centre = centre_block.shape[0]
    box = templates.shape[1]
    margin = box // 2
    extent = centre + box
    tile_rows = tile_count // GRID
    grid_place = (position + GRID // 2) % tile_count
    column, tile_row = grid_place % GRID, grid_place // GRID
    tables = make_tables(extent, box)

    def send(block, target):
        return lax.ppermute(block, "tile", [(i, target(i)) for i in range(tile_count)])

    paired = tile_rows == 2
    if paired:
        odd = position % 2 == 1
        distances = flips(tile_count)
        pair = send(templates, lambda i: i ^ distances[0])
        block, orients, counts, focus, own, to_ends, to_mate, to_peer = pack(
            orient_list, lengths, defocus, centre_block, templates
        )
        ends = send(to_ends, lambda i: i ^ GRID)
        weights = early(focus, extent)

        def strip(own, use_first):
            edge = jnp.where(use_first, ends[:, :margin], ends[:, centre - margin :])
            edge = jnp.concatenate([edge[: margin // 2], edge[margin // 2 :]], axis=1)
            return jnp.concatenate([own, edge], axis=0)

        two = jnp.concatenate([own, pair], axis=0)
        group = [two]
        for apart in (distances[2] | distances[1], distances[1], distances[2]):
            group.append(send(two, lambda i, apart=apart: i ^ apart))
        from_peer = send(strip(to_peer, ~odd), lambda i: (i + 1 if i % 2 else i - 1) % tile_count)
        from_mate = send(strip(to_mate, odd), lambda i: i ^ 1)
        near = jnp.concatenate([group[0], group[2], group[3], group[1]], axis=0)
        far = send(near, lambda i: i ^ 1)
        pieces = (block, from_mate, from_peer, ends)
    else:

        def arrive(block, distance):
            return lax.ppermute(
                block, "tile", [((i + distance) % tile_count, i) for i in range(tile_count)]
            )

        _, orients, counts, focus, *_ = pack(orient_list, lengths, defocus, centre_block, templates)
        weights = early(focus, extent)
        right = arrive(centre_block[:, :margin], 1)
        left = arrive(centre_block[:, centre - margin :], -1)
        right = jnp.where(column == GRID - 1, jnp.zeros_like(right), right)
        left = jnp.where(column == 0, jnp.zeros_like(left), left)
        cols = jnp.concatenate([right, left], axis=1)
        wide = jnp.concatenate([centre_block, cols], axis=1)
        below = arrive(wide[:margin], GRID)
        above = arrive(wide[centre - margin :], -GRID)
        below = jnp.where(tile_row == tile_rows - 1, jnp.zeros_like(below), below)
        above = jnp.where(tile_row == 0, jnp.zeros_like(above), above)
        rows = jnp.concatenate([below, above], axis=0)
        near = templates
        for distance in flips(tile_count)[:-1]:
            near = jnp.concatenate([near, send(near, lambda i, d=distance: i ^ d)], axis=0)
        far = send(near, lambda i: i ^ 1)
        pieces = (centre_block, cols, rows)
    return match(orients, counts, pieces, weights, near, far, tables)


def solution(mesh):
    return jax.shard_map(
        shards,
        mesh=mesh,
        in_specs=(
            P(("mic", "tile"), None, None),
            P("tile", None, None),
            P("mic", None),
            P("mic"),
            P("mic"),
        ),
        out_specs=(
            P(("mic", "tile"), None, None),
            P(("mic", "tile"), None, None),
            P(("mic", "tile"), None, None),
        ),
        check_vma=False,
    )
```

```python
import functools
import math

import jax
import jax.numpy as jnp
import numpy as np
from jax import lax
from jax.experimental import pallas as pl
from jax.experimental.pallas import tpu as pltpu
from jax.sharding import PartitionSpec as P


GRID = 8
LMAX = 4

wave_length = 0.0197
spherical = 27000000.0
contrast = 0.07
var_floor = 0.1


def wave_tables(index, position, extent):
    product = index[:, None] * position[None, :] % extent
    angle = product * (2.0 * math.pi / extent)
    nyquist = 1.0 - 2.0 * (position[None, :] % 2)
    return np.cos(angle), np.where(index[:, None] == 0, nyquist, np.sin(angle))


def make_tables(extent, box):
    half = extent // 2
    position = np.arange(half)
    even, odd = position[::2], position[1::2]
    tables = []
    for index in (even, odd):
        cosine, sine = wave_tables(index, position, extent)
        tables.append(np.concatenate([cosine, sine], axis=0).T)
    tables += [table.T for table in tables]
    for index in (even, odd):
        cosine, sine = wave_tables(index, position, extent)
        first = index[:, None] == 0
        cosine = np.where(first, 0.5 + 0.5 * sine, cosine)
        tables.append(np.concatenate([cosine, np.where(first, 0.5 - 0.5 * sine, -sine)], axis=0))
    order = np.concatenate([even, odd])
    centred = np.arange(box) - box // 2
    cosine, sine = wave_tables(order, centred, extent)
    tables.append(np.concatenate([cosine, sine], axis=0).T)
    first = order[:, None] == 0
    plain = np.where(first, 0.0, sine)
    nyquist, zero = sine[:1] + 0 * sine, 0 * sine
    tables.append(
        np.concatenate(
            [
                np.concatenate([cosine, -plain], axis=1),
                np.concatenate([-plain, -cosine], axis=1),
                np.where(first, np.concatenate([nyquist, zero], axis=1), np.concatenate([cosine, plain], axis=1)),
                np.where(first, np.concatenate([zero, -nyquist], axis=1), np.concatenate([plain, -cosine], axis=1)),
            ],
            axis=0,
        )
    )
    return [jnp.asarray(table, jnp.bfloat16) for table in tables]


def sine_of_turns(turns):
    part = turns - jnp.round(turns)
    folded = jnp.where(jnp.abs(part) > 0.25, jnp.where(part > 0, 0.5, -0.5) - part, part)
    angle = folded * (2.0 * math.pi)
    square = angle * angle
    series = -1.0 / 39916800.0
    for factor in (362880.0, -5040.0, 120.0, -6.0, 1.0):
        series = series * square + 1.0 / factor
    return angle * series


def transfer(row, column, focus_value, extent):
    radius = (row * row + column * column) * (1.0 / (extent * extent))
    turns = (0.5 * wave_length) * focus_value * radius - (
        0.25 * spherical * wave_length**3
    ) * radius * radius
    return -sine_of_turns(turns + math.asin(contrast) / (2.0 * math.pi))


def flips(tile_count):
    if tile_count == 2 * GRID:
        return [GRID, 2, 4, 1]
    return [1 << k for k in reversed(range(tile_count.bit_length() - 1))]


def dot(left, right):
    return jnp.dot(left, right, preferred_element_type=jnp.float32)


def swap_halves(block, lanes):
    return pltpu.roll(block, lanes, 1)


def pack_kernel(*refs):
    sources, held, (ends_ref, mate_ref, peer_ref, sem) = refs[:5], refs[5:10], refs[10:]
    copies = [pltpu.make_async_copy(sources[k], held[k], sem.at[k]) for k in range(5)]
    for copy in copies:
        copy.start()
    me = lax.axis_index("tile")
    tile_count = lax.axis_size("tile")
    place = lax.rem(me + GRID // 2, tile_count)
    centre_ref = held[0]
    centre, lane, margin = centre_ref.shape[0], mate_ref.shape[1], ends_ref.shape[0]
    copies[0].wait()
    top = centre_ref[:margin].astype(jnp.float32)
    bottom = centre_ref[centre - margin :].astype(jnp.float32)
    ends_ref[...] = jnp.where(place < GRID, bottom, top).astype(jnp.bfloat16)
    half = centre // 2
    first = centre_ref[:, :lane].astype(jnp.float32)
    last = centre_ref[:, centre - lane :].astype(jnp.float32)
    low = lax.broadcasted_iota(jnp.int32, (half, lane), 1) < lane // 2
    first = jnp.where(low, first[:half], swap_halves(first[half:], lane // 2))
    last = jnp.where(low, swap_halves(last[:half], lane // 2), last[half:])
    odd = lax.rem(me, 2) == 1
    mate_ref[...] = jnp.where(odd, first, last).astype(jnp.bfloat16)
    peer_ref[...] = jnp.where(odd, last, first).astype(jnp.bfloat16)
    for copy in copies[1:]:
        copy.wait()


def early_kernel(defocus, weight_ref):
    me = lax.axis_index("tile")
    focus_value = defocus[0, me]
    lane = weight_ref.shape[1] // 2
    extent = 4 * lane
    edge = float(2 * lane)
    scale = 2.0 / (extent * extent)
    i = lax.broadcasted_iota(jnp.int32, (lane, lane), 0)
    j = lax.broadcasted_iota(jnp.int32, (lane, lane), 1)
    for row_odd in range(2):
        for col_odd in range(2):
            row = (2 * i + row_odd).astype(jnp.float32)
            col = (2 * j + col_odd).astype(jnp.float32)
            rows = slice(row_odd * lane, (row_odd + 1) * lane)
            cols = slice(col_odd * lane, (col_odd + 1) * lane)
            if row_odd and col_odd:
                value = scale * transfer(row, col, focus_value, extent)
                parts = (value,) * 4
            elif row_odd or col_odd:
                value = scale * transfer(row, col, focus_value, extent)
                if row_odd:
                    other = transfer(row, jnp.where(j == 0, edge, col), focus_value, extent)
                else:
                    other = transfer(jnp.where(i == 0, edge, row), col, focus_value, extent)
                other = scale * other
                parts = (value, value, other, other)
            else:
                col_first = j == 0
                corner = col_first & (i == 0)
                row_first = (i == 0) & (j != 0)
                row_minus = jnp.where(row_first, edge, row)
                col_minus = jnp.where(col_first, edge, col)
                at_corner = jnp.where(corner, 0.5 * scale, scale)
                parts = (
                    at_corner * transfer(row, col, focus_value, extent),
                    at_corner * transfer(jnp.where(corner, edge, row), col, focus_value, extent),
                    at_corner * transfer(row_minus, col_minus, focus_value, extent),
                    at_corner * transfer(jnp.where(corner, edge, row_minus), col_minus, focus_value, extent),
                )
            for k in range(4):
                weight_ref[k, rows, cols] = parts[k]


def packed_sides(mate, peer, lane, start, stop, left_open, right_open):
    odd = lax.rem(lax.axis_index("tile"), 2) == 1
    mate = mate[start:stop].astype(jnp.float32)
    peer = peer[start:stop].astype(jnp.float32)
    right = jnp.where(right_open, jnp.where(odd, peer, mate), 0.0)
    left = jnp.where(left_open, jnp.where(odd, mate, peer), 0.0)
    low = lax.broadcasted_iota(jnp.int32, right.shape, 1) < lane // 2
    upper = jnp.where(low, right, swap_halves(left, lane // 2))
    lower = jnp.where(low, swap_halves(right, lane // 2), left)
    return jnp.concatenate([upper, lower], axis=0)


def tile_steps(paired, pieces, weight_ref, tables, filt, uv):
    fwd_e, fwd_o, fwd_et, fwd_ot = tables
    centre_ref = pieces[0]
    centre, extent = centre_ref.shape[0], uv.shape[0]
    half, lane = extent // 2, extent // 4
    held = {}

    def assemble():
        if paired:
            _, mate_ref, peer_ref, ends_ref = pieces
            place = lax.rem(lax.axis_index("tile") + GRID // 2, 2 * GRID)
            column, upper_row = lax.rem(place, GRID), place < GRID
            opens = (column != 0, column != GRID - 1)
            held["side"] = packed_sides(mate_ref, peer_ref, lane, 0, centre // 2, *opens)
            corners = packed_sides(mate_ref, peer_ref, lane, centre // 2, mate_ref.shape[0], *opens)
            ends = jnp.concatenate([ends_ref[...].astype(jnp.float32), corners], axis=1)
            held["rim"] = jnp.concatenate([jnp.where(upper_row, ends, 0.0), jnp.where(upper_row, 0.0, ends)], axis=0)
        else:
            held["side"] = pieces[1][...].astype(jnp.float32)
            held["rim"] = pieces[2][...].astype(jnp.float32)

    def own_rows(first):
        rows = slice(first * lane, (first + 1) * lane)
        own = centre_ref[rows].astype(jnp.float32)
        far = jnp.concatenate([own[:, half:], held["side"][rows]], axis=1)
        near = own[:, :half]
        uv[rows, :half] = dot((near + far).astype(jnp.bfloat16), fwd_e[...])
        uv[rows, half:] = dot((near - far).astype(jnp.bfloat16), fwd_o[...])

    def rim_rows():
        near, far = held["rim"][:, :half], held["rim"][:, half:]
        uv[centre:, :half] = dot((near + far).astype(jnp.bfloat16), fwd_e[...])
        uv[centre:, half:] = dot((near - far).astype(jnp.bfloat16), fwd_o[...])

    def columns(row_odd, col_odd):
        cols = slice(col_odd * half, (col_odd + 1) * half)
        near, far = uv[:half, cols], uv[half:, cols]
        total = near - far if row_odd else near + far
        block = dot((fwd_ot if row_odd else fwd_et)[...], total.astype(jnp.bfloat16))
        i = lax.broadcasted_iota(jnp.int32, (lane, lane), 0)
        j = lax.broadcasted_iota(jnp.int32, (lane, lane), 1)
        uc, vc, us, vs = block[:lane, :lane], block[:lane, lane:], block[lane:, :lane], block[lane:, lane:]
        parts = [uc - vs, -(us + vc), uc + vs, us - vc]
        if not row_odd:
            row_first = i == 0
            parts = [jnp.where(row_first, a, b) for a, b in zip((uc, -vc, us, -vs), parts)]
        if not col_odd:
            col_first = j == 0
            parts = [jnp.where(col_first, a, b) for a, b in zip((uc, -us, vc, vs), parts)]
        rows = slice(row_odd * lane, (row_odd + 1) * lane)
        cols = slice(col_odd * lane, (col_odd + 1) * lane)
        for k in range(4):
            filt[k, rows, cols] = (weight_ref[k, rows, cols] * parts[k]).astype(jnp.bfloat16)

    steps = [assemble] + [functools.partial(own_rows, first) for first in range(centre // lane)] + [rim_rows]
    return steps + [functools.partial(columns, r, c) for r in range(2) for c in range(2)]


def weave(*tracks):
    steps = []
    for order, track in enumerate(tracks):
        steps += [((k + 0.5) / len(track), order, k, step) for k, step in enumerate(track)]
    for *_, step in sorted(steps, key=lambda entry: entry[:3]):
        step()


def rows_kernel(orients, lengths, near_ref, far_ref, temp_rows, waves, edges):
    me = lax.axis_index("tile")
    half = waves.shape[3]
    lane = half // 2
    box = near_ref.shape[1]
    tile_count = lax.axis_size("tile")
    distances = flips(tile_count)
    held = near_ref.shape[0] // (tile_count // 2)
    count = lengths[0, me]
    bf16, f32 = jnp.bfloat16, jnp.float32
    sign = 1.0 - 2.0 * (lax.broadcasted_iota(jnp.int32, (box, lane), 0) % 2).astype(f32)
    box_col = lax.broadcasted_iota(jnp.int32, (box, lane), 1) == 0

    def chosen(slot):
        orient = orients[slot, me]
        if slot:
            orient = jnp.where(slot < count, orient, orients[0, me])
        orient = jnp.clip(orient, 0, 2 * near_ref.shape[0] - 1)
        apart = lax.div(orient, held) ^ me
        at = lax.rem(orient, held)
        for k, distance in enumerate(distances[:-1]):
            at = at + (lax.div(apart, distance) & 1) * (held << k)
        return jnp.where(apart & 1 == 1, far_ref[at], near_ref[at])

    stacked = jnp.concatenate([chosen(slot) for slot in range(LMAX)], axis=0)
    first_u, rest_u = dot(stacked, temp_rows[:, :lane]), dot(stacked, temp_rows[:, lane:half])
    first_v, rest_v = dot(stacked, temp_rows[:, half : half + lane]), dot(stacked, temp_rows[:, half + lane :])
    for slot in range(LMAX):
        rows = slice(slot * box, (slot + 1) * box)
        u, v = first_u[rows], first_v[rows]
        row_edge = -jnp.sum(u * sign, axis=0, keepdims=True)
        col_edge = jnp.sum(v, axis=0, keepdims=True)
        edges[slot, :1], edges[slot, 1:2] = beside(row_edge, row_edge), beside(col_edge, col_edge)
        v_part = beside(jnp.where(box_col, 0.0, v), rest_v[rows]).astype(bf16)
        waves[slot, 0, :box] = beside(u, rest_u[rows]).astype(bf16)
        waves[slot, 1, :box] = beside(jnp.where(box_col, v, u), rest_u[rows]).astype(bf16)
        waves[slot, 0, box:] = v_part
        waves[slot, 1, box:] = v_part


def match_kernel(paired, lengths, *refs):
    count_in = 4 if paired else 3
    pieces, (weight_ref, waves, edges) = refs[:count_in], refs[count_in : count_in + 3]
    fwd_e, fwd_o, fwd_et, fwd_ot, inv_e, inv_o, temp_cols = refs[count_in + 3 : count_in + 10]
    snr_ref, mean_ref, var_ref = refs[count_in + 10 : count_in + 13]
    filt, uv, proj, mixed, combos, out_buf, out_sem = refs[count_in + 13 :]
    me = lax.axis_index("tile")
    half = filt.shape[1]
    lane = half // 2
    centre = out_buf.shape[1]
    strip = combos.shape[3] // LMAX
    count = lengths[0, me]
    bf16, f32 = jnp.bfloat16, jnp.float32
    step = 16
    col_first = lax.broadcasted_iota(jnp.int32, (step, half), 1) == 0
    row_first = lax.broadcasted_iota(jnp.int32, (step, half), 0) == 0
    corner = col_first & row_first
    thin_first = col_first.astype(f32).astype(bf16) > 0

    def project(slot):
        def cols(k):
            here = slice(k * half, (k + 1) * half)
            proj[slot % 2, here] = dot(temp_cols[here], waves[slot, k // 2]).astype(bf16)

        return [functools.partial(cols, k) for k in range(4)]

    def mix_first(slot, fs, ps):
        fpr, fpi, fmr, fmi = (f.astype(f32) for f in fs)
        ppr, ppi, pmr, pmi = (p.astype(f32) for p in ps)
        row_edge, col_edge = edges[slot, :1], edges[slot, 1:2]
        ppi = jnp.where(corner, row_edge, ppi)
        pmi = jnp.where(corner, pmr, pmi)
        pmr = jnp.where(corner, col_edge, pmr)
        plus_r, plus_i = fpr * ppr + fpi * ppi, fpi * ppr - fpr * ppi
        minus_r, minus_i = fmr * pmr + fmi * pmi, fmi * pmr - fmr * pmi
        cos_r, sin_r = plus_r + minus_r, minus_i - plus_i
        cos_i, sin_i = plus_i + minus_i, plus_r - minus_r
        cos_i, sin_i = jnp.where(col_first, sin_i, cos_i), jnp.where(col_first, -cos_i, sin_i)
        cos_r = jnp.where(row_first, plus_r, cos_r)
        sin_r = jnp.where(row_first, minus_r, sin_r)
        cos_i = jnp.where(row_first, plus_i, cos_i)
        sin_i = jnp.where(row_first, minus_i, sin_i)
        cos_r = jnp.where(corner, fpr * ppr + fmr * pmr, cos_r)
        sin_r = jnp.where(corner, fpi * ppi + fmi * pmi, sin_r)
        cos_i = jnp.where(corner, fpr * ppr - fmr * pmr, cos_i)
        sin_i = jnp.where(corner, fpi * ppi - fmi * pmi, sin_i)
        return cos_r.astype(bf16), sin_r.astype(bf16), cos_i.astype(bf16), sin_i.astype(bf16)

    def mix(slot, start):
        row_odd, at = start // lane, start % lane
        buffer = slot % 2
        fs = [filt[k, start : start + step] for k in range(4)]
        ps = [proj[buffer, k * half + start : k * half + start + step] for k in range(4)]
        if start == 0:
            cos_r, sin_r, cos_i, sin_i = mix_first(slot, fs, ps)
        else:
            fpr, fpi, fmr, fmi = fs
            ppr, ppi, pmr, pmi = ps
            plus_r, plus_i = fpr * ppr + fpi * ppi, fpi * ppr - fpr * ppi
            minus_r, minus_i = fmr * pmr + fmi * pmi, fmi * pmr - fmr * pmi
            cos_r, sin_r = plus_r + minus_r, minus_i - plus_i
            cos_i, sin_i = plus_i + minus_i, plus_r - minus_r
            cos_i, sin_i = jnp.where(thin_first, sin_i, cos_i), jnp.where(thin_first, -cos_i, sin_i)
        mixed[slot, row_odd, 0, at : at + step] = cos_r
        mixed[slot, row_odd, 0, lane + at : lane + at + step] = sin_r
        mixed[slot, row_odd, 1, at : at + step] = cos_i
        mixed[slot, row_odd, 1, lane + at : lane + at + step] = sin_i

    def combine(slot, first):
        def rows(imag):
            here = slice(first * lane, (first + 1) * lane)
            even = dot(fwd_e[here], mixed[slot, 0, imag])
            odd = dot(fwd_o[here], mixed[slot, 1, imag])
            starts = [(first * lane, even + odd)]
            if half + first * lane < centre:
                starts.append((half + first * lane, even - odd))
            for start, value in starts:
                value = value.astype(bf16)
                for k in range(lane // strip):
                    place = slice(slot * strip, (slot + 1) * strip)
                    piece = value[k * strip : (k + 1) * strip]
                    combos[0, imag, start // strip + k, place] = piece[:, :lane]
                    combos[1, imag, start // strip + k, place] = piece[:, lane:]

        return [functools.partial(rows, imag) for imag in range(2)]

    share = 1.0 / jnp.full((1, 1), count, jnp.int32).astype(f32)
    shares = [jnp.where(slot < count, share, 0.0) for slot in range(LMAX)]
    fields, out_copies = {}, []

    def back(part):
        fields[part] = (
            dot(beside(combos[0, 0, part], combos[0, 1, part]), inv_e[...]),
            dot(beside(combos[1, 0, part], combos[1, 1, part]), inv_o[...]),
        )

    def gather(part):
        even, odd = fields.pop(part)
        for slot in range(LMAX):
            here = slice(slot * strip, (slot + 1) * strip)
            near, far = even[here], odd[here]
            score = beside(near + far, near[:, : centre - half] - far[:, : centre - half])
            scaled = score * shares[slot]
            if slot == 0:
                best, mean, squares = score, scaled, scaled * score
            else:
                best = jnp.maximum(best, score)
                mean, squares = mean + scaled, squares + scaled * score
        variance = squares - mean * mean
        rows = slice(part * strip, (part + 1) * strip)
        out_buf[0, rows] = (best - mean) * lax.rsqrt(jnp.maximum(variance, var_floor))
        out_buf[1, rows] = mean
        out_buf[2, rows] = variance
        for k, out in enumerate((snr_ref, mean_ref, var_ref)):
            copy = pltpu.make_async_copy(out_buf.at[k, rows], out.at[0, rows], out_sem.at[k, part])
            copy.start()
            out_copies.append(copy)

    tile = tile_steps(paired, pieces, weight_ref, (fwd_e, fwd_o, fwd_et, fwd_ot), filt, uv)
    weave(tile, project(0) + project(1))
    for tick in range(1, LMAX + 1):
        products = project(tick) if 1 < tick < LMAX else []
        if tick > 1:
            products = products + combine(tick - 2, 0)
        sums = [functools.partial(mix, tick - 1, start) for start in range(0, half, step)]
        weave(products, sums)
    for step_ in combine(LMAX - 1, 0):
        step_()
    for first in range(half // lane):
        later = []
        if first + 1 < half // lane:
            later = [step_ for slot in range(LMAX) for step_ in combine(slot, first + 1)]
        ready = []
        for start in range(first * lane, centre, half):
            for part in range(start // strip, (start + lane) // strip):
                ready += [functools.partial(back, part), functools.partial(gather, part)]
        weave(later, ready)
    for copy in out_copies:
        copy.wait()


def beside(left, right):
    return jnp.concatenate([left, right], axis=1)


def vmem_call(kernel, inputs, outs, scratch, scalars, limit, out_spec=pltpu.VMEM, in_space=pltpu.VMEM):
    if in_space == pltpu.HBM:
        fixed = [pltpu.with_memory_space_constraint(array, pltpu.HBM) for array in inputs[scalars:]]
        inputs = (*inputs[:scalars], *fixed)
    smem = pl.BlockSpec(memory_space=pltpu.SMEM)
    vmem = pl.BlockSpec(memory_space=in_space)
    return pl.pallas_call(
        kernel,
        out_shape=tuple(jax.ShapeDtypeStruct(shape, dtype) for shape, dtype in outs),
        in_specs=[smem] * scalars + [vmem] * (len(inputs) - scalars),
        out_specs=tuple(pl.BlockSpec(memory_space=out_spec) for _ in outs),
        scratch_shapes=scratch,
        compiler_params=pltpu.CompilerParams(vmem_limit_bytes=limit << 20),
    )(*inputs)


def pack(orient_list, lengths, defocus, centre_block, templates):
    centre, box = centre_block.shape[0], templates.shape[1]
    lane = (centre + box) // 4
    held = (centre_block, orient_list.T, lengths[None], defocus[None], templates)
    strip = ((centre // 2, lane), jnp.bfloat16)
    outs = [(array.shape, array.dtype) for array in held] + [((box // 2, centre), jnp.bfloat16), strip, strip]
    return vmem_call(pack_kernel, held, outs, [pltpu.SemaphoreType.DMA((5,))], 0, 8, in_space=pltpu.HBM)


def early(defocus, extent):
    half = extent // 2
    return vmem_call(early_kernel, (defocus,), (((4, half, half), jnp.float32),), [], 1, 8)[0]


def rows(orient_list, lengths, near, far, tables, half):
    box = near.shape[1]
    outs = (((LMAX, 2, 2 * box, half), jnp.bfloat16), ((LMAX, 8, half), jnp.float32))
    return vmem_call(rows_kernel, (orient_list, lengths, near, far, tables[6]), outs, [], 2, 8)


def match(lengths, pieces, weights, waves, edges, tables):
    centre, half = pieces[0].shape[0], weights.shape[1]
    lane, extent = half // 2, 2 * half
    strip = lane // 2
    out = ((1, centre, centre), jnp.float32)
    kernel = functools.partial(match_kernel, len(pieces) == 4)
    return vmem_call(
        kernel, (lengths, *pieces, weights, waves, edges, *tables[:6], tables[7]), (out, out, out),
        [
            pltpu.VMEM((4, half, half), jnp.bfloat16),
            pltpu.VMEM((extent, extent), jnp.float32),
            pltpu.VMEM((2, 2 * extent, half), jnp.bfloat16),
            pltpu.VMEM((LMAX, 2, 2, half, half), jnp.bfloat16),
            pltpu.VMEM((2, 2, centre // strip, LMAX * strip, lane), jnp.bfloat16),
            pltpu.VMEM((3, centre, centre), jnp.float32),
            pltpu.SemaphoreType.DMA((3, centre // strip)),
        ],
        1, 24, pl.ANY,
    )


def shards(micrograph, templates, orient_list, lengths, defocus):
    position = lax.axis_index("tile")
    tile_count = lax.axis_size("tile")
    centre_block = micrograph[0]
    centre = centre_block.shape[0]
    box = templates.shape[1]
    margin = box // 2
    extent = centre + box
    tile_rows = tile_count // GRID
    grid_place = (position + GRID // 2) % tile_count
    column, tile_row = grid_place % GRID, grid_place // GRID
    tables = make_tables(extent, box)

    def send(block, target):
        return lax.ppermute(block, "tile", [(i, target(i)) for i in range(tile_count)])

    paired = tile_rows == 2
    if paired:
        odd = position % 2 == 1
        distances = flips(tile_count)
        pair = send(templates, lambda i: i ^ distances[0])
        block, orients, counts, focus, own, to_ends, to_mate, to_peer = pack(
            orient_list, lengths, defocus, centre_block, templates
        )
        ends = send(to_ends, lambda i: i ^ GRID)
        weights = early(focus, extent)

        def strip(own, use_first):
            edge = jnp.where(use_first, ends[:, :margin], ends[:, centre - margin :])
            edge = jnp.concatenate([edge[: margin // 2], edge[margin // 2 :]], axis=1)
            return jnp.concatenate([own, edge], axis=0)

        two = jnp.concatenate([own, pair], axis=0)
        group = [two]
        for apart in (distances[2] | distances[1], distances[1], distances[2]):
            group.append(send(two, lambda i, apart=apart: i ^ apart))
        from_peer = send(strip(to_peer, ~odd), lambda i: (i + 1 if i % 2 else i - 1) % tile_count)
        from_mate = send(strip(to_mate, odd), lambda i: i ^ 1)
        near = jnp.concatenate([group[0], group[2], group[3], group[1]], axis=0)
        far = send(near, lambda i: i ^ 1)
        pieces = (block, from_mate, from_peer, ends)
    else:

        def arrive(block, distance):
            return lax.ppermute(
                block, "tile", [((i + distance) % tile_count, i) for i in range(tile_count)]
            )

        _, orients, counts, focus, *_ = pack(orient_list, lengths, defocus, centre_block, templates)
        weights = early(focus, extent)
        right = arrive(centre_block[:, :margin], 1)
        left = arrive(centre_block[:, centre - margin :], -1)
        right = jnp.where(column == GRID - 1, jnp.zeros_like(right), right)
        left = jnp.where(column == 0, jnp.zeros_like(left), left)
        cols = jnp.concatenate([right, left], axis=1)
        wide = jnp.concatenate([centre_block, cols], axis=1)
        below = arrive(wide[:margin], GRID)
        above = arrive(wide[centre - margin :], -GRID)
        below = jnp.where(tile_row == tile_rows - 1, jnp.zeros_like(below), below)
        above = jnp.where(tile_row == 0, jnp.zeros_like(above), above)
        rims = jnp.concatenate([below, above], axis=0)
        near = templates
        for distance in flips(tile_count)[:-1]:
            near = jnp.concatenate([near, send(near, lambda i, d=distance: i ^ d)], axis=0)
        far = send(near, lambda i: i ^ 1)
        pieces = (centre_block, cols, rims)
    waves, edges = rows(orients, counts, near, far, tables, extent // 2)
    return match(counts, pieces, weights, waves, edges, tables)


def solution(mesh):
    return jax.shard_map(
        shards,
        mesh=mesh,
        in_specs=(
            P(("mic", "tile"), None, None),
            P("tile", None, None),
            P("mic", None),
            P("mic"),
            P("mic"),
        ),
        out_specs=(
            P(("mic", "tile"), None, None),
            P(("mic", "tile"), None, None),
            P(("mic", "tile"), None, None),
        ),
        check_vma=False,
    )
```
